32 devices in a mesh: grp: 4 (over z), seq: 8 (over y, x, core).
Axes of the slice: x: 2, y: 2, z: 4, core: 2. Of those that a mesh axis runs over, the one named last changes fastest.
Arguments:
- mixer_input: bfloat16 [8192, 1024], P(('grp', 'seq')), may hold values from -6 to 6
- write_proj: bfloat16 [8192, 128], P(('grp', 'seq')), may hold values from -0.29882812 to 0.29882812
- read_proj: bfloat16 [8192, 128], P(('grp', 'seq')), may hold values from -0.29882812 to 0.29882812
- log_decay: float32 [8192, 16], P(('grp', 'seq')), may hold values from -2 to 0
- resid: bfloat16 [8192, 1024], P(('grp', 'seq')), may hold values from -134 to 134
- out_grad: bfloat16 [8192, 1024], P(('grp', 'seq')), may hold values from -6 to 6
- gate_probs: float32 [8192, 2], P(('grp', 'seq')), may hold values from 0.1 to 0.9
- expert_ids: int32 [8192, 2], P(('grp', 'seq')), may hold values from 0 to 31, as said below
- expert_up: bfloat16 [32, 1024, 1024], P(('grp', 'seq')), may hold values from -0.1875 to 0.1875
- expert_down: bfloat16 [32, 1024, 1024], P(('grp', 'seq')), may hold values from -0.1875 to 0.1875
Outputs:
- input_grad: bfloat16 [8192, 1024], P(('grp', 'seq'))
- write_grad: float32 [8192, 128], P(('grp', 'seq'))
- read_grad: float32 [8192, 128], P(('grp', 'seq'))
- decay_grad: float32 [8192, 16], P(('grp', 'seq'))
- resid_grad: bfloat16 [8192, 1024], P(('grp', 'seq'))
- gate_grad: bfloat16 [8192, 2], P(('grp', 'seq'))
- up_grad: bfloat16 [32, 1024, 1024], P(('grp', 'seq'))
- down_grad: bfloat16 [32, 1024, 1024], P(('grp', 'seq'))
The draws below stay inside these ranges and needn't reach their ends.
Inputs may be any that keep to these rules, and one draw needn't show every extreme that they name: `expert_ids`: each row names two different experts; among the 256 rows of one device no expert is named more than 32 times.
All inputs are finite; a program needn't handle non-finite values.
Results may differ from the reference program's by a relative error of at most 0.0072.
Values may be sent and summed in bfloat16 or wider, within the bound.
No kernel may reach another device: no remote copies, remote signals or barrier semaphores. Data moves between devices by JAX's collectives and lax.ppermute only.
A program may use at most 192 MiB of HBM per device.

```python
import math
import jax
import jax.numpy as jnp
from jax import lax

H = 16
P_SIZE = 64
N = 128
F = 1024
BLOCK_POSITIONS = 256
TOK_DEV = 256
D = 1024
SEQUENCE_LENGTH = 2048
TOKENS = 8192
EXPERTS = 32
CAP = 32


def order_with_first(member):
    shuffled, leader = member
    swapped = jnp.where(shuffled == leader, shuffled[0], shuffled)
    return swapped.at[0].set(leader)


def draw_expert_ids(key, part):
    source_blocks = TOKENS // TOK_DEV
    half_cap = CAP // 2
    key_hot, key_order, key_load, key_tok, key_swap = jax.random.split(key, 5)
    hottest = jax.random.randint(key_hot, (), 0, EXPERTS).astype(jnp.int32)
    order_keys = jax.random.split(key_order, source_blocks)
    shuffled = jax.vmap(lambda inner: jax.random.permutation(inner, EXPERTS))(order_keys).astype(jnp.int32)
    ordering = jax.vmap(order_with_first)((shuffled, jnp.full((source_blocks,), hottest, jnp.int32)))
    shifts = jax.random.randint(key_load, (source_blocks, EXPERTS // 2), 0, half_cap + 1).astype(jnp.int32)
    shifts = shifts.at[:, 0].set(half_cap)
    block_rows = jnp.arange(source_blocks, dtype=jnp.int32)[:, None]
    loads = jnp.zeros((source_blocks, EXPERTS), jnp.int32)
    loads = loads.at[block_rows, ordering[:, 0::2]].set(half_cap + shifts)
    loads = loads.at[block_rows, ordering[:, 1::2]].set(half_cap - shifts)
    ends = jnp.cumsum(loads, axis=1)
    place_list = jnp.arange(2 * TOK_DEV, dtype=jnp.int32)
    listing = jax.vmap(lambda bounds: jnp.searchsorted(bounds, place_list, side='right'))(ends).astype(jnp.int32)
    first_col = listing[:, :TOK_DEV]
    second_col = listing[:, TOK_DEV:]
    token_keys = jax.random.split(key_tok, source_blocks)
    shuffle = jax.vmap(lambda inner: jax.random.permutation(inner, TOK_DEV))(token_keys)
    first_col = jnp.take_along_axis(first_col, shuffle, axis=1)
    second_col = jnp.take_along_axis(second_col, shuffle, axis=1)
    flips = jax.random.randint(key_swap, (source_blocks, TOK_DEV), 0, 2)
    left_col = jnp.where(flips == 1, second_col, first_col)
    right_col = jnp.where(flips == 1, first_col, second_col)
    return jnp.stack([left_col, right_col], axis=-1).reshape(TOKENS, 2).astype(jnp.int32)


def draw_log_decay(key, part):
    key_variety, key_quick_heads, key_gradual_heads, key_placement_unit, key_position, key_surge, key_objective = jax.random.split(key, 7)
    sequence_batch = TOKENS // SEQUENCE_LENGTH
    fast_cut = 4
    fast_heads = jax.random.randint(key_variety, (sequence_batch, 1, 1, H), 0, 8) < fast_cut
    fast_rate = jax.random.uniform(key_quick_heads, (sequence_batch, 1, 1, H), minval=1.0 / 50.0, maxval=1.0 / 30.0)
    slow_rate = jax.random.uniform(key_gradual_heads, (sequence_batch, 1, 1, H), minval=0.1, maxval=0.45) / SEQUENCE_LENGTH
    rates = jnp.where(fast_heads, fast_rate, slow_rate)
    per_seq = SEQUENCE_LENGTH // TOK_DEV
    device_factor = jnp.exp(jax.random.uniform(key_placement_unit, (sequence_batch, per_seq, 1, H), minval=-0.4, maxval=0.4))
    position_factor = jnp.exp(jax.random.uniform(key_position, (sequence_batch, per_seq, TOK_DEV, H), minval=-0.7, maxval=0.7))
    rates = (rates * device_factor * position_factor).reshape(sequence_batch, SEQUENCE_LENGTH, H)
    surge_position = jax.random.randint(key_surge, (sequence_batch, 2), 0, SEQUENCE_LENGTH)
    losses = jax.random.uniform(key_objective, (sequence_batch, 2, H), minval=0.22, maxval=0.51)
    place_list = jnp.arange(SEQUENCE_LENGTH)
    struck_entries = (place_list[None, :, None] == surge_position[:, None, :]).astype(jnp.float32)
    extra = jnp.sum(struck_entries[:, :, :, None] * losses[:, None, :, :], axis=2)
    return (-(rates + extra)).reshape(TOKENS, H).astype(jnp.float32)


def draw_resid(key, part):
    key_val, key_row, key_col = jax.random.split(key, 3)
    base = jnp.clip(jax.random.normal(key_val, (TOKENS, D)), -4.0, 4.0)
    row_scale = jnp.exp(jax.random.uniform(key_row, (TOKENS, 1), minval=0.0, maxval=math.log(10.0)))
    col_scale = jnp.exp(jax.random.uniform(key_col, (1, D), minval=0.0, maxval=math.log(10.0)))
    return (base * row_scale * col_scale / 3.0).astype(jnp.bfloat16)


def levels(stream_key, extent, cuts, low, high):
    level = 1.0
    for position, parts in cuts:
        steps = jax.random.uniform(jax.random.fold_in(jax.random.fold_in(stream_key, 6), position), (parts,), jnp.float32, low / len(cuts), high / len(cuts))
        level = level * jnp.repeat(jnp.exp(steps), extent[position] // parts).reshape((-1,) + (1,) * (len(extent) - 1 - position))
    return level


def normal_values(stream_key, extent, width, reach, cuts=(), kind=jnp.bfloat16):
    factor_of = levels(stream_key, extent, cuts, -0.22, 0.18) if cuts else 1.0
    result = jax.random.normal(stream_key, extent, jnp.float32) * width * factor_of
    return jnp.minimum(jnp.maximum(result, -reach), reach).astype(kind)


def setup_inputs(seed: int = 0) -> dict:
    streams_of = jax.random.split(jax.random.key(seed), 11)
    return {
        "mixer_input": normal_values(streams_of[0], (TOKENS, D), 1.0, 6.0, ((0, 32),)),
        "write_proj": normal_values(streams_of[1], (TOKENS, N), 0.05, 0.29882812, ((0, 32),)),
        "read_proj": normal_values(streams_of[2], (TOKENS, N), 0.05, 0.29882812, ((0, 32),)),
        "log_decay": draw_log_decay(jax.random.fold_in(streams_of[10], 71), 0),
        "resid": draw_resid(jax.random.fold_in(streams_of[10], 71), 0),
        "out_grad": normal_values(streams_of[5], (TOKENS, D), 1.0, 6.0, ((0, 32),)),
        "gate_probs": jnp.clip(0.1 + 0.79999997 * jax.random.uniform(streams_of[6], (TOKENS, 2), jnp.float32) ** levels(streams_of[6], (TOKENS, 2), ((0, 32),), -0.2, 0.2), 0.1, 0.9),
        "expert_ids": draw_expert_ids(jax.random.fold_in(streams_of[10], 71), 0),
        "expert_up": normal_values(streams_of[8], (EXPERTS, D, F), D ** -0.5, 0.1875, ((0, 32),)),
        "expert_down": normal_values(streams_of[9], (EXPERTS, F, D), F ** -0.5, 0.1875, ((0, 32),)),
    }


TOP_PRECISION = lax.Precision.HIGHEST
EPSILON = 1e-06

def score_blocks(readers_batch, writes_batch):
    block_groups = readers_batch.shape[0] // BLOCK_POSITIONS
    return jnp.einsum('fxz,flz->fxl', readers_batch.reshape(block_groups, BLOCK_POSITIONS, readers_batch.shape[1]), writes_batch.reshape(block_groups, BLOCK_POSITIONS, writes_batch.shape[1]), preferred_element_type=jnp.float32)

def score_pullback(score_cotangent, readers, writes):
    block_groups = readers.shape[0] // BLOCK_POSITIONS
    readers_by_block = readers.reshape(block_groups, BLOCK_POSITIONS, readers.shape[1])
    writes_by_block = writes.reshape(block_groups, BLOCK_POSITIONS, writes.shape[1])
    read_surplus = jnp.einsum('hto,hov->htv', score_cotangent, writes_by_block, precision=TOP_PRECISION)
    write_surplus = jnp.einsum('rcz,rca->rza', score_cotangent, readers_by_block, precision=TOP_PRECISION)
    return (read_surplus.reshape(readers.shape), write_surplus.reshape(writes.shape))

def block_forward(carried, pieces):
    inputs, writes, readers, decays, scores = pieces
    cumulative = jnp.cumsum(decays, axis=0)
    length = decays.shape[0]
    causal = jnp.arange(length)[:, None] >= jnp.arange(length)[None, :]
    spread = cumulative.T[:, :, None] - cumulative.T[:, None, :]
    weights = jnp.exp(jnp.where(causal[None], spread, -jnp.inf))
    inside = jnp.einsum('hts,shp->thp', weights * scores[None], inputs, precision=TOP_PRECISION)
    carried_read = jnp.einsum('hpn,tn->thp', carried, readers, precision=TOP_PRECISION)
    outputs = inside + jnp.exp(cumulative)[:, :, None] * carried_read
    remaining = jnp.exp(cumulative[-1][None, :] - cumulative)
    updated = jnp.exp(cumulative[-1])[:, None, None] * carried + jnp.einsum('sh,shp,sn->hpn', remaining, inputs, writes, precision=TOP_PRECISION)
    return (updated, outputs)

def ssd_forward(inputs, writes, readers, decays, scores, initial):
    block_groups = inputs.shape[0] // BLOCK_POSITIONS
    pieces = (inputs.reshape(block_groups, BLOCK_POSITIONS, inputs.shape[1], inputs.shape[2]), writes.reshape(block_groups, BLOCK_POSITIONS, writes.shape[1]), readers.reshape(block_groups, BLOCK_POSITIONS, readers.shape[1]), decays.reshape(block_groups, BLOCK_POSITIONS, decays.shape[1]), scores)
    last_state, outputs = lax.scan(block_forward, initial, pieces)
    return (last_state, outputs.reshape(inputs.shape))

def expert_back(routed_rows, routed_grads, routed_gates, up_weight, down_weight):
    hidden_pre = jnp.dot(routed_rows, up_weight, preferred_element_type=jnp.float32)
    sigmoid = jax.nn.sigmoid(hidden_pre)
    activated = (hidden_pre * sigmoid).astype(jnp.bfloat16)
    produced = jnp.dot(activated, down_weight, preferred_element_type=jnp.float32)
    grads_float = routed_grads.astype(jnp.float32)
    gate_term = lax.optimization_barrier(jnp.sum(grads_float * produced, axis=1)).astype(jnp.bfloat16)
    scaled = (routed_gates.astype(jnp.float32)[:, None] * grads_float).astype(jnp.bfloat16)
    act_grad = jnp.dot(scaled, down_weight.T, preferred_element_type=jnp.float32)
    pre_grad = (act_grad * sigmoid * (1.0 + hidden_pre * (1.0 - sigmoid))).astype(jnp.bfloat16)
    down_total = jnp.dot(activated.T, scaled, preferred_element_type=jnp.float32).astype(jnp.bfloat16)
    up_total = jnp.dot(routed_rows.T, pre_grad, preferred_element_type=jnp.float32).astype(jnp.bfloat16)
    row_grad = jnp.dot(pre_grad, up_weight.T, preferred_element_type=jnp.float32).astype(jnp.bfloat16)
    return (row_grad, gate_term, up_total, down_total)

def assignment_ranks(pair_ids):
    listed = pair_ids.reshape(-1)
    listed_count = listed.shape[0]
    matches = (listed[:, None] == jnp.arange(EXPERTS, dtype=jnp.int32)[None, :]).astype(jnp.float32)
    earlier = (jnp.arange(listed_count)[:, None] > jnp.arange(listed_count)[None, :]).astype(jnp.float32)
    before = jnp.dot(earlier, matches, precision=TOP_PRECISION)
    return lax.optimization_barrier(jnp.sum(before * matches, axis=1)).astype(jnp.int32).reshape(pair_ids.shape)

def reference(mixer_input, write_proj, read_proj, log_decay, resid, out_grad, gate_probs, expert_ids, expert_up, expert_down):
    resid_float = resid.astype(jnp.float32)
    inverse = lax.rsqrt(lax.optimization_barrier(jnp.mean(resid_float * resid_float, axis=1, keepdims=True)) + EPSILON)
    normed = resid_float * inverse
    normed_b = normed.astype(jnp.bfloat16)
    gates_b = gate_probs.astype(jnp.bfloat16)
    source_blocks = TOKENS // TOK_DEV
    slot_ranks = lax.map(assignment_ranks, expert_ids.reshape(source_blocks, TOK_DEV, 2)).reshape(TOKENS, 2)
    owners = (jnp.arange(TOKENS, dtype=jnp.int32) // TOK_DEV)[:, None]
    per_expert = source_blocks * CAP
    positions = (expert_ids * per_expert + owners * CAP + slot_ranks).reshape(-1).astype(jnp.int32)
    token_index = jnp.repeat(jnp.arange(TOKENS, dtype=jnp.int32), 2)
    table = jnp.full((EXPERTS * per_expert,), TOKENS, jnp.int32).at[positions].set(token_index).reshape(EXPERTS, per_expert)
    gate_table = jnp.zeros((EXPERTS * per_expert,), jnp.bfloat16).at[positions].set(gates_b.reshape(-1)).reshape(EXPERTS, per_expert)
    padded_rows = jnp.concatenate([normed_b, jnp.zeros((1, D), jnp.bfloat16)], axis=0)
    padded_grads = jnp.concatenate([out_grad, jnp.zeros((1, D), jnp.bfloat16)], axis=0)

    def one_expert(member):
        slot_index, gate_column, up_weight, down_weight = member
        return expert_back(padded_rows[slot_index], padded_grads[slot_index], gate_column, up_weight, down_weight)
    row_grads, gate_terms, up_grad, down_grad = lax.map(one_expert, (table, gate_table, expert_up, expert_down))
    picked = row_grads.reshape(EXPERTS * per_expert, D)[positions].reshape(TOKENS, 2, D).astype(jnp.float32)
    d_normed = picked[:, 0] + picked[:, 1]
    gate_grad = gate_terms.reshape(-1)[positions].reshape(TOKENS, 2)
    resid_grad = (out_grad.astype(jnp.float32) + inverse * (d_normed - normed * lax.optimization_barrier(jnp.mean(d_normed * normed, axis=1, keepdims=True)))).astype(jnp.bfloat16)
    sequence_batch = TOKENS // SEQUENCE_LENGTH

    def one_sequence(member):
        inputs_b, writes_batch, readers_batch, decays, cotangent = member
        inputs = inputs_b.astype(jnp.float32)
        writes = writes_batch.astype(jnp.float32)
        readers = readers_batch.astype(jnp.float32)
        scores = score_blocks(readers_batch, writes_batch)

        def forward(inputs_arg, writes_arg, readers_arg, decays_arg, scores_arg):
            return ssd_forward(inputs_arg, writes_arg, readers_arg, decays_arg, scores_arg, jnp.zeros((H, P_SIZE, N), jnp.float32))[1]
        ignored, pullback = jax.vjp(forward, inputs, writes, readers, decays, scores)
        input_part, write_part, read_part, decay_part, score_cotangent = pullback(cotangent)
        read_surplus, write_surplus = score_pullback(score_cotangent, readers, writes)
        return (input_part, write_part + write_surplus, read_part + read_surplus, decay_part)
    grads = lax.map(one_sequence, (mixer_input.reshape(sequence_batch, SEQUENCE_LENGTH, H, P_SIZE), write_proj.reshape(sequence_batch, SEQUENCE_LENGTH, N), read_proj.reshape(sequence_batch, SEQUENCE_LENGTH, N), log_decay.reshape(sequence_batch, SEQUENCE_LENGTH, H), resid_grad.astype(jnp.float32).reshape(sequence_batch, SEQUENCE_LENGTH, H, P_SIZE)))
    input_grad = grads[0].reshape(TOKENS, D).astype(jnp.bfloat16)
    write_grad = grads[1].reshape(TOKENS, N)
    read_grad = grads[2].reshape(TOKENS, N)
    decay_grad = grads[3].reshape(TOKENS, H)
    return (input_grad, write_grad, read_grad, decay_grad, resid_grad, gate_grad, up_grad, down_grad)
```

```python
import functools

import jax
import jax.numpy as jnp
from jax import lax
from jax.experimental import pallas as pl
from jax.experimental.pallas import tpu as pltpu
from jax.sharding import PartitionSpec as P

EPSILON = 1e-06
HIGHEST = lax.Precision.HIGHEST
F32 = jnp.float32
BF16 = jnp.bfloat16
VMEM_LIMIT = 60 * 1024 * 1024


def iota(shape, axis):
    return lax.broadcasted_iota(jnp.int32, shape, axis)


def dot(a, b, ca, cb, precision=None):
    return lax.dot_general(
        a, b, (((ca,), (cb,)), ((), ())), precision=precision, preferred_element_type=F32
    )


def call(kernel, outs, *args, grid=None, in_specs=None, out_specs=None, scratch=(), cost=None):
    whole = pl.BlockSpec(memory_space=pltpu.VMEM)
    many = isinstance(outs, (tuple, list))
    kwargs = {}
    if grid is not None:
        kwargs["grid"] = grid
    return pl.pallas_call(
        kernel,
        out_shape=outs,
        in_specs=in_specs if in_specs is not None else [whole] * len(args),
        out_specs=out_specs
        if out_specs is not None
        else (tuple([whole] * len(outs)) if many else whole),
        scratch_shapes=list(scratch),
        compiler_params=pltpu.CompilerParams(vmem_limit_bytes=VMEM_LIMIT),
        cost_estimate=cost,
        **kwargs,
    )(*args)


def shape(dims, dtype):
    return jax.ShapeDtypeStruct(dims, dtype)


def one_hot(targets, slots):
    slot = iota((slots, targets.shape[1]), 0)
    first = slot == targets[0:1, :]
    second = slot == targets[1:2, :]
    return first, second


def rows_kernel(experts, cap, resid_ref, ids_ref, rows_ref, targets_ref):
    resid = resid_ref[...].astype(F32)
    inverse = lax.rsqrt(jnp.mean(resid * resid, axis=1, keepdims=True) + EPSILON)
    normed_b = (resid * inverse).astype(BF16)
    ids = ids_ref[...]
    tokens = ids.shape[1]
    number = iota((experts, tokens), 0)
    first = (number == ids[0:1, :]).astype(F32)
    second = (number == ids[1:2, :]).astype(F32)
    earlier = (iota((tokens, tokens), 0) < iota((tokens, tokens), 1)).astype(BF16)
    before = dot((first + second).astype(BF16), earlier, 1, 0)
    rank0 = jnp.sum(before * first, axis=0, keepdims=True).astype(jnp.int32)
    rank1 = jnp.sum(before * second, axis=0, keepdims=True).astype(jnp.int32)
    targets = jnp.concatenate([ids[0:1, :] * cap + rank0, ids[1:2, :] * cap + rank1], axis=0)
    targets_ref[...] = targets
    hit0, hit1 = one_hot(targets, experts * cap)
    select = jnp.where(hit0 | hit1, 1.0, 0.0).astype(BF16)
    rows_ref[...] = dot(select, normed_b, 1, 0).astype(BF16)


def grads_kernel(out_grad_ref, gates_ref, targets_ref, rows_ref):
    slots = rows_ref.shape[0]
    hit0, hit1 = one_hot(targets_ref[...], slots)
    gates = gates_ref[...].astype(BF16).astype(F32)
    select = jnp.where(hit0, gates[0:1, :], 0.0) + jnp.where(hit1, gates[1:2, :], 0.0)
    rows_ref[...] = dot(select.astype(BF16), out_grad_ref[...], 1, 0).astype(BF16)


def expert_kernel(scaled_ref, act_ref, slope_ref, up_ref, down_ref, pre_ref, row_ref, term_ref):
    act_grad = dot(scaled_ref[...], down_ref[...], 1, 1)
    pre = (act_grad * slope_ref[...]).astype(BF16)
    pre_ref[...] = pre
    row_ref[...] = dot(pre, up_ref[...], 1, 1).astype(BF16)
    prod = act_grad * act_ref[...].astype(F32)
    high = prod.astype(BF16)
    low = (prod - high.astype(F32)).astype(BF16)
    ones = jnp.ones((8, prod.shape[1]), BF16)
    term_ref[...] = (dot(ones, high, 1, 1) + dot(ones, low, 1, 1))[None]


def expert_stage(scaled, act, slope, up, down):
    rows, width = scaled.shape
    hidden = act.shape[1]
    tile = min(256, rows)
    steps = rows // tile
    by_rows = lambda w: pl.BlockSpec((tile, w), lambda i: (i, 0))
    whole = pl.BlockSpec(memory_space=pltpu.VMEM)
    pre, row_grad, term = call(
        expert_kernel,
        (shape((rows, hidden), BF16), shape((rows, width), BF16), shape((steps, 8, tile), F32)),
        scaled,
        act,
        slope,
        up,
        down,
        grid=(steps,),
        in_specs=[by_rows(width), by_rows(hidden), by_rows(hidden), whole, whole],
        out_specs=(by_rows(hidden), by_rows(width), pl.BlockSpec((1, 8, tile), lambda i: (i, 0, 0))),
        cost=pl.CostEstimate(
            flops=4 * rows * width * hidden, bytes_accessed=20 * rows * width, transcendentals=0
        ),
    )
    return pre, row_grad, term[:, 0, :].reshape(-1)


def gate_kernel(terms_ref, targets_ref, gates_ref, out_ref):
    slots = terms_ref.shape[1]
    hit0, hit1 = one_hot(targets_ref[...], slots)
    terms = terms_ref[...]
    gates = gates_ref[...].astype(BF16).astype(F32)
    first = dot(terms, jnp.where(hit0, 1.0, 0.0).astype(BF16), 1, 0)
    second = dot(terms, jnp.where(hit1, 1.0, 0.0).astype(BF16), 1, 0)
    out_ref[...] = jnp.concatenate([first[0:1, :], second[0:1, :]], axis=0) / gates


def spread(heads, width):
    return (iota((heads, width), 1) // (width // heads) == iota((heads, width), 0)).astype(F32)


def ends_kernel(inputs_ref, writes_ref, decays_ref, cum_ref, cumt_ref, send_ref):
    decays = decays_ref[...]
    tokens, heads = decays.shape
    parts, padded, width = send_ref.shape
    upto = (iota((tokens, tokens), 0) >= iota((tokens, tokens), 1)).astype(F32)
    cum = dot(upto, decays, 1, 0, HIGHEST)
    cum_ref[...] = cum
    cumt_ref[...] = dot(decays, upto, 0, 1, HIGHEST)
    total = cum[tokens - 1 : tokens, :]
    wide = spread(heads, width)
    remaining = dot(jnp.exp(total - cum), wide, 1, 0, HIGHEST)
    scaled = (inputs_ref[...].astype(F32) * remaining).astype(BF16)
    ends = dot(writes_ref[...], scaled, 0, 0)
    kept = dot(jnp.exp(jnp.broadcast_to(total, (8, heads))), wide, 1, 0, HIGHEST)[0:1, :]
    high = kept.astype(BF16)
    low = (kept - high.astype(F32)).astype(BF16)
    rows = ends.shape[0] // parts
    for part in range(parts):
        send_ref[part, 0:rows, :] = ends[part * rows : (part + 1) * rows, :].astype(BF16)
        send_ref[part, rows : rows + 1, :] = high
        send_ref[part, rows + 1 : rows + 2, :] = low
        send_ref[part, rows + 2 :, :] = jnp.zeros((padded - rows - 2, width), BF16)


def scan_kernel(reverse, ends_ref, kept_ref, out_ref):
    parts, rows, _ = out_ref.shape
    state = jnp.zeros(out_ref.shape[1:], F32)
    for step in range(parts):
        at = parts - 1 - step if reverse else step
        out_ref[at] = state.astype(BF16)
        kept = kept_ref[at, rows : rows + 1, :].astype(F32) + kept_ref[
            at, rows + 1 : rows + 2, :
        ].astype(F32)
        state = state * kept + ends_ref[at, 0:rows, :].astype(F32)


def home_kernel(
    back_ref, targets_ref, resid_ref, out_grad_ref, reads_ref, cum_ref, grad_ref, adjoint_ref
):
    slots, width = back_ref.shape
    heads = cum_ref.shape[1]
    hit0, hit1 = one_hot(targets_ref[...], slots)
    select = jnp.where(hit0 | hit1, 1.0, 0.0).astype(BF16)
    d_normed = dot(select, back_ref[...], 0, 0)
    resid = resid_ref[...].astype(F32)
    inverse = lax.rsqrt(jnp.mean(resid * resid, axis=1, keepdims=True) + EPSILON)
    normed = resid * inverse
    mean = jnp.mean(d_normed * normed, axis=1, keepdims=True)
    grad = (out_grad_ref[...].astype(F32) + inverse * (d_normed - normed * mean)).astype(BF16)
    grad_ref[...] = grad
    grown = dot(jnp.exp(cum_ref[...]), spread(heads, width), 1, 0, HIGHEST)
    scaled = (grad.astype(F32) * grown).astype(BF16)
    adjoint_ref[...] = dot(reads_ref[...], scaled, 0, 0).astype(BF16)


def inside_kernel(
    inputs_ref,
    grads_ref,
    writes_ref,
    reads_ref,
    state_ref,
    cum_ref,
    cumt_ref,
    dx_ref,
    dwrite_ref,
    dread_ref,
    dcum_ref,
    dcumt_ref,
    score_ref,
    total_ref,
):
    step = pl.program_id(0)
    steps = pl.num_programs(0)
    tokens, lanes = inputs_ref.shape
    each = cumt_ref.shape[0]
    size = lanes // each

    @pl.when(step == 0)
    def _():
        score_ref[...] = dot(reads_ref[...], writes_ref[...], 1, 1)
        total_ref[...] = jnp.zeros_like(total_ref)
        dread_ref[...] = jnp.zeros_like(dread_ref)
        dcum_ref[...] = jnp.zeros_like(dcum_ref)

    inputs = inputs_ref[...]
    grads = grads_ref[...]
    cum = cum_ref[...]
    scores = score_ref[...]
    causal = iota((tokens, tokens), 0) >= iota((tokens, tokens), 1)
    column = iota(cum.shape, 1)
    lane = iota((tokens, lanes), 1) // size
    dx = jnp.zeros((tokens, lanes), F32)
    sums = jnp.zeros(cum.shape, F32)
    grown = jnp.zeros((tokens, lanes), F32)
    state = state_ref[...]
    read_state = dot(reads_ref[...], state, 1, 0)
    inter = grads.astype(F32) * read_state
    total = jnp.zeros((tokens, tokens), F32)
    for k in range(each):
        head = step * each + k
        at_t = jnp.sum(jnp.where(column == head, cum, 0.0), axis=1, keepdims=True)
        at_s = cumt_ref[k]
        decay = jnp.exp(jnp.where(causal, at_t - at_s, -1e30))
        mine = lane == k
        grads_k = jnp.where(mine, grads, jnp.zeros_like(grads))
        weights = dot(grads_k, inputs, 1, 1) * decay
        total = total + weights
        dx = dx + dot((decay * scores).astype(BF16), grads_k, 0, 0)
        both = weights * scores
        grow = jnp.exp(at_t)
        row = jnp.sum(both, axis=1, keepdims=True) + grow * jnp.sum(
            jnp.where(mine, inter, 0.0), axis=1, keepdims=True
        )
        sums = sums + jnp.where(column == head, row, 0.0)
        dcumt_ref[k] = jnp.sum(both, axis=0, keepdims=True)
        grown = grown + jnp.where(mine, grow, 0.0)
    total_ref[...] += total
    dcum_ref[...] += sums
    dx_ref[...] = dx
    dread_ref[...] += dot((grown * grads.astype(F32)).astype(BF16), state, 1, 1)

    @pl.when(step == steps - 1)
    def _():
        total_b = total_ref[...].astype(BF16)
        dread_ref[...] += dot(total_b, writes_ref[...], 1, 0)
        dwrite_ref[...] = dot(total_b, reads_ref[...], 0, 0)


def inside_stage(inputs, grads, writes, reads, state, cum, cumt):
    tokens, width = inputs.shape
    heads = cum.shape[1]
    n = writes.shape[1]
    lanes = max(128, width // heads)
    steps = width // lanes
    each = heads // steps
    part = pl.BlockSpec((tokens, lanes), lambda i: (0, i))
    whole = pl.BlockSpec(memory_space=pltpu.VMEM)
    fixed = lambda dims: pl.BlockSpec(dims, lambda i: (0,) * len(dims))
    return call(
        inside_kernel,
        (
            shape((tokens, width), F32),
            shape((tokens, n), F32),
            shape((tokens, n), F32),
            shape((tokens, heads), F32),
            shape((heads, 1, tokens), F32),
        ),
        inputs,
        grads,
        writes,
        reads,
        state,
        cum,
        cumt.reshape(heads, 1, tokens),
        grid=(steps,),
        in_specs=[
            part,
            part,
            whole,
            whole,
            pl.BlockSpec((n, lanes), lambda i: (0, i)),
            whole,
            pl.BlockSpec((each, 1, tokens), lambda i: (i, 0, 0)),
        ],
        out_specs=(
            part,
            fixed((tokens, n)),
            fixed((tokens, n)),
            fixed((tokens, heads)),
            pl.BlockSpec((each, 1, tokens), lambda i: (i, 0, 0)),
        ),
        scratch=[pltpu.VMEM((tokens, tokens), F32), pltpu.VMEM((tokens, tokens), F32)],
        cost=pl.CostEstimate(
            flops=8 * heads * tokens * tokens * 64, bytes_accessed=8 * tokens * width, transcendentals=heads * tokens * tokens
        ),
    )


def last_kernel(
    inputs_ref,
    writes_ref,
    state_ref,
    adjoint_ref,
    cum_ref,
    dx_ref,
    dwrite_in_ref,
    dcum_ref,
    dcumt_ref,
    input_grad_ref,
    dwrite_ref,
    decay_ref,
):
    tokens, width = inputs_ref.shape
    heads = cum_ref.shape[1]
    cum = cum_ref[...]
    total = cum[tokens - 1 : tokens, :]
    wide = spread(heads, width)
    remaining = dot(jnp.exp(total - cum), wide, 1, 0, HIGHEST)
    adjoint = adjoint_ref[...]
    inputs = inputs_ref[...].astype(F32)
    moved = remaining * dot(writes_ref[...], adjoint, 1, 0)
    input_grad_ref[...] = (dx_ref[...] + moved).astype(BF16)
    dwrite_ref[...] = dwrite_in_ref[...] + dot((remaining * inputs).astype(BF16), adjoint, 1, 1)
    shares = dot(moved * inputs, wide, 1, 1, HIGHEST)
    kept = state_ref[...].astype(F32) * adjoint.astype(F32)
    kept = jnp.broadcast_to(jnp.sum(kept, axis=0, keepdims=True), (8, width))
    tail = dot(kept, wide, 1, 1, HIGHEST)[0:1, :] * jnp.exp(total)
    after = (iota((tokens, tokens), 1) >= iota((tokens, tokens), 0)).astype(F32)
    before = (iota((tokens, tokens), 1) < iota((tokens, tokens), 0)).astype(F32)
    decay_ref[...] = (
        dot(after, dcum_ref[...], 1, 0, HIGHEST)
        - dot(after, dcumt_ref[...], 1, 1, HIGHEST)
        + dot(before, shares, 1, 0, HIGHEST)
        + tail
    )


def shards(
    mixer_input,
    write_proj,
    read_proj,
    log_decay,
    resid,
    out_grad,
    gate_probs,
    expert_ids,
    expert_up,
    expert_down,
):
    tokens, width = resid.shape
    heads = log_decay.shape[1]
    n = write_proj.shape[1]
    shard_count = lax.axis_size("seq")
    experts = lax.axis_size("grp") * shard_count
    cap = 4 * tokens // experts
    slots = experts * cap
    everyone = ("grp", "seq")
    up, down = expert_up[0], expert_down[0]
    ids = expert_ids.T
    gates = gate_probs.T

    def swap(x, axes):
        return lax.all_to_all(x, axes, split_axis=0, concat_axis=0, tiled=True)

    send_rows, targets = call(
        functools.partial(rows_kernel, experts, cap),
        (shape((slots, width), BF16), shape((2, tokens), jnp.int32)),
        resid,
        ids,
    )
    rows = swap(send_rows, everyone)
    send_scaled = call(grads_kernel, shape((slots, width), BF16), out_grad, gates, targets)
    scaled = swap(send_scaled, everyone)

    state_rows = n // shard_count
    padded = -(-(state_rows + 2) // 16) * 16
    cum, cumt, send_ends = call(
        ends_kernel,
        (
            shape((tokens, heads), F32),
            shape((heads, tokens), F32),
            shape((shard_count, padded, width), BF16),
        ),
        mixer_input,
        write_proj,
        log_decay,
    )
    ends = swap(send_ends, "seq")
    parts = shape((shard_count, state_rows, width), BF16)
    starts = call(functools.partial(scan_kernel, False), parts, ends, ends)
    state = swap(starts, "seq").reshape(n, width)

    hidden = jnp.dot(rows, up, preferred_element_type=F32)
    sigmoid = jax.nn.sigmoid(hidden)
    act = (hidden * sigmoid).astype(BF16)
    slope = sigmoid * (1.0 + hidden * (1.0 - sigmoid))
    pre_grad, row_grad, term = expert_stage(scaled, act, slope, up, down)
    back = swap(row_grad, everyone)
    terms = swap(term.astype(BF16).reshape(experts, cap), everyone)
    down_grad = dot(act, scaled, 0, 0).astype(BF16)
    up_grad = dot(rows, pre_grad, 0, 0).astype(BF16)

    resid_grad, send_adjoint = call(
        home_kernel,
        (shape((tokens, width), BF16), shape((n, width), BF16)),
        back,
        targets,
        resid,
        out_grad,
        read_proj,
        cum,
    )
    adjoints = swap(send_adjoint.reshape(shard_count, state_rows, width), "seq")
    later = call(functools.partial(scan_kernel, True), parts, adjoints, ends)
    adjoint = swap(later, "seq").reshape(n, width)

    gate_grad = call(
        gate_kernel,
        shape((2, tokens), F32),
        jnp.broadcast_to(terms.reshape(1, slots), (8, slots)),
        targets,
        gates,
    )
    gate_grad = gate_grad.T.astype(BF16)

    dx, dwrite, read_grad, dcum, dcumt = inside_stage(
        mixer_input, resid_grad, write_proj, read_proj, state, cum, cumt
    )
    input_grad, write_grad, decay_grad = call(
        last_kernel,
        (shape((tokens, width), BF16), shape((tokens, n), F32), shape((tokens, heads), F32)),
        mixer_input,
        write_proj,
        state,
        adjoint,
        cum,
        dx,
        dwrite,
        dcum,
        dcumt.reshape(heads, tokens),
    )
    return (
        input_grad,
        write_grad,
        read_grad,
        decay_grad,
        resid_grad,
        gate_grad,
        up_grad[None],
        down_grad[None],
    )


def solution(mesh):
    flat = P(("grp", "seq"), None)
    cube = P(("grp", "seq"), None, None)
    return jax.shard_map(
        shards,
        mesh=mesh,
        in_specs=(flat,) * 8 + (cube,) * 2,
        out_specs=(flat,) * 6 + (cube,) * 2,
        check_vma=False,
    )
```

```python
import functools

import jax
import jax.numpy as jnp
from jax import lax
from jax.experimental import pallas as pl
from jax.experimental.pallas import tpu as pltpu
from jax.sharding import PartitionSpec as P


EPSILON = 1e-06
HIGHEST = lax.Precision.HIGHEST
F32 = jnp.float32
BF16 = jnp.bfloat16
VMEM_LIMIT = 20 * 1024 * 1024


def iota(shape, axis):
    return lax.broadcasted_iota(jnp.int32, shape, axis)


def dot(a, b, ca, cb, precision=None):
    return lax.dot_general(
        a, b, (((ca,), (cb,)), ((), ())), precision=precision, preferred_element_type=F32
    )


def call(kernel, outs, *args, grid=None, in_specs=None, out_specs=None, scratch=(), cost=None):
    whole = pl.BlockSpec(memory_space=pltpu.VMEM)
    many = isinstance(outs, (tuple, list))
    kwargs = {}
    if grid is not None:
        kwargs["grid"] = grid
    return pl.pallas_call(
        kernel,
        out_shape=outs,
        in_specs=in_specs if in_specs is not None else [whole] * len(args),
        out_specs=out_specs
        if out_specs is not None
        else (tuple([whole] * len(outs)) if many else whole),
        scratch_shapes=list(scratch),
        compiler_params=pltpu.CompilerParams(vmem_limit_bytes=VMEM_LIMIT),
        cost_estimate=cost,
        **kwargs,
    )(*args)


def shape(dims, dtype):
    return jax.ShapeDtypeStruct(dims, dtype)


def one_hot(targets, slots):
    slot = iota((slots, targets.shape[1]), 0)
    first = slot == targets[0:1, :]
    second = slot == targets[1:2, :]
    return first, second


def rows_kernel(experts, cap, resid_ref, ids_ref, rows_ref, targets_ref):
    resid = resid_ref[...].astype(F32)
    inverse = lax.rsqrt(jnp.mean(resid * resid, axis=1, keepdims=True) + EPSILON)
    normed_b = (resid * inverse).astype(BF16)
    ids = ids_ref[...]
    tokens = ids.shape[1]
    number = iota((experts, tokens), 0)
    first = (number == ids[0:1, :]).astype(F32)
    second = (number == ids[1:2, :]).astype(F32)
    earlier = (iota((tokens, tokens), 0) < iota((tokens, tokens), 1)).astype(BF16)
    before = dot((first + second).astype(BF16), earlier, 1, 0)
    rank0 = jnp.sum(before * first, axis=0, keepdims=True).astype(jnp.int32)
    rank1 = jnp.sum(before * second, axis=0, keepdims=True).astype(jnp.int32)
    targets = jnp.concatenate([ids[0:1, :] * cap + rank0, ids[1:2, :] * cap + rank1], axis=0)
    targets_ref[...] = targets
    hit0, hit1 = one_hot(targets, experts * cap)
    select = jnp.where(hit0 | hit1, 1.0, 0.0).astype(BF16)
    rows_ref[...] = dot(select, normed_b, 1, 0).astype(BF16)


def grads_kernel(out_grad_ref, gates_ref, targets_ref, rows_ref):
    slots = rows_ref.shape[0]
    hit0, hit1 = one_hot(targets_ref[...], slots)
    gates = gates_ref[...].astype(BF16).astype(F32)
    select = jnp.where(hit0, gates[0:1, :], 0.0) + jnp.where(hit1, gates[1:2, :], 0.0)
    rows_ref[...] = dot(select.astype(BF16), out_grad_ref[...], 1, 0).astype(BF16)


def expert_kernel(scaled_ref, act_ref, slope_ref, up_ref, down_ref, pre_ref, row_ref, term_ref):
    act_grad = dot(scaled_ref[...], down_ref[...], 1, 1)
    pre = (act_grad * slope_ref[...]).astype(BF16)
    pre_ref[...] = pre
    row_ref[...] = dot(pre, up_ref[...], 1, 1).astype(BF16)
    prod = act_grad * act_ref[...].astype(F32)
    high = prod.astype(BF16)
    low = (prod - high.astype(F32)).astype(BF16)
    ones = jnp.ones((8, prod.shape[1]), BF16)
    term_ref[...] = (dot(ones, high, 1, 1) + dot(ones, low, 1, 1))[None]


def expert_stage(scaled, act, slope, up, down):
    rows, width = scaled.shape
    hidden = act.shape[1]
    tile = min(256, rows)
    steps = rows // tile
    by_rows = lambda w: pl.BlockSpec((tile, w), lambda i: (i, 0))
    whole = pl.BlockSpec(memory_space=pltpu.VMEM)
    pre, row_grad, term = call(
        expert_kernel,
        (shape((rows, hidden), BF16), shape((rows, width), BF16), shape((steps, 8, tile), F32)),
        scaled,
        act,
        slope,
        up,
        down,
        grid=(steps,),
        in_specs=[by_rows(width), by_rows(hidden), by_rows(hidden), whole, whole],
        out_specs=(by_rows(hidden), by_rows(width), pl.BlockSpec((1, 8, tile), lambda i: (i, 0, 0))),
        cost=pl.CostEstimate(
            flops=4 * rows * width * hidden, bytes_accessed=20 * rows * width, transcendentals=0
        ),
    )
    return pre, row_grad, term[:, 0, :].reshape(-1)


def gate_kernel(terms_ref, targets_ref, gates_ref, out_ref):
    slots = terms_ref.shape[1]
    hit0, hit1 = one_hot(targets_ref[...], slots)
    terms = terms_ref[...]
    gates = gates_ref[...].astype(BF16).astype(F32)
    first = dot(terms, jnp.where(hit0, 1.0, 0.0).astype(BF16), 1, 0)
    second = dot(terms, jnp.where(hit1, 1.0, 0.0).astype(BF16), 1, 0)
    out_ref[...] = jnp.concatenate([first[0:1, :], second[0:1, :]], axis=0) / gates


def message_kernel(planes, shard_count, cap, resid_ref, ids_ref, gates_ref, message_ref, targets_ref):
    tokens, width = resid_ref.shape
    experts = planes * shard_count
    resid = resid_ref[...].astype(F32)
    inverse = lax.rsqrt(jnp.mean(resid * resid, axis=1, keepdims=True) + EPSILON)
    message_ref[0:tokens, :] = (resid * inverse).astype(BF16)
    ids = ids_ref[...]
    number = iota((experts, tokens), 0)
    first = (number == ids[0:1, :]).astype(F32)
    second = (number == ids[1:2, :]).astype(F32)
    earlier = (iota((tokens, tokens), 0) < iota((tokens, tokens), 1)).astype(BF16)
    before = dot((first + second).astype(BF16), earlier, 1, 0)
    ranks = jnp.concatenate(
        [
            jnp.sum(before * first, axis=0, keepdims=True),
            jnp.sum(before * second, axis=0, keepdims=True),
        ],
        axis=0,
    )
    targets_ref[...] = ids * cap + ranks.astype(jnp.int32)
    named = ids.astype(F32)
    plane = jnp.floor((named + 0.5) * (1.0 / shard_count))
    shard = named - plane * shard_count
    facts = jnp.concatenate(
        [plane, shard, ranks, gates_ref[...], jnp.zeros((8, tokens), F32)], axis=0
    )
    message_ref[tokens:, 0:tokens] = facts.astype(BF16)
    if width > tokens:
        message_ref[tokens:, tokens:] = jnp.zeros((16, width - tokens), BF16)


def named_rows(me_ref, message, slots, cap):
    tokens = message.shape[0] - 16
    facts = message[tokens:, 0:tokens].astype(F32)
    places = (facts[2:4, :].astype(jnp.int32) ^ me_ref[1]) * cap
    places = places + facts[4:6, :].astype(jnp.int32)
    places = jnp.where(facts[0:2, :] == me_ref[0].astype(F32), places, -1)
    hit0, hit1 = one_hot(places, slots)
    select = jnp.where(hit0 | hit1, 1.0, 0.0).astype(BF16)
    rows = dot(select, message[0:tokens, :], 1, 0).astype(BF16)
    keys = jnp.concatenate(
        [places.astype(F32), facts[6:8, :], jnp.zeros((4, tokens), F32)], axis=0
    )
    return keys, rows


def pick_rows_kernel(blocks, cap, me_ref, *refs):
    messages, outs, keys_ref = refs[:blocks], refs[blocks:-1], refs[-1]
    for m, message in enumerate(messages):
        keys_ref[m], rows = named_rows(me_ref, message, len(outs) * cap, cap)
        for x, out in enumerate(outs):
            out[m * cap : (m + 1) * cap, :] = rows[x * cap : (x + 1) * cap, :]


def scaled_rows(keys, grads, slots):
    hit0, hit1 = one_hot(keys[0:2, :].astype(jnp.int32), slots)
    select = jnp.where(hit0, keys[2:3, :], 0.0) + jnp.where(hit1, keys[3:4, :], 0.0)
    return dot(select.astype(BF16), grads, 1, 0).astype(BF16)


def pick_grads_kernel(blocks, cap, keys_ref, *refs):
    grads, outs = refs[:blocks], refs[blocks:]
    for m, grad in enumerate(grads):
        rows = scaled_rows(keys_ref[m], grad[...], len(outs) * cap)
        for x, out in enumerate(outs):
            out[m * cap : (m + 1) * cap, :] = rows[x * cap : (x + 1) * cap, :]


def pick_both_kernel(cap, me_ref, message_ref, grads_ref, *outs):
    slots = len(outs) * cap
    keys, rows = named_rows(me_ref, message_ref, slots, cap)
    scaled = scaled_rows(keys, grads_ref[...], slots)
    for x, out in enumerate(outs):
        out[0:cap, :] = rows[x * cap : (x + 1) * cap, :]
        out[cap:, :] = scaled[x * cap : (x + 1) * cap, :]


def gather_group(me_ref, parts, group_ref):
    cap = parts[0].shape[0]
    for x, part in enumerate(parts):
        at = pl.multiple_of((me_ref[1] ^ x) * cap, cap)
        group_ref[pl.ds(at, cap), :] = part[...]
    return group_ref[...]


def forward_group(rows, up_ref):
    hidden = dot(rows, up_ref[...], 1, 0)
    sigmoid = jax.nn.sigmoid(hidden)
    return (hidden * sigmoid).astype(BF16), sigmoid * (1.0 + hidden * (1.0 - sigmoid))


def hidden_kernel(count, me_ref, *refs):
    parts, (up_ref, rows_ref, act_ref, slope_ref) = refs[:count], refs[count:]
    act_ref[...], slope_ref[...] = forward_group(gather_group(me_ref, parts, rows_ref), up_ref)


def backward_group(scaled, act, slope, up_ref, down_ref, pre_ref, row_ref, term_ref):
    act_grad = dot(scaled, down_ref[...], 1, 1)
    pre = (act_grad * slope).astype(BF16)
    pre_ref[...] = pre
    row_ref[0] = dot(pre, up_ref[...], 1, 1).astype(BF16)
    prod = act_grad * act.astype(F32)
    high = prod.astype(BF16)
    low = (prod - high.astype(F32)).astype(BF16)
    ones = jnp.ones((8, prod.shape[1]), BF16)
    term_ref[0] = dot(ones, high, 1, 1) + dot(ones, low, 1, 1)


def routed_kernel(count, me_ref, *refs):
    parts = refs[:count]
    act_ref, slope_ref, up_ref, down_ref, scaled_ref, pre_ref, row_ref, term_ref = refs[count:]
    scaled = gather_group(me_ref, parts, scaled_ref)
    backward_group(
        scaled, act_ref[...], slope_ref[...], up_ref, down_ref, pre_ref, row_ref, term_ref
    )


def far_kernel(count, me_ref, *refs):
    cap = refs[0].shape[0] // 2
    up_ref, down_ref = refs[count : count + 2]
    rows_ref, act_ref, scaled_ref, pre_ref, row_ref, term_ref = refs[-6:]
    rows = gather_group(me_ref, [part.at[0:cap, :] for part in refs[:count]], rows_ref)
    act, slope = forward_group(rows, up_ref)
    act_ref[...] = act
    scaled = gather_group(me_ref, [part.at[cap:, :] for part in refs[:count]], scaled_ref)
    backward_group(scaled, act, slope, up_ref, down_ref, pre_ref, row_ref, term_ref)


def grouped(kernel, me, parts, each, extras, extra_specs, outs, out_specs, steps, aliases, flops):
    width = parts[0].shape[1]
    return pl.pallas_call(
        functools.partial(kernel, len(parts)),
        out_shape=outs,
        grid_spec=pltpu.PrefetchScalarGridSpec(
            num_scalar_prefetch=1,
            grid=(steps,),
            in_specs=[pl.BlockSpec((each, width), lambda i, me: (i, 0))] * len(parts) + extra_specs,
            out_specs=out_specs,
        ),
        input_output_aliases=aliases,
        compiler_params=pltpu.CompilerParams(vmem_limit_bytes=VMEM_LIMIT),
        cost_estimate=pl.CostEstimate(
            flops=flops, bytes_accessed=6 * width * width, transcendentals=0
        ),
    )(me, *parts, *extras)


def outer_kernel(a1_ref, b1_ref, a2_ref, b2_ref, out_ref):
    out_ref[...] = (
        dot(a1_ref[...], b1_ref[...], 0, 0) + dot(a2_ref[...], b2_ref[...], 0, 0)
    ).astype(BF16)


def outer_stage(a1, b1, a2, b2):
    left, right = a1.shape[1], b1.shape[1]
    tile = min(256, right)
    whole = pl.BlockSpec(memory_space=pltpu.VMEM)
    column = lambda b: pl.BlockSpec((b.shape[0], tile), lambda i: (0, i))
    rows = a1.shape[0] + a2.shape[0]
    return call(
        outer_kernel,
        shape((left, right), BF16),
        a1,
        b1,
        a2,
        b2,
        grid=(right // tile,),
        in_specs=[whole, column(b1), whole, column(b2)],
        out_specs=pl.BlockSpec((left, tile), lambda i: (0, i)),
        cost=pl.CostEstimate(
            flops=2 * rows * left * right, bytes_accessed=6 * left * right, transcendentals=0
        ),
    )


def routed_experts(resid, out_grad, ids, gates, up, down, cap, shard_count, planes, early):
    tokens, width = resid.shape
    hidden = up.shape[1]
    group = shard_count * cap
    plane, shard = lax.axis_index("grp"), lax.axis_index("seq")
    me = jnp.stack([plane, shard]).astype(jnp.int32)
    smem = pl.BlockSpec(memory_space=pltpu.SMEM)
    vmem = pl.BlockSpec(memory_space=pltpu.VMEM)

    def across(x, bit):
        return lax.ppermute(x, "grp", [(i, i ^ bit) for i in range(planes)])

    def spread_out(parts):
        moved = [
            lax.ppermute(part, "seq", [(i, i ^ x) for i in range(shard_count)])
            for x, part in enumerate(parts)
            if x
        ]
        return [parts[0]] + moved

    def pick_rows(messages):
        count = len(messages)
        outs = [shape((count * cap, width), BF16)] * shard_count
        *parts, keys = call(
            functools.partial(pick_rows_kernel, count, cap),
            tuple(outs + [shape((count, 8, tokens), F32)]),
            me,
            *messages,
            in_specs=[smem] + [vmem] * count,
        )
        return parts, keys

    def pick_grads(keys, grads):
        count = len(grads)
        outs = [shape((count * cap, width), BF16)] * shard_count
        return call(functools.partial(pick_grads_kernel, count, cap), tuple(outs), keys, *grads)

    def block(width):
        return pl.BlockSpec((group, width), lambda i, me: (i, 0))

    def hidden_stage(parts, steps):
        rows = steps * group
        return grouped(
            hidden_kernel,
            me,
            parts,
            cap,
            (up,),
            [vmem],
            (shape((rows, width), BF16), shape((rows, hidden), BF16), shape((rows, hidden), F32)),
            (block(width), block(hidden), block(hidden)),
            steps,
            {},
            2 * rows * width * hidden,
        )

    rows_of = lambda steps, size, dtype: shape((steps * group, size), dtype)
    backs = (shape((planes, group, width), BF16), shape((planes, 8, group), F32))

    def back_blocks(base):
        to_plane = lambda i, me: (me[0] ^ (base + i), 0, 0)
        return (pl.BlockSpec((1, group, width), to_plane), pl.BlockSpec((1, 8, group), to_plane))

    def routed_stage(parts, act, slope, steps):
        return grouped(
            routed_kernel,
            me,
            parts,
            cap,
            (act, slope, up, down),
            [block(hidden), block(hidden), vmem, vmem],
            (rows_of(steps, width, BF16), rows_of(steps, hidden, BF16)) + backs,
            (block(width), block(hidden)) + back_blocks(0),
            steps,
            {},
            4 * steps * group * width * hidden,
        )

    def far_stage(parts, filled):
        first = 1 + len(parts) + 2
        return grouped(
            far_kernel,
            me,
            parts,
            2 * cap,
            (up, down) + tuple(filled),
            [vmem, vmem] + [pl.BlockSpec(memory_space=pl.ANY)] * 2,
            (
                rows_of(1, width, BF16),
                rows_of(1, hidden, BF16),
                rows_of(1, width, BF16),
                rows_of(1, hidden, BF16),
            )
            + backs,
            (block(width), block(hidden), block(width), block(hidden)) + back_blocks(3),
            1,
            {first: 4, first + 1: 5},
            6 * group * width * hidden,
        )

    message, targets = call(
        functools.partial(message_kernel, planes, shard_count, cap),
        (shape((tokens + 16, width), BF16), shape((2, tokens), jnp.int32)),
        resid,
        ids,
        gates,
    )
    message2 = across(message, 2)
    message1 = across(message, 1)
    grad2 = across(out_grad, 2)
    grad1 = across(out_grad, 1)
    message3 = across(message2, 1)
    near_rows, near_keys = pick_rows([message, message1, message2])
    near_rows = spread_out(near_rows)
    grad3 = across(grad2, 1)
    near_grads = pick_grads(near_keys, [out_grad, grad1, grad2])
    near_grads = spread_out(near_grads)
    rows_a, act_a, slope_a = hidden_stage(near_rows, 3)
    far = call(
        functools.partial(pick_both_kernel, cap),
        tuple([shape((2 * cap, width), BF16)] * shard_count),
        me,
        message3,
        grad3,
        in_specs=[smem, vmem, vmem],
    )
    far = spread_out(far)
    act_a, early = lax.optimization_barrier((act_a, early))
    scaled_a, pre_a, row_grad, term = routed_stage(near_grads, act_a, slope_a, 3)
    rows_b, act_b, scaled_b, pre_b, row_grad, term = far_stage(far, (row_grad, term))
    pieces = lambda: (
        outer_stage(act_a, scaled_a, act_b, scaled_b),
        outer_stage(rows_a, pre_a, rows_b, pre_b),
    )
    return targets, row_grad.reshape(-1, width), term[:, 0, :], pieces, early


def plain_experts(resid, out_grad, ids, gates, up, down, cap, experts, swap, early):
    tokens, width = resid.shape
    slots = experts * cap
    send_rows, targets = call(
        functools.partial(rows_kernel, experts, cap),
        (shape((slots, width), BF16), shape((2, tokens), jnp.int32)),
        resid,
        ids,
    )
    rows = swap(send_rows)
    send_scaled = call(grads_kernel, shape((slots, width), BF16), out_grad, gates, targets)
    scaled = swap(send_scaled)
    hidden = jnp.dot(rows, up, preferred_element_type=F32)
    sigmoid = jax.nn.sigmoid(hidden)
    act = (hidden * sigmoid).astype(BF16)
    slope = sigmoid * (1.0 + hidden * (1.0 - sigmoid))
    pre_grad, row_grad, term = expert_stage(scaled, act, slope, up, down)
    pieces = lambda: (dot(act, scaled, 0, 0).astype(BF16), dot(rows, pre_grad, 0, 0).astype(BF16))
    return targets, row_grad, term, pieces, early


def spread(heads, width):
    return (iota((heads, width), 1) // (width // heads) == iota((heads, width), 0)).astype(F32)


def ends_kernel(inputs_ref, writes_ref, decays_ref, cum_ref, cumt_ref, send_ref):
    decays = decays_ref[...]
    heads, tokens = decays.shape
    parts, padded, width = send_ref.shape
    upto = (iota((tokens, tokens), 0) >= iota((tokens, tokens), 1)).astype(F32)
    cum = dot(upto, decays, 1, 1, HIGHEST)
    cum_ref[...] = cum
    cumt_ref[...] = dot(decays, upto, 1, 1, HIGHEST)
    total = cum[tokens - 1 : tokens, :]
    wide = spread(heads, width)
    remaining = dot(jnp.exp(total - cum), wide, 1, 0, HIGHEST)
    scaled = (inputs_ref[...].astype(F32) * remaining).astype(BF16)
    ends = dot(writes_ref[...], scaled, 0, 0)
    kept = dot(jnp.exp(jnp.broadcast_to(total, (8, heads))), wide, 1, 0, HIGHEST)[0:1, :]
    high = kept.astype(BF16)
    low = (kept - high.astype(F32)).astype(BF16)
    rows = ends.shape[0] // parts
    for part in range(parts):
        send_ref[part, 0:rows, :] = ends[part * rows : (part + 1) * rows, :].astype(BF16)
        send_ref[part, rows : rows + 1, :] = high
        send_ref[part, rows + 1 : rows + 2, :] = low
        send_ref[part, rows + 2 :, :] = jnp.zeros((padded - rows - 2, width), BF16)


def scan_kernel(reverse, ends_ref, kept_ref, out_ref):
    parts, rows, _ = out_ref.shape
    state = jnp.zeros(out_ref.shape[1:], F32)
    for step in range(parts):
        at = parts - 1 - step if reverse else step
        out_ref[at] = state.astype(BF16)
        kept = kept_ref[at, rows : rows + 1, :].astype(F32) + kept_ref[
            at, rows + 1 : rows + 2, :
        ].astype(F32)
        state = state * kept + ends_ref[at, 0:rows, :].astype(F32)


def home_kernel(
    back_ref, targets_ref, resid_ref, out_grad_ref, reads_ref, cum_ref, grad_ref, adjoint_ref
):
    slots, width = back_ref.shape
    heads = cum_ref.shape[1]
    hit0, hit1 = one_hot(targets_ref[...], slots)
    select = jnp.where(hit0 | hit1, 1.0, 0.0).astype(BF16)
    d_normed = dot(select, back_ref[...], 0, 0)
    resid = resid_ref[...].astype(F32)
    inverse = lax.rsqrt(jnp.mean(resid * resid, axis=1, keepdims=True) + EPSILON)
    normed = resid * inverse
    mean = jnp.mean(d_normed * normed, axis=1, keepdims=True)
    grad = (out_grad_ref[...].astype(F32) + inverse * (d_normed - normed * mean)).astype(BF16)
    grad_ref[...] = grad
    grown = dot(jnp.exp(cum_ref[...]), spread(heads, width), 1, 0, HIGHEST)
    scaled = (grad.astype(F32) * grown).astype(BF16)
    adjoint_ref[...] = dot(reads_ref[...], scaled, 0, 0).astype(BF16)


def inside_kernel(
    inputs_ref,
    grads_ref,
    writes_ref,
    reads_ref,
    state_ref,
    cum_ref,
    cumt_ref,
    dx_ref,
    dwrite_ref,
    dread_ref,
    dcum_ref,
    dcumt_ref,
    score_ref,
    total_ref,
):
    step = pl.program_id(0)
    steps = pl.num_programs(0)
    tokens, lanes = inputs_ref.shape
    each = cumt_ref.shape[0]
    size = lanes // each

    @pl.when(step == 0)
    def _():
        score_ref[...] = dot(reads_ref[...], writes_ref[...], 1, 1)
        total_ref[...] = jnp.zeros_like(total_ref)
        dread_ref[...] = jnp.zeros_like(dread_ref)
        dcum_ref[...] = jnp.zeros_like(dcum_ref)

    inputs = inputs_ref[...]
    grads = grads_ref[...]
    cum = cum_ref[...]
    scores = score_ref[...]
    causal = iota((tokens, tokens), 0) >= iota((tokens, tokens), 1)
    column = iota(cum.shape, 1)
    lane = iota((tokens, lanes), 1) // size
    dx = jnp.zeros((tokens, lanes), F32)
    sums = jnp.zeros(cum.shape, F32)
    grown = jnp.zeros((tokens, lanes), F32)
    state = state_ref[...]
    read_state = dot(reads_ref[...], state, 1, 0)
    inter = grads.astype(F32) * read_state
    total = jnp.zeros((tokens, tokens), F32)
    for k in range(each):
        head = step * each + k
        at_t = jnp.sum(jnp.where(column == head, cum, 0.0), axis=1, keepdims=True)
        at_s = cumt_ref[k]
        decay = jnp.exp(jnp.where(causal, at_t - at_s, -1e30))
        mine = lane == k
        grads_k = jnp.where(mine, grads, jnp.zeros_like(grads))
        weights = dot(grads_k, inputs, 1, 1) * decay
        total = total + weights
        dx = dx + dot((decay * scores).astype(BF16), grads_k, 0, 0)
        both = weights * scores
        grow = jnp.exp(at_t)
        row = jnp.sum(both, axis=1, keepdims=True) + grow * jnp.sum(
            jnp.where(mine, inter, 0.0), axis=1, keepdims=True
        )
        sums = sums + jnp.where(column == head, row, 0.0)
        dcumt_ref[k] = jnp.sum(both, axis=0, keepdims=True)
        grown = grown + jnp.where(mine, grow, 0.0)
    total_ref[...] += total
    dcum_ref[...] += sums
    dx_ref[...] = dx
    dread_ref[...] += dot((grown * grads.astype(F32)).astype(BF16), state, 1, 1)

    @pl.when(step == steps - 1)
    def _():
        total_b = total_ref[...].astype(BF16)
        dread_ref[...] += dot(total_b, writes_ref[...], 1, 0)
        dwrite_ref[...] = dot(total_b, reads_ref[...], 0, 0)


def inside_stage(inputs, grads, writes, reads, state, cum, cumt):
    tokens, width = inputs.shape
    heads = cum.shape[1]
    n = writes.shape[1]
    lanes = max(128, width // heads)
    steps = width // lanes
    each = heads // steps
    part = pl.BlockSpec((tokens, lanes), lambda i: (0, i))
    whole = pl.BlockSpec(memory_space=pltpu.VMEM)
    fixed = lambda dims: pl.BlockSpec(dims, lambda i: (0,) * len(dims))
    return call(
        inside_kernel,
        (
            shape((tokens, width), F32),
            shape((tokens, n), F32),
            shape((tokens, n), F32),
            shape((tokens, heads), F32),
            shape((heads, 1, tokens), F32),
        ),
        inputs,
        grads,
        writes,
        reads,
        state,
        cum,
        cumt.reshape(heads, 1, tokens),
        grid=(steps,),
        in_specs=[
            part,
            part,
            whole,
            whole,
            pl.BlockSpec((n, lanes), lambda i: (0, i)),
            whole,
            pl.BlockSpec((each, 1, tokens), lambda i: (i, 0, 0)),
        ],
        out_specs=(
            part,
            fixed((tokens, n)),
            fixed((tokens, n)),
            fixed((tokens, heads)),
            pl.BlockSpec((each, 1, tokens), lambda i: (i, 0, 0)),
        ),
        scratch=[pltpu.VMEM((tokens, tokens), F32), pltpu.VMEM((tokens, tokens), F32)],
        cost=pl.CostEstimate(
            flops=8 * heads * tokens * tokens * 64, bytes_accessed=8 * tokens * width, transcendentals=heads * tokens * tokens
        ),
    )


def last_kernel(
    inputs_ref,
    writes_ref,
    state_ref,
    adjoint_ref,
    cum_ref,
    cumt_ref,
    dx_ref,
    dwrite_in_ref,
    dcum_ref,
    dcumt_ref,
    input_grad_ref,
    dwrite_ref,
    decay_ref,
):
    tokens, width = inputs_ref.shape
    heads = cum_ref.shape[1]
    cum = cum_ref[...]
    total = cum[tokens - 1 : tokens, :]
    wide = spread(heads, width)
    remaining = dot(jnp.exp(total - cum), wide, 1, 0, HIGHEST)
    adjoint = adjoint_ref[...]
    inputs = inputs_ref[...].astype(F32)
    moved = remaining * dot(writes_ref[...], adjoint, 1, 0)
    input_grad_ref[...] = (dx_ref[...] + moved).astype(BF16)
    dwrite_ref[...] = dwrite_in_ref[...] + dot((remaining * inputs).astype(BF16), adjoint, 1, 1)
    shares = dot(moved * inputs, wide, 1, 1, HIGHEST)
    kept = state_ref[...].astype(F32) * adjoint.astype(F32)
    kept = jnp.broadcast_to(jnp.sum(kept, axis=0, keepdims=True), (8, width))
    tail = dot(wide, kept, 1, 1, HIGHEST)[:, 0:1] * jnp.exp(cumt_ref[...][:, tokens - 1 : tokens])
    after = (iota((tokens, tokens), 1) >= iota((tokens, tokens), 0)).astype(F32)
    before = (iota((tokens, tokens), 1) < iota((tokens, tokens), 0)).astype(F32)
    decay_ref[...] = (
        dot(dcum_ref[...], after, 0, 1, HIGHEST)
        - dot(dcumt_ref[...], after, 1, 1, HIGHEST)
        + dot(shares, before, 0, 1, HIGHEST)
        + tail
    )


def shards(
    mixer_input,
    write_proj,
    read_proj,
    log_decay,
    resid,
    out_grad,
    gate_probs,
    expert_ids,
    expert_up,
    expert_down,
):
    tokens, width = resid.shape
    heads = log_decay.shape[1]
    n = write_proj.shape[1]
    shard_count = lax.axis_size("seq")
    experts = lax.axis_size("grp") * shard_count
    cap = 4 * tokens // experts
    slots = experts * cap
    everyone = ("grp", "seq")
    up, down = expert_up[0], expert_down[0]
    ids = expert_ids.T
    gates = gate_probs.T

    def swap(x, axes):
        return lax.all_to_all(x, axes, split_axis=0, concat_axis=0, tiled=True)

    state_rows = n // shard_count
    padded = -(-(state_rows + 2) // 16) * 16
    cum, cumt, send_ends = call(
        ends_kernel,
        (
            shape((tokens, heads), F32),
            shape((heads, tokens), F32),
            shape((shard_count, padded, width), BF16),
        ),
        mixer_input,
        write_proj,
        log_decay.T,
    )
    ends = swap(send_ends, "seq")
    parts = shape((shard_count, state_rows, width), BF16)
    starts = call(functools.partial(scan_kernel, False), parts, ends, ends)
    state = swap(starts, "seq").reshape(n, width)

    planes = experts // shard_count
    if planes == 4 and shard_count <= 8 and cap % 16 == 0 and tokens <= width:
        targets, row_grad, term, outers, state = routed_experts(
            resid, out_grad, ids, gates, up, down, cap, shard_count, planes, state
        )
    else:
        targets, row_grad, term, outers, state = plain_experts(
            resid, out_grad, ids, gates, up, down, cap, experts, lambda x: swap(x, everyone), state
        )
    back = swap(row_grad, everyone)
    down_grad, up_grad = outers()
    back, down_grad, up_grad = lax.optimization_barrier((back, down_grad, up_grad))
    terms, back = lax.optimization_barrier((term.astype(BF16).reshape(experts, cap), back))
    terms = swap(terms, everyone)
    resid_grad, send_adjoint = call(
        home_kernel,
        (shape((tokens, width), BF16), shape((n, width), BF16)),
        back,
        targets,
        resid,
        out_grad,
        read_proj,
        cum,
    )
    send_adjoint, terms = lax.optimization_barrier((send_adjoint, terms))
    adjoints = swap(send_adjoint.reshape(shard_count, state_rows, width), "seq")
    dx, dwrite, read_grad, dcum, dcumt = inside_stage(
        mixer_input, resid_grad, write_proj, read_proj, state, cum, cumt
    )
    later = call(functools.partial(scan_kernel, True), parts, adjoints, ends)
    adjoint = swap(later, "seq").reshape(n, width)
    gate_grad = call(
        gate_kernel,
        shape((2, tokens), F32),
        jnp.broadcast_to(terms.reshape(1, slots), (8, slots)),
        targets,
        gates,
    )
    gate_grad = gate_grad.T.astype(BF16)

    input_grad, write_grad, decay_grad = call(
        last_kernel,
        (shape((tokens, width), BF16), shape((tokens, n), F32), shape((heads, tokens), F32)),
        mixer_input,
        write_proj,
        state,
        adjoint,
        cum,
        cumt,
        dx,
        dwrite,
        dcum,
        dcumt.reshape(heads, tokens),
    )
    return (
        input_grad,
        write_grad,
        read_grad,
        decay_grad.T,
        resid_grad,
        gate_grad,
        up_grad[None],
        down_grad[None],
    )


def solution(mesh):
    flat = P(("grp", "seq"), None)
    cube = P(("grp", "seq"), None, None)
    return jax.shard_map(
        shards,
        mesh=mesh,
        in_specs=(flat,) * 8 + (cube,) * 2,
        out_specs=(flat,) * 6 + (cube,) * 2,
        check_vma=False,
    )
```

```python
import functools

import jax
import jax.numpy as jnp
from jax import lax
from jax.experimental import pallas as pl
from jax.experimental.pallas import tpu as pltpu
from jax.sharding import PartitionSpec as P


EPSILON = 1e-06
F32 = jnp.float32
BF16 = jnp.bfloat16
VMEM_LIMIT = 20 * 1024 * 1024


def iota(shape, axis):
    return lax.broadcasted_iota(jnp.int32, shape, axis)


def dot(a, b, ca, cb, precision=None):
    return lax.dot_general(
        a, b, (((ca,), (cb,)), ((), ())), precision=precision, preferred_element_type=F32
    )


def call(kernel, outs, *args, grid=None, in_specs=None, out_specs=None, scratch=(), cost=None):
    whole = pl.BlockSpec(memory_space=pltpu.VMEM)
    many = isinstance(outs, (tuple, list))
    kwargs = {}
    if grid is not None:
        kwargs["grid"] = grid
    return pl.pallas_call(
        kernel,
        out_shape=outs,
        in_specs=in_specs if in_specs is not None else [whole] * len(args),
        out_specs=out_specs
        if out_specs is not None
        else (tuple([whole] * len(outs)) if many else whole),
        scratch_shapes=list(scratch),
        compiler_params=pltpu.CompilerParams(vmem_limit_bytes=VMEM_LIMIT),
        cost_estimate=cost,
        **kwargs,
    )(*args)


def pieces_of(x, count):
    parts = []
    for _ in range(count):
        part = x.astype(BF16)
        parts.append(part)
        x = x - part.astype(F32)
    return parts


def fine_dot(a, exact, ca, cb, count):
    return sum(dot(part, exact, ca, cb) for part in pieces_of(a, count))


def shape(dims, dtype):
    return jax.ShapeDtypeStruct(dims, dtype)


def far_shape(dims, dtype):
    return pltpu.HBM(dims, dtype)


def from_hbm(*arrays):
    return [pltpu.with_memory_space_constraint(x, pltpu.HBM) for x in arrays]


def one_step(dims):
    return pl.BlockSpec(dims, lambda i: (0,) * len(dims))


def streamed(kernel, outs, *args, near=(), scalars=None):
    fixed = [x if k in near else from_hbm(x)[0] for k, x in enumerate(args)]
    specs = [one_step(x.shape) for x in args]
    if scalars is not None:
        fixed = [scalars] + fixed
        specs = [pl.BlockSpec(memory_space=pltpu.SMEM)] + specs
    many = isinstance(outs, (tuple, list))
    blocks = tuple(one_step(out.shape) for out in outs) if many else one_step(outs.shape)
    return call(
        kernel,
        outs,
        *fixed,
        grid=(1,),
        in_specs=specs,
        out_specs=blocks,
    )


def one_hot(targets, slots):
    slot = iota((slots, targets.shape[1]), 0)
    first = slot == targets[0:1, :]
    second = slot == targets[1:2, :]
    return first, second


def rows_kernel(experts, cap, resid_ref, ids_ref, rows_ref, targets_ref):
    resid = resid_ref[...].astype(F32)
    inverse = lax.rsqrt(jnp.mean(resid * resid, axis=1, keepdims=True) + EPSILON)
    normed_b = (resid * inverse).astype(BF16)
    ids = ids_ref[...]
    tokens = ids.shape[1]
    number = iota((experts, tokens), 0)
    first = (number == ids[0:1, :]).astype(F32)
    second = (number == ids[1:2, :]).astype(F32)
    earlier = (iota((tokens, tokens), 0) < iota((tokens, tokens), 1)).astype(BF16)
    before = dot((first + second).astype(BF16), earlier, 1, 0)
    rank0 = jnp.sum(before * first, axis=0, keepdims=True).astype(jnp.int32)
    rank1 = jnp.sum(before * second, axis=0, keepdims=True).astype(jnp.int32)
    targets = jnp.concatenate([ids[0:1, :] * cap + rank0, ids[1:2, :] * cap + rank1], axis=0)
    targets_ref[...] = targets
    hit0, hit1 = one_hot(targets, experts * cap)
    select = jnp.where(hit0 | hit1, 1.0, 0.0).astype(BF16)
    rows_ref[...] = dot(select, normed_b, 1, 0).astype(BF16)


def grads_kernel(out_grad_ref, gates_ref, targets_ref, rows_ref):
    slots = rows_ref.shape[0]
    hit0, hit1 = one_hot(targets_ref[...], slots)
    gates = gates_ref[...].astype(BF16).astype(F32)
    select = jnp.where(hit0, gates[0:1, :], 0.0) + jnp.where(hit1, gates[1:2, :], 0.0)
    rows_ref[...] = dot(select.astype(BF16), out_grad_ref[...], 1, 0).astype(BF16)


def expert_kernel(scaled_ref, act_ref, slope_ref, up_ref, down_ref, pre_ref, row_ref, term_ref):
    act_grad = dot(scaled_ref[...], down_ref[...], 1, 1)
    pre = (act_grad * slope_ref[...]).astype(BF16)
    pre_ref[...] = pre
    row_ref[...] = dot(pre, up_ref[...], 1, 1).astype(BF16)
    prod = act_grad * act_ref[...].astype(F32)
    high = prod.astype(BF16)
    low = (prod - high.astype(F32)).astype(BF16)
    ones = jnp.ones((8, prod.shape[1]), BF16)
    term_ref[...] = (dot(ones, high, 1, 1) + dot(ones, low, 1, 1))[None]


def expert_stage(scaled, act, slope, up, down):
    rows, width = scaled.shape
    hidden = act.shape[1]
    tile = min(256, rows)
    steps = rows // tile
    by_rows = lambda w: pl.BlockSpec((tile, w), lambda i: (i, 0))
    whole = pl.BlockSpec(memory_space=pltpu.VMEM)
    pre, row_grad, term = call(
        expert_kernel,
        (shape((rows, hidden), BF16), shape((rows, width), BF16), shape((steps, 8, tile), F32)),
        scaled,
        act,
        slope,
        up,
        down,
        grid=(steps,),
        in_specs=[by_rows(width), by_rows(hidden), by_rows(hidden), whole, whole],
        out_specs=(by_rows(hidden), by_rows(width), pl.BlockSpec((1, 8, tile), lambda i: (i, 0, 0))),
        cost=pl.CostEstimate(
            flops=4 * rows * width * hidden, bytes_accessed=20 * rows * width, transcendentals=0
        ),
    )
    return pre, row_grad, term[:, 0, :].reshape(-1)


def gate_kernel(terms_ref, targets_ref, gates_ref, out_ref):
    slots = terms_ref.shape[1]
    hit0, hit1 = one_hot(targets_ref[...], slots)
    terms = terms_ref[...]
    gates = gates_ref[...].astype(BF16).astype(F32)
    first = dot(terms, jnp.where(hit0, 1.0, 0.0).astype(BF16), 1, 0)
    second = dot(terms, jnp.where(hit1, 1.0, 0.0).astype(BF16), 1, 0)
    out_ref[...] = jnp.concatenate([first[0:1, :], second[0:1, :]], axis=0) / gates


def message_kernel(planes, shard_count, cap, resid_ref, ids_ref, gates_ref, message_ref, targets_ref):
    tokens, width = resid_ref.shape
    experts = planes * shard_count
    resid = resid_ref[...].astype(F32)
    inverse = lax.rsqrt(jnp.mean(resid * resid, axis=1, keepdims=True) + EPSILON)
    message_ref[0:tokens, :] = (resid * inverse).astype(BF16)
    ids = ids_ref[...]
    number = iota((experts, tokens), 0)
    first = (number == ids[0:1, :]).astype(F32)
    second = (number == ids[1:2, :]).astype(F32)
    earlier = (iota((tokens, tokens), 0) < iota((tokens, tokens), 1)).astype(BF16)
    before = dot((first + second).astype(BF16), earlier, 1, 0)
    ranks = jnp.concatenate(
        [
            jnp.sum(before * first, axis=0, keepdims=True),
            jnp.sum(before * second, axis=0, keepdims=True),
        ],
        axis=0,
    )
    targets_ref[...] = ids * cap + ranks.astype(jnp.int32)
    named = ids.astype(F32)
    plane = jnp.floor((named + 0.5) * (1.0 / shard_count))
    shard = named - plane * shard_count
    facts = jnp.concatenate(
        [plane, shard, ranks, gates_ref[...], jnp.zeros((8, tokens), F32)], axis=0
    )
    message_ref[tokens:, 0:tokens] = facts.astype(BF16)
    if width > tokens:
        message_ref[tokens:, tokens:] = jnp.zeros((16, width - tokens), BF16)


def named_rows(me_ref, message, slots, cap):
    tokens = message.shape[0] - 16
    facts = message[tokens:, 0:tokens].astype(F32)
    places = (facts[2:4, :].astype(jnp.int32) ^ me_ref[1]) * cap
    places = places + facts[4:6, :].astype(jnp.int32)
    places = jnp.where(facts[0:2, :] == me_ref[0].astype(F32), places, -1)
    hit0, hit1 = one_hot(places, slots)
    select = jnp.where(hit0 | hit1, 1.0, 0.0).astype(BF16)
    rows = dot(select, message[0:tokens, :], 1, 0).astype(BF16)
    keys = jnp.concatenate(
        [places.astype(F32), facts[6:8, :], jnp.zeros((4, tokens), F32)], axis=0
    )
    return keys, rows


def pick_rows_kernel(blocks, cap, me_ref, *refs):
    messages, outs, keys_ref = refs[:blocks], refs[blocks:-1], refs[-1]
    for m, message in enumerate(messages):
        keys_ref[m], rows = named_rows(me_ref, message, len(outs) * cap, cap)
        for x, out in enumerate(outs):
            out[m * cap : (m + 1) * cap, :] = rows[x * cap : (x + 1) * cap, :]


def scaled_rows(keys, grads, slots):
    hit0, hit1 = one_hot(keys[0:2, :].astype(jnp.int32), slots)
    select = jnp.where(hit0, keys[2:3, :], 0.0) + jnp.where(hit1, keys[3:4, :], 0.0)
    return dot(select.astype(BF16), grads, 1, 0).astype(BF16)


def pick_grads_kernel(blocks, cap, keys_ref, *refs):
    grads, outs = refs[:blocks], refs[blocks:]
    for m, grad in enumerate(grads):
        rows = scaled_rows(keys_ref[m], grad[...], len(outs) * cap)
        for x, out in enumerate(outs):
            out[m * cap : (m + 1) * cap, :] = rows[x * cap : (x + 1) * cap, :]


def pick_both_kernel(cap, me_ref, message_ref, grads_ref, *outs):
    slots = len(outs) * cap
    keys, rows = named_rows(me_ref, message_ref, slots, cap)
    scaled = scaled_rows(keys, grads_ref[...], slots)
    for x, out in enumerate(outs):
        out[0:cap, :] = rows[x * cap : (x + 1) * cap, :]
        out[cap:, :] = scaled[x * cap : (x + 1) * cap, :]


def gather_group(me_ref, parts, group_ref):
    cap = parts[0].shape[0]
    for x, part in enumerate(parts):
        at = pl.multiple_of((me_ref[1] ^ x) * cap, cap)
        group_ref[pl.ds(at, cap), :] = part[...]
    return group_ref[...]


def forward_group(rows, up_ref):
    hidden = dot(rows, up_ref[...], 1, 0)
    sigmoid = jax.nn.sigmoid(hidden)
    return (hidden * sigmoid).astype(BF16), sigmoid * (1.0 + hidden * (1.0 - sigmoid))


def hidden_kernel(count, me_ref, *refs):
    parts, (up_ref, rows_ref, act_ref, slope_ref) = refs[:count], refs[count:]
    act_ref[...], slope_ref[...] = forward_group(gather_group(me_ref, parts, rows_ref), up_ref)


def backward_group(scaled, act, slope, up_ref, down_ref, pre_ref, row_ref, term_ref):
    act_grad = dot(scaled, down_ref[...], 1, 1)
    pre = (act_grad * slope).astype(BF16)
    pre_ref[...] = pre
    row_ref[0] = dot(pre, up_ref[...], 1, 1).astype(BF16)
    prod = act_grad * act.astype(F32)
    high = prod.astype(BF16)
    low = (prod - high.astype(F32)).astype(BF16)
    ones = jnp.ones((8, prod.shape[1]), BF16)
    term_ref[0] = dot(ones, high, 1, 1) + dot(ones, low, 1, 1)


def routed_kernel(count, me_ref, *refs):
    parts = refs[:count]
    act_ref, slope_ref, up_ref, down_ref = refs[count : count + 4]
    scaled_ref, pre_ref, row_ref, term_ref = refs[-4:]
    scaled = gather_group(me_ref, parts, scaled_ref)
    backward_group(
        scaled, act_ref[...], slope_ref[...], up_ref, down_ref, pre_ref, row_ref, term_ref
    )


def far_kernel(count, me_ref, *refs):
    cap = refs[0].shape[0] // 2
    up_ref, down_ref = refs[count : count + 2]
    rows_ref, act_ref, scaled_ref, pre_ref, row_ref, term_ref = refs[-6:]
    rows = gather_group(me_ref, [part.at[0:cap, :] for part in refs[:count]], rows_ref)
    act, slope = forward_group(rows, up_ref)
    act_ref[...] = act
    scaled = gather_group(me_ref, [part.at[cap:, :] for part in refs[:count]], scaled_ref)
    backward_group(scaled, act, slope, up_ref, down_ref, pre_ref, row_ref, term_ref)


def mix_kernel(planes, cap, me_ref, *refs):
    blocks, outs = refs[:planes], refs[planes:]
    group = blocks[0].shape[1]
    table = jnp.concatenate(
        [block[0:1, :] for block in blocks] + [jnp.zeros((8 - planes, group), F32)], axis=0
    )
    for x, out in enumerate(outs):
        place, lane = iota((group, 128), 0), iota((group, 128), 1)
        take = (place == (me_ref[1] ^ x) * cap + lane) & (lane < cap)
        out[...] = fine_dot(table, jnp.where(take, 1.0, 0.0).astype(BF16), 1, 0, 2)


def found_kernel(cap, shard_count, me_ref, targets_ref, gates_ref, *refs):
    tables, out_ref = refs[:-1], refs[-1]
    targets = targets_ref[...].astype(F32)
    expert = jnp.floor((targets + 0.5) * (1.0 / cap))
    rank = (targets - expert * cap).astype(jnp.int32)
    plane = jnp.floor((expert + 0.5) * (1.0 / shard_count))
    shard = (expert - plane * shard_count).astype(jnp.int32)
    row = (shard ^ me_ref[1]) * 8 + (plane.astype(jnp.int32) ^ me_ref[0])
    table = jnp.concatenate([ref[...] for ref in tables], axis=0)
    gates = gates_ref[...].astype(BF16).astype(F32)
    tokens = targets.shape[1]
    found = []
    for k in range(2):
        hit = iota((table.shape[0], tokens), 0) == row[k : k + 1, :]
        hit = jnp.where(hit, 1.0, 0.0).astype(BF16)
        values = fine_dot(table, hit, 0, 0, 2)
        mine = iota(values.shape, 0) == rank[k : k + 1, :]
        found.append(jnp.sum(jnp.where(mine, values, 0.0), axis=0, keepdims=True))
    out_ref[...] = jnp.concatenate(found, axis=0) / gates


def grouped(kernel, me, parts, each, extras, extra_specs, outs, out_specs, steps, aliases, flops):
    width = parts[0].shape[1]
    return pl.pallas_call(
        functools.partial(kernel, len(parts)),
        out_shape=outs,
        grid_spec=pltpu.PrefetchScalarGridSpec(
            num_scalar_prefetch=1,
            grid=(steps,),
            in_specs=[pl.BlockSpec((each, width), lambda i, me: (i, 0))] * len(parts) + extra_specs,
            out_specs=out_specs,
        ),
        input_output_aliases=aliases,
        compiler_params=pltpu.CompilerParams(vmem_limit_bytes=VMEM_LIMIT),
        cost_estimate=pl.CostEstimate(
            flops=flops, bytes_accessed=6 * width * width, transcendentals=0
        ),
    )(me, *from_hbm(*parts), *extras)


def outer_kernel(*refs):
    pairs, out_ref = zip(refs[0:-1:2], refs[1:-1:2]), refs[-1]
    out_ref[...] = sum(dot(a[...], b[...], 0, 0) for a, b in pairs).astype(BF16)


def outer_stage(*pairs):
    left, right = pairs[0][0].shape[1], pairs[0][1].shape[1]
    tile = min(256, right)
    column = lambda b: pl.BlockSpec((b.shape[0], tile), lambda i: (0, i))
    specs, args = [], []
    for a, b in pairs:
        specs += [one_step(a.shape), column(b)]
        args += from_hbm(a, b)
    rows = sum(a.shape[0] for a, _ in pairs)
    return call(
        outer_kernel,
        far_shape((left, right), BF16),
        *args,
        grid=(right // tile,),
        in_specs=specs,
        out_specs=pl.BlockSpec((left, tile), lambda i: (0, i)),
        cost=pl.CostEstimate(
            flops=2 * rows * left * right, bytes_accessed=6 * left * right, transcendentals=0
        ),
    )


def routed_experts(resid, out_grad, ids, gates, up, down, cap, shard_count, planes, early):
    tokens, width = resid.shape
    hidden = up.shape[1]
    group = shard_count * cap
    plane, shard = lax.axis_index("grp"), lax.axis_index("seq")
    me = jnp.stack([plane, shard]).astype(jnp.int32)
    smem = pl.BlockSpec(memory_space=pltpu.SMEM)
    vmem = pl.BlockSpec(memory_space=pltpu.VMEM)

    def across(x, bit):
        return lax.ppermute(x, "grp", [(i, i ^ bit) for i in range(planes)])

    def spread_out(parts):
        moved = [
            lax.ppermute(part, "seq", [(i, i ^ x) for i in range(shard_count)])
            for x, part in enumerate(parts)
            if x
        ]
        return [parts[0]] + moved

    def pick_rows(messages):
        count = len(messages)
        outs = [far_shape((count * cap, width), BF16)] * shard_count
        *parts, keys = streamed(
            functools.partial(pick_rows_kernel, count, cap),
            tuple(outs + [far_shape((count, 8, tokens), F32)]),
            *messages,
            scalars=me,
        )
        return parts, keys

    def pick_grads(keys, grads):
        count = len(grads)
        outs = [far_shape((count * cap, width), BF16)] * shard_count
        kernel = functools.partial(pick_grads_kernel, count, cap)
        return streamed(kernel, tuple(outs), keys, *grads)

    def pick_both(message, grad):
        outs = [far_shape((2 * cap, width), BF16)] * shard_count
        kernel = functools.partial(pick_both_kernel, cap)
        return streamed(kernel, tuple(outs), message, grad, scalars=me)

    def block(width):
        return pl.BlockSpec((group, width), lambda i, me: (i, 0))

    def hidden_stage(parts, steps):
        rows = steps * group
        return grouped(
            hidden_kernel,
            me,
            parts,
            cap,
            (up,),
            [vmem],
            (far_shape((rows, width), BF16), far_shape((rows, hidden), BF16), shape((rows, hidden), F32)),
            (block(width), block(hidden), block(hidden)),
            steps,
            {},
            2 * rows * width * hidden,
        )

    rows_of = lambda steps, size, dtype: far_shape((steps * group, size), dtype)

    def backs(steps):
        return (far_shape((planes, group, width), BF16), far_shape((steps, 8, group), F32))

    def back_blocks(base):
        return (
            pl.BlockSpec((1, group, width), lambda i, me: (me[0] ^ (base + i), 0, 0)),
            pl.BlockSpec((1, 8, group), lambda i, me: (i, 0, 0)),
        )

    def routed_stage(parts, act, slope, steps, base, filled):
        return grouped(
            routed_kernel,
            me,
            parts,
            cap,
            (act, slope, up, down, filled),
            [block(hidden), block(hidden), vmem, vmem, pl.BlockSpec(memory_space=pl.ANY)],
            (rows_of(steps, width, BF16), rows_of(steps, hidden, BF16)) + backs(steps),
            (block(width), block(hidden)) + back_blocks(base),
            steps,
            {1 + len(parts) + 4: 2},
            4 * steps * group * width * hidden,
        )

    def whole_stage(parts, base, filled):
        extra = () if filled is None else (filled,)
        return grouped(
            far_kernel,
            me,
            parts,
            2 * cap,
            (up, down) + extra,
            [vmem, vmem] + [pl.BlockSpec(memory_space=pl.ANY)] * len(extra),
            (
                rows_of(1, width, BF16),
                rows_of(1, hidden, BF16),
                rows_of(1, width, BF16),
                rows_of(1, hidden, BF16),
            )
            + backs(1),
            (block(width), block(hidden), block(width), block(hidden)) + back_blocks(base),
            1,
            {1 + len(parts) + 2: 4} if extra else {},
            6 * group * width * hidden,
        )

    message, targets = streamed(
        functools.partial(message_kernel, planes, shard_count, cap),
        (far_shape((tokens + 16, width), BF16), far_shape((2, tokens), jnp.int32)),
        resid,
        ids,
        gates,
    )
    message2 = across(message, 2)
    message1 = across(message, 1)
    grad2 = across(out_grad, 2)
    grad1 = across(out_grad, 1)
    message3 = across(message2, 1)
    own = pick_both(message, out_grad)
    own = spread_out(own)
    rows_0, act_0, scaled_0, pre_0, row_grad, own_terms = whole_stage(own, 0, None)
    near_rows, near_keys = pick_rows([message1, message2])
    near_rows = spread_out(near_rows)
    arrived, early = lax.optimization_barrier((near_rows[1], early))
    near_rows[1] = arrived
    grad3 = across(grad2, 1)
    near_grads = pick_grads(near_keys, [grad1, grad2])
    near_grads = spread_out(near_grads)
    rows_1, act_1, slope_1 = hidden_stage(near_rows, 2)
    far = pick_both(message3, grad3)
    far = spread_out(far)
    scaled_1, pre_1, row_grad, near_terms = routed_stage(near_grads, act_1, slope_1, 2, 1, row_grad)
    rows_2, act_2, scaled_2, pre_2, row_grad, far_terms = whole_stage(far, 3, row_grad)

    def finish():
        blocks = [own_terms[0]]
        blocks += [across(near_terms[bit - 1], bit) for bit in (1, 2)]
        blocks += [across(far_terms[0], 3)]
        mixed = call(
            functools.partial(mix_kernel, planes, cap),
            tuple([shape((8, 128), F32)] * shard_count),
            me,
            *blocks,
            in_specs=[smem] + [vmem] * planes,
        )
        down_grad = outer_stage((act_0, scaled_0), (act_1, scaled_1), (act_2, scaled_2))
        mixed = spread_out(mixed)
        up_grad = outer_stage((rows_0, pre_0), (rows_1, pre_1), (rows_2, pre_2))
        gate_grad = call(
            functools.partial(found_kernel, cap, shard_count),
            far_shape((2, tokens), F32),
            me,
            targets,
            gates,
            *mixed,
            in_specs=[smem] + [vmem] * (2 + shard_count),
            out_specs=vmem,
        )
        return down_grad, up_grad, gate_grad

    return targets, row_grad.reshape(-1, width), finish, early


def plain_experts(resid, out_grad, ids, gates, up, down, cap, experts, swap, early):
    tokens, width = resid.shape
    slots = experts * cap
    send_rows, targets = call(
        functools.partial(rows_kernel, experts, cap),
        (shape((slots, width), BF16), shape((2, tokens), jnp.int32)),
        resid,
        ids,
    )
    rows = swap(send_rows)
    send_scaled = call(grads_kernel, shape((slots, width), BF16), out_grad, gates, targets)
    scaled = swap(send_scaled)
    hidden = jnp.dot(rows, up, preferred_element_type=F32)
    sigmoid = jax.nn.sigmoid(hidden)
    act = (hidden * sigmoid).astype(BF16)
    slope = sigmoid * (1.0 + hidden * (1.0 - sigmoid))
    pre_grad, row_grad, term = expert_stage(scaled, act, slope, up, down)

    def finish():
        terms = swap(term.astype(BF16).reshape(experts, cap))
        gate_grad = call(
            gate_kernel,
            shape((2, tokens), F32),
            jnp.broadcast_to(terms.reshape(1, slots), (8, slots)),
            targets,
            gates,
        )
        return (
            dot(act, scaled, 0, 0).astype(BF16),
            dot(rows, pre_grad, 0, 0).astype(BF16),
            gate_grad,
        )

    return targets, row_grad, finish, early


def spread(heads, width):
    return (iota((heads, width), 1) // (width // heads) == iota((heads, width), 0)).astype(F32)


def ends_kernel(
    inputs_ref, writes_ref, decays_ref, cum_ref, cumt_ref, grown_ref, left_ref, faded_ref, send_ref
):
    decays = decays_ref[...]
    heads, tokens = decays.shape
    parts, padded, width = send_ref.shape
    upto = (iota((tokens, tokens), 0) >= iota((tokens, tokens), 1)).astype(BF16)
    cum = sum(dot(upto, part, 1, 1) for part in pieces_of(decays, 3))
    cum_ref[...] = cum
    cumt = fine_dot(decays, upto, 1, 1, 3)
    for head in range(heads):
        cumt_ref[head] = cumt[head : head + 1, :]
    total = cum[tokens - 1 : tokens, :]
    wide = spread(heads, width).astype(BF16)
    grown_ref[...] = fine_dot(jnp.exp(cum), wide, 1, 0, 1).astype(BF16)
    remaining = fine_dot(jnp.exp(total - cum), wide, 1, 0, 2)
    left_ref[...] = remaining.astype(BF16)
    scaled = (inputs_ref[...].astype(F32) * remaining).astype(BF16)
    faded_ref[...] = scaled
    ends = dot(writes_ref[...], scaled, 0, 0)
    kept = fine_dot(jnp.exp(jnp.broadcast_to(total, (8, heads))), wide, 1, 0, 3)[0:1, :]
    high, low = pieces_of(kept, 2)
    rows = ends.shape[0] // parts
    for part in range(parts):
        send_ref[part, 0:rows, :] = ends[part * rows : (part + 1) * rows, :].astype(BF16)
        send_ref[part, rows : rows + 1, :] = high
        send_ref[part, rows + 1 : rows + 2, :] = low
        send_ref[part, rows + 2 :, :] = jnp.zeros((padded - rows - 2, width), BF16)


def scan_kernel(reverse, ends_ref, kept_ref, out_ref):
    parts, rows, _ = out_ref.shape
    state = jnp.zeros(out_ref.shape[1:], F32)
    for step in range(parts):
        at = parts - 1 - step if reverse else step
        out_ref[at] = state.astype(BF16)
        kept = kept_ref[at, rows : rows + 1, :].astype(F32) + kept_ref[
            at, rows + 1 : rows + 2, :
        ].astype(F32)
        state = state * kept + ends_ref[at, 0:rows, :].astype(F32)


def home_kernel(
    back_ref, targets_ref, resid_ref, out_grad_ref, reads_ref, grown_ref, grad_ref, adjoint_ref
):
    hit0, hit1 = one_hot(targets_ref[...], back_ref.shape[0])
    select = jnp.where(hit0 | hit1, 1.0, 0.0).astype(BF16)
    d_normed = dot(select, back_ref[...], 0, 0)
    resid = resid_ref[...].astype(F32)
    inverse = lax.rsqrt(jnp.mean(resid * resid, axis=1, keepdims=True) + EPSILON)
    normed = resid * inverse
    mean = jnp.mean(d_normed * normed, axis=1, keepdims=True)
    grad = (out_grad_ref[...].astype(F32) + inverse * (d_normed - normed * mean)).astype(BF16)
    grad_ref[...] = grad
    scaled = (grad.astype(F32) * grown_ref[...].astype(F32)).astype(BF16)
    adjoint_ref[...] = dot(reads_ref[...], scaled, 0, 0).astype(BF16)


def inside_kernel(
    base,
    inputs_ref,
    grads_ref,
    writes_ref,
    reads_ref,
    state_ref,
    cum_ref,
    cumt_ref,
    dx_ref,
    dwrite_ref,
    dread_ref,
    dcum_ref,
    dcumt_ref,
    score_ref,
    total_ref,
):
    step = pl.program_id(0)
    steps = pl.num_programs(0)
    tokens, lanes = inputs_ref.shape
    each = cumt_ref.shape[0]
    size = lanes // each

    @pl.when(step == 0)
    def _():
        score_ref[...] = dot(reads_ref[...], writes_ref[...], 1, 1)
        total_ref[...] = jnp.zeros_like(total_ref)
        dread_ref[...] = jnp.zeros_like(dread_ref)
        dcum_ref[...] = jnp.zeros_like(dcum_ref)

    inputs = inputs_ref[...]
    grads = grads_ref[...]
    cum = cum_ref[...]
    scores = score_ref[...]
    causal = iota((tokens, tokens), 0) >= iota((tokens, tokens), 1)
    column = iota(cum.shape, 1)
    lane = iota((tokens, lanes), 1) // size
    dx = jnp.zeros((tokens, lanes), F32)
    sums = jnp.zeros(cum.shape, F32)
    grown = jnp.zeros((tokens, lanes), F32)
    state = state_ref[...]
    read_state = dot(reads_ref[...], state, 1, 0)
    inter = grads.astype(F32) * read_state
    total = jnp.zeros((tokens, tokens), F32)
    for k in range(each):
        head = (base + step) * each + k
        at_t = jnp.sum(jnp.where(column == head, cum, 0.0), axis=1, keepdims=True)
        at_s = cumt_ref[k]
        decay = jnp.exp(jnp.where(causal, at_t - at_s, -1e30))
        mine = lane == k
        grads_k = jnp.where(mine, grads, jnp.zeros_like(grads))
        weights = dot(grads_k, inputs, 1, 1) * decay
        total = total + weights
        dx = dx + dot((decay * scores).astype(BF16), grads_k, 0, 0)
        both = weights * scores
        grow = jnp.exp(at_t)
        row = jnp.sum(both, axis=1, keepdims=True) + grow * jnp.sum(
            jnp.where(mine, inter, 0.0), axis=1, keepdims=True
        )
        sums = sums + jnp.where(column == head, row, 0.0)
        dcumt_ref[k] = jnp.sum(both, axis=0, keepdims=True)
        grown = grown + jnp.where(mine, grow, 0.0)
    total_ref[...] += total
    dcum_ref[...] += sums
    dx_ref[...] = dx.astype(BF16)
    dread_ref[...] += dot((grown * grads.astype(F32)).astype(BF16), state, 1, 1)

    @pl.when(step == steps - 1)
    def _():
        total_b = total_ref[...].astype(BF16)
        dread_ref[...] += dot(total_b, writes_ref[...], 1, 0)
        dwrite_ref[...] = dot(total_b, reads_ref[...], 0, 0)


def inside_stage(inputs, grads, writes, reads, state, cum, cumt, half):
    tokens, width = inputs.shape
    heads = cum.shape[1]
    n = writes.shape[1]
    lanes = max(128, width // heads)
    steps = width // lanes // 2
    each = heads // (width // lanes)
    base = half * steps
    part = pl.BlockSpec((tokens, lanes), lambda i: (0, base + i))
    return call(
        functools.partial(inside_kernel, base),
        (
            far_shape((tokens, width // 2), BF16),
            far_shape((tokens, n), F32),
            far_shape((tokens, n), F32),
            far_shape((tokens, heads), F32),
            far_shape((heads // 2, 1, tokens), F32),
        ),
        *from_hbm(inputs, grads, writes, reads, state, cum, cumt),
        grid=(steps,),
        in_specs=[
            part,
            part,
            one_step((tokens, n)),
            one_step((tokens, n)),
            pl.BlockSpec((n, lanes), lambda i: (0, base + i)),
            one_step((tokens, heads)),
            pl.BlockSpec((each, 1, tokens), lambda i: (base + i, 0, 0)),
        ],
        out_specs=(
            pl.BlockSpec((tokens, lanes), lambda i: (0, i)),
            one_step((tokens, n)),
            one_step((tokens, n)),
            one_step((tokens, heads)),
            pl.BlockSpec((each, 1, tokens), lambda i: (i, 0, 0)),
        ),
        scratch=[pltpu.VMEM((tokens, tokens), F32), pltpu.VMEM((tokens, tokens), F32)],
        cost=pl.CostEstimate(
            flops=4 * tokens * tokens * width,
            bytes_accessed=4 * tokens * width,
            transcendentals=heads * tokens * tokens // 2,
        ),
    )


def last_kernel(
    writes_ref,
    state_ref,
    adjoint_ref,
    cumt_ref,
    left_ref,
    faded_ref,
    dx0_ref,
    dwrite0_ref,
    dread0_ref,
    dcum0_ref,
    dcumt0_ref,
    dx1_ref,
    dwrite1_ref,
    dread1_ref,
    dcum1_ref,
    dcumt1_ref,
    input_grad_ref,
    dwrite_ref,
    dread_ref,
    decay_ref,
):
    tokens, width = left_ref.shape
    heads = cumt_ref.shape[0]
    half = width // 2
    wide = spread(heads, width).astype(BF16)
    adjoint = adjoint_ref[...]
    faded = faded_ref[...]
    values = dot(writes_ref[...], adjoint, 1, 0)
    moved = left_ref[...].astype(F32) * values
    input_grad_ref[:, 0:half] = (dx0_ref[...].astype(F32) + moved[:, 0:half]).astype(BF16)
    input_grad_ref[:, half:] = (dx1_ref[...].astype(F32) + moved[:, half:]).astype(BF16)
    dwrite_ref[...] = dwrite0_ref[...] + dwrite1_ref[...] + dot(faded, adjoint, 1, 1)
    dread_ref[...] = dread0_ref[...] + dread1_ref[...]
    shares = pieces_of(values * faded.astype(F32), 2)
    shares = sum(dot(wide, part, 1, 1) for part in shares)
    kept = jnp.sum(state_ref[...].astype(F32) * adjoint.astype(F32), axis=0, keepdims=True)
    kept = pieces_of(jnp.broadcast_to(kept, (8, width)), 3)
    kept = sum(dot(wide, part, 1, 1) for part in kept)[:, 0:1]
    flow = [ref[h] for ref in (dcumt0_ref, dcumt1_ref) for h in range(heads // 2)]
    total = jnp.concatenate([cumt_ref[h][:, tokens - 1 : tokens] for h in range(heads)], axis=0)
    after = (iota((tokens, tokens), 1) >= iota((tokens, tokens), 0)).astype(BF16)
    rows = -jnp.concatenate(flow, axis=0) - shares
    columns = dcum0_ref[...] + dcum1_ref[...]
    decay_ref[...] = (
        sum(dot(part, after, 0, 1) for part in pieces_of(columns, 3))
        + sum(dot(part, after, 1, 1) for part in pieces_of(rows, 3))
        + jnp.sum(shares, axis=1, keepdims=True)
        + kept * jnp.exp(total)
    )


def shards(
    mixer_input,
    write_proj,
    read_proj,
    log_decay,
    resid,
    out_grad,
    gate_probs,
    expert_ids,
    expert_up,
    expert_down,
):
    tokens, width = resid.shape
    heads = log_decay.shape[1]
    n = write_proj.shape[1]
    shard_count = lax.axis_size("seq")
    experts = lax.axis_size("grp") * shard_count
    cap = 4 * tokens // experts
    everyone = ("grp", "seq")
    up, down = expert_up[0], expert_down[0]
    ids = expert_ids.T
    gates = gate_probs.T

    def swap(x, axes):
        return lax.all_to_all(x, axes, split_axis=0, concat_axis=0, tiled=True)

    state_rows = n // shard_count
    padded = -(-(state_rows + 2) // 8) * 8
    cum, cumt, grown, left, faded, send_ends = streamed(
        ends_kernel,
        (
            far_shape((tokens, heads), F32),
            far_shape((heads, 1, tokens), F32),
            far_shape((tokens, width), BF16),
            far_shape((tokens, width), BF16),
            far_shape((tokens, width), BF16),
            far_shape((shard_count, padded, width), BF16),
        ),
        mixer_input,
        write_proj,
        log_decay.T,
    )
    ends = swap(send_ends, "seq")
    parts = far_shape((shard_count, state_rows, width), BF16)
    starts = call(functools.partial(scan_kernel, False), parts, ends, ends)
    state = swap(starts, "seq").reshape(n, width)

    planes = experts // shard_count
    if planes == 4 and shard_count <= 8 and cap in (16, 32, 64, 128) and tokens <= width:
        targets, row_grad, finish, state = routed_experts(
            resid, out_grad, ids, gates, up, down, cap, shard_count, planes, state
        )
    else:
        targets, row_grad, finish, state = plain_experts(
            resid, out_grad, ids, gates, up, down, cap, experts, lambda x: swap(x, everyone), state
        )
    back = swap(row_grad, everyone)
    down_grad, up_grad, gate_grad = finish()
    back, down_grad, up_grad = lax.optimization_barrier((back, down_grad, up_grad))
    resid_grad, send_adjoint = streamed(
        home_kernel,
        (far_shape((tokens, width), BF16), far_shape((n, width), BF16)),
        back,
        targets,
        resid,
        out_grad,
        read_proj,
        grown,
        near=(0,),
    )
    adjoints = swap(send_adjoint.reshape(shard_count, state_rows, width), "seq")
    inside = (mixer_input, resid_grad, write_proj, read_proj, state, cum, cumt)
    first = inside_stage(*inside, 0)
    later = call(functools.partial(scan_kernel, True), parts, adjoints, ends)
    adjoint = swap(later, "seq").reshape(n, width)
    second = inside_stage(*inside, 1)
    input_grad, write_grad, read_grad, decay_grad = streamed(
        last_kernel,
        (
            far_shape((tokens, width), BF16),
            far_shape((tokens, n), F32),
            far_shape((tokens, n), F32),
            far_shape((heads, tokens), F32),
        ),
        write_proj,
        state,
        adjoint,
        cumt,
        left,
        faded,
        *first,
        *second,
        near=(2,),
    )
    return (
        input_grad,
        write_grad,
        read_grad,
        decay_grad.T,
        resid_grad,
        gate_grad.T.astype(BF16),
        up_grad[None],
        down_grad[None],
    )


def solution(mesh):
    flat = P(("grp", "seq"), None)
    cube = P(("grp", "seq"), None, None)
    return jax.shard_map(
        shards,
        mesh=mesh,
        in_specs=(flat,) * 8 + (cube,) * 2,
        out_specs=(flat,) * 6 + (cube,) * 2,
        check_vma=False,
    )
```

```python
import functools

import jax
import jax.numpy as jnp
from jax import lax
from jax.experimental import pallas as pl
from jax.experimental.pallas import tpu as pltpu
from jax.sharding import PartitionSpec as P


EPSILON = 1e-06
F32 = jnp.float32
BF16 = jnp.bfloat16
VMEM_LIMIT = 20 * 1024 * 1024


def iota(shape, axis):
    return lax.broadcasted_iota(jnp.int32, shape, axis)


def dot(a, b, ca, cb, precision=None):
    return lax.dot_general(
        a, b, (((ca,), (cb,)), ((), ())), precision=precision, preferred_element_type=F32
    )


def call(kernel, outs, *args, grid=None, in_specs=None, out_specs=None, scratch=(), cost=None):
    whole = pl.BlockSpec(memory_space=pltpu.VMEM)
    many = isinstance(outs, (tuple, list))
    kwargs = {}
    if grid is not None:
        kwargs["grid"] = grid
    return pl.pallas_call(
        kernel,
        out_shape=outs,
        in_specs=in_specs if in_specs is not None else [whole] * len(args),
        out_specs=out_specs
        if out_specs is not None
        else (tuple([whole] * len(outs)) if many else whole),
        scratch_shapes=list(scratch),
        compiler_params=pltpu.CompilerParams(vmem_limit_bytes=VMEM_LIMIT),
        cost_estimate=cost,
        **kwargs,
    )(*args)


def pieces_of(x, count):
    parts = []
    for _ in range(count):
        part = x.astype(BF16)
        parts.append(part)
        x = x - part.astype(F32)
    return parts


def fine_dot(a, exact, ca, cb, count):
    return sum(dot(part, exact, ca, cb) for part in pieces_of(a, count))


def shape(dims, dtype):
    return jax.ShapeDtypeStruct(dims, dtype)


def far_shape(dims, dtype):
    return pltpu.HBM(dims, dtype)


def from_hbm(*arrays):
    return [pltpu.with_memory_space_constraint(x, pltpu.HBM) for x in arrays]


def one_step(dims):
    return pl.BlockSpec(dims, lambda i: (0,) * len(dims))


def streamed(kernel, outs, *args, near=(), scalars=None):
    fixed = [x if k in near else from_hbm(x)[0] for k, x in enumerate(args)]
    specs = [one_step(x.shape) for x in args]
    if scalars is not None:
        fixed = [scalars] + fixed
        specs = [pl.BlockSpec(memory_space=pltpu.SMEM)] + specs
    many = isinstance(outs, (tuple, list))
    blocks = tuple(one_step(out.shape) for out in outs) if many else one_step(outs.shape)
    return call(
        kernel,
        outs,
        *fixed,
        grid=(1,),
        in_specs=specs,
        out_specs=blocks,
    )


def one_hot(targets, slots):
    slot = iota((slots, targets.shape[1]), 0)
    first = slot == targets[0:1, :]
    second = slot == targets[1:2, :]
    return first, second


def rows_kernel(experts, cap, resid_ref, ids_ref, rows_ref, targets_ref):
    resid = resid_ref[...].astype(F32)
    inverse = lax.rsqrt(jnp.mean(resid * resid, axis=1, keepdims=True) + EPSILON)
    normed_b = (resid * inverse).astype(BF16)
    ids = ids_ref[...]
    tokens = ids.shape[1]
    number = iota((experts, tokens), 0)
    first = (number == ids[0:1, :]).astype(F32)
    second = (number == ids[1:2, :]).astype(F32)
    earlier = (iota((tokens, tokens), 0) < iota((tokens, tokens), 1)).astype(BF16)
    before = dot((first + second).astype(BF16), earlier, 1, 0)
    rank0 = jnp.sum(before * first, axis=0, keepdims=True).astype(jnp.int32)
    rank1 = jnp.sum(before * second, axis=0, keepdims=True).astype(jnp.int32)
    targets = jnp.concatenate([ids[0:1, :] * cap + rank0, ids[1:2, :] * cap + rank1], axis=0)
    targets_ref[...] = targets
    hit0, hit1 = one_hot(targets, experts * cap)
    select = jnp.where(hit0 | hit1, 1.0, 0.0).astype(BF16)
    rows_ref[...] = dot(select, normed_b, 1, 0).astype(BF16)


def grads_kernel(out_grad_ref, gates_ref, targets_ref, rows_ref):
    slots = rows_ref.shape[0]
    hit0, hit1 = one_hot(targets_ref[...], slots)
    gates = gates_ref[...].astype(BF16).astype(F32)
    select = jnp.where(hit0, gates[0:1, :], 0.0) + jnp.where(hit1, gates[1:2, :], 0.0)
    rows_ref[...] = dot(select.astype(BF16), out_grad_ref[...], 1, 0).astype(BF16)


def expert_kernel(scaled_ref, act_ref, slope_ref, up_ref, down_ref, pre_ref, row_ref, term_ref):
    act_grad = dot(scaled_ref[...], down_ref[...], 1, 1)
    pre = (act_grad * slope_ref[...]).astype(BF16)
    pre_ref[...] = pre
    row_ref[...] = dot(pre, up_ref[...], 1, 1).astype(BF16)
    prod = act_grad * act_ref[...].astype(F32)
    high = prod.astype(BF16)
    low = (prod - high.astype(F32)).astype(BF16)
    ones = jnp.ones((8, prod.shape[1]), BF16)
    term_ref[...] = (dot(ones, high, 1, 1) + dot(ones, low, 1, 1))[None]


def expert_stage(scaled, act, slope, up, down):
    rows, width = scaled.shape
    hidden = act.shape[1]
    tile = min(256, rows)
    steps = rows // tile
    by_rows = lambda w: pl.BlockSpec((tile, w), lambda i: (i, 0))
    whole = pl.BlockSpec(memory_space=pltpu.VMEM)
    pre, row_grad, term = call(
        expert_kernel,
        (shape((rows, hidden), BF16), shape((rows, width), BF16), shape((steps, 8, tile), F32)),
        scaled,
        act,
        slope,
        up,
        down,
        grid=(steps,),
        in_specs=[by_rows(width), by_rows(hidden), by_rows(hidden), whole, whole],
        out_specs=(by_rows(hidden), by_rows(width), pl.BlockSpec((1, 8, tile), lambda i: (i, 0, 0))),
        cost=pl.CostEstimate(
            flops=4 * rows * width * hidden, bytes_accessed=20 * rows * width, transcendentals=0
        ),
    )
    return pre, row_grad, term[:, 0, :].reshape(-1)


def gate_kernel(terms_ref, targets_ref, gates_ref, out_ref):
    slots = terms_ref.shape[1]
    hit0, hit1 = one_hot(targets_ref[...], slots)
    terms = terms_ref[...]
    gates = gates_ref[...].astype(BF16).astype(F32)
    first = dot(terms, jnp.where(hit0, 1.0, 0.0).astype(BF16), 1, 0)
    second = dot(terms, jnp.where(hit1, 1.0, 0.0).astype(BF16), 1, 0)
    out_ref[...] = jnp.concatenate([first[0:1, :], second[0:1, :]], axis=0) / gates


def message_kernel(planes, shard_count, cap, resid_ref, ids_ref, gates_ref, message_ref, targets_ref):
    tokens, width = resid_ref.shape
    experts = planes * shard_count
    resid = resid_ref[...].astype(F32)
    inverse = lax.rsqrt(jnp.mean(resid * resid, axis=1, keepdims=True) + EPSILON)
    message_ref[0:tokens, :] = (resid * inverse).astype(BF16)
    ids = ids_ref[...]
    number = iota((experts, tokens), 0)
    first = (number == ids[0:1, :]).astype(F32)
    second = (number == ids[1:2, :]).astype(F32)
    earlier = (iota((tokens, tokens), 0) < iota((tokens, tokens), 1)).astype(BF16)
    before = dot((first + second).astype(BF16), earlier, 1, 0)
    ranks = jnp.concatenate(
        [
            jnp.sum(before * first, axis=0, keepdims=True),
            jnp.sum(before * second, axis=0, keepdims=True),
        ],
        axis=0,
    )
    targets_ref[...] = ids * cap + ranks.astype(jnp.int32)
    named = ids.astype(F32)
    plane = jnp.floor((named + 0.5) * (1.0 / shard_count))
    shard = named - plane * shard_count
    facts = jnp.concatenate(
        [plane, shard, ranks, gates_ref[...], jnp.zeros((8, tokens), F32)], axis=0
    )
    message_ref[tokens:, 0:tokens] = facts.astype(BF16)
    if width > tokens:
        message_ref[tokens:, tokens:] = jnp.zeros((16, width - tokens), BF16)


def named_rows(me_ref, message, slots, cap):
    tokens = message.shape[0] - 16
    facts = message[tokens:, 0:tokens].astype(F32)
    places = (facts[2:4, :].astype(jnp.int32) ^ me_ref[1]) * cap
    places = places + facts[4:6, :].astype(jnp.int32)
    places = jnp.where(facts[0:2, :] == me_ref[0].astype(F32), places, -1)
    hit0, hit1 = one_hot(places, slots)
    select = jnp.where(hit0 | hit1, 1.0, 0.0).astype(BF16)
    rows = dot(select, message[0:tokens, :], 1, 0).astype(BF16)
    keys = jnp.concatenate(
        [places.astype(F32), facts[6:8, :], jnp.zeros((4, tokens), F32)], axis=0
    )
    return keys, rows


def pick_rows_kernel(blocks, cap, me_ref, *refs):
    messages, outs, keys_ref = refs[:blocks], refs[blocks:-1], refs[-1]
    for m, message in enumerate(messages):
        keys_ref[m], rows = named_rows(me_ref, message, len(outs) * cap, cap)
        for x, out in enumerate(outs):
            out[m * cap : (m + 1) * cap, :] = rows[x * cap : (x + 1) * cap, :]


def scaled_rows(keys, grads, slots):
    hit0, hit1 = one_hot(keys[0:2, :].astype(jnp.int32), slots)
    select = jnp.where(hit0, keys[2:3, :], 0.0) + jnp.where(hit1, keys[3:4, :], 0.0)
    return dot(select.astype(BF16), grads, 1, 0).astype(BF16)


def pick_grads_kernel(blocks, cap, keys_ref, *refs):
    grads, outs = refs[:blocks], refs[blocks:]
    for m, grad in enumerate(grads):
        rows = scaled_rows(keys_ref[m], grad[...], len(outs) * cap)
        for x, out in enumerate(outs):
            out[m * cap : (m + 1) * cap, :] = rows[x * cap : (x + 1) * cap, :]


def pick_both_kernel(cap, me_ref, message_ref, grads_ref, *outs):
    slots = len(outs) * cap
    keys, rows = named_rows(me_ref, message_ref, slots, cap)
    scaled = scaled_rows(keys, grads_ref[...], slots)
    for x, out in enumerate(outs):
        out[0:cap, :] = rows[x * cap : (x + 1) * cap, :]
        out[cap:, :] = scaled[x * cap : (x + 1) * cap, :]


def gather_group(me_ref, parts, group_ref):
    cap = parts[0].shape[0]
    for x, part in enumerate(parts):
        at = pl.multiple_of((me_ref[1] ^ x) * cap, cap)
        group_ref[pl.ds(at, cap), :] = part[...]
    return group_ref[...]


def forward_group(rows, up_ref):
    hidden = dot(rows, up_ref[...], 1, 0)
    sigmoid = jax.nn.sigmoid(hidden)
    return (hidden * sigmoid).astype(BF16), sigmoid * (1.0 + hidden * (1.0 - sigmoid))


def hidden_kernel(count, me_ref, *refs):
    parts, (up_ref, rows_ref, act_ref, slope_ref) = refs[:count], refs[count:]
    act_ref[...], slope_ref[...] = forward_group(gather_group(me_ref, parts, rows_ref), up_ref)


def backward_group(scaled, act, slope, up_ref, down_ref, pre_ref, row_ref, term_ref):
    act_grad = dot(scaled, down_ref[...], 1, 1)
    pre = (act_grad * slope).astype(BF16)
    pre_ref[...] = pre
    row_ref[0] = dot(pre, up_ref[...], 1, 1).astype(BF16)
    prod = act_grad * act.astype(F32)
    high = prod.astype(BF16)
    low = (prod - high.astype(F32)).astype(BF16)
    ones = jnp.ones((8, prod.shape[1]), BF16)
    term_ref[0] = dot(ones, high, 1, 1) + dot(ones, low, 1, 1)


def routed_kernel(count, me_ref, *refs):
    parts = refs[:count]
    act_ref, slope_ref, up_ref, down_ref = refs[count : count + 4]
    scaled_ref, pre_ref, row_ref, term_ref = refs[-4:]
    scaled = gather_group(me_ref, parts, scaled_ref)
    backward_group(
        scaled, act_ref[...], slope_ref[...], up_ref, down_ref, pre_ref, row_ref, term_ref
    )


def far_kernel(count, me_ref, *refs):
    cap = refs[0].shape[0] // 2
    up_ref, down_ref = refs[count : count + 2]
    rows_ref, act_ref, scaled_ref, pre_ref, row_ref, term_ref = refs[-6:]
    rows = gather_group(me_ref, [part.at[0:cap, :] for part in refs[:count]], rows_ref)
    act, slope = forward_group(rows, up_ref)
    act_ref[...] = act
    scaled = gather_group(me_ref, [part.at[cap:, :] for part in refs[:count]], scaled_ref)
    backward_group(scaled, act, slope, up_ref, down_ref, pre_ref, row_ref, term_ref)


def mix_kernel(planes, cap, me_ref, *refs):
    blocks, outs = refs[:planes], refs[planes:]
    group = blocks[0].shape[1]
    table = jnp.concatenate(
        [block[0:1, :] for block in blocks] + [jnp.zeros((8 - planes, group), F32)], axis=0
    )
    for x, out in enumerate(outs):
        place, lane = iota((group, 128), 0), iota((group, 128), 1)
        take = (place == (me_ref[1] ^ x) * cap + lane) & (lane < cap)
        out[...] = fine_dot(table, jnp.where(take, 1.0, 0.0).astype(BF16), 1, 0, 2)


def found_kernel(cap, shard_count, me_ref, targets_ref, gates_ref, *refs):
    tables, out_ref = refs[:-1], refs[-1]
    targets = targets_ref[...].astype(F32)
    expert = jnp.floor((targets + 0.5) * (1.0 / cap))
    rank = (targets - expert * cap).astype(jnp.int32)
    plane = jnp.floor((expert + 0.5) * (1.0 / shard_count))
    shard = (expert - plane * shard_count).astype(jnp.int32)
    row = (shard ^ me_ref[1]) * 8 + (plane.astype(jnp.int32) ^ me_ref[0])
    table = jnp.concatenate([ref[...] for ref in tables], axis=0)
    gates = gates_ref[...].astype(BF16).astype(F32)
    tokens = targets.shape[1]
    found = []
    for k in range(2):
        hit = iota((table.shape[0], tokens), 0) == row[k : k + 1, :]
        hit = jnp.where(hit, 1.0, 0.0).astype(BF16)
        values = fine_dot(table, hit, 0, 0, 2)
        mine = iota(values.shape, 0) == rank[k : k + 1, :]
        found.append(jnp.sum(jnp.where(mine, values, 0.0), axis=0, keepdims=True))
    out_ref[...] = jnp.concatenate(found, axis=0) / gates


def grouped(kernel, me, parts, each, extras, extra_specs, outs, out_specs, steps, aliases, flops):
    width = parts[0].shape[1]
    return pl.pallas_call(
        functools.partial(kernel, len(parts)),
        out_shape=outs,
        grid_spec=pltpu.PrefetchScalarGridSpec(
            num_scalar_prefetch=1,
            grid=(steps,),
            in_specs=[pl.BlockSpec((each, width), lambda i, me: (i, 0))] * len(parts) + extra_specs,
            out_specs=out_specs,
        ),
        input_output_aliases=aliases,
        compiler_params=pltpu.CompilerParams(vmem_limit_bytes=VMEM_LIMIT),
        cost_estimate=pl.CostEstimate(
            flops=flops, bytes_accessed=6 * width * width, transcendentals=0
        ),
    )(me, *parts, *extras)


def outer_kernel(*refs):
    pairs, out_ref = zip(refs[0:-1:2], refs[1:-1:2]), refs[-1]
    out_ref[...] = sum(dot(a[...], b[...], 0, 0) for a, b in pairs).astype(BF16)


def outer_stage(*pairs):
    left, right = pairs[0][0].shape[1], pairs[0][1].shape[1]
    tile = min(256, right)
    column = lambda b: pl.BlockSpec((b.shape[0], tile), lambda i: (0, i))
    specs, args = [], []
    for a, b in pairs:
        specs += [one_step(a.shape), column(b)]
        args += from_hbm(a, b)
    rows = sum(a.shape[0] for a, _ in pairs)
    return call(
        outer_kernel,
        far_shape((left, right), BF16),
        *args,
        grid=(right // tile,),
        in_specs=specs,
        out_specs=pl.BlockSpec((left, tile), lambda i: (0, i)),
        cost=pl.CostEstimate(
            flops=2 * rows * left * right, bytes_accessed=6 * left * right, transcendentals=0
        ),
    )


def routed_experts(resid, out_grad, ids, gates, up, down, cap, shard_count, planes, early):
    tokens, width = resid.shape
    hidden = up.shape[1]
    group = shard_count * cap
    plane, shard = lax.axis_index("grp"), lax.axis_index("seq")
    me = jnp.stack([plane, shard]).astype(jnp.int32)
    smem = pl.BlockSpec(memory_space=pltpu.SMEM)
    vmem = pl.BlockSpec(memory_space=pltpu.VMEM)

    def across(x, bit):
        return lax.ppermute(x, "grp", [(i, i ^ bit) for i in range(planes)])

    def spread_out(parts):
        moved = [
            lax.ppermute(part, "seq", [(i, i ^ x) for i in range(shard_count)])
            for x, part in enumerate(parts)
            if x
        ]
        return [parts[0]] + moved

    def pick_rows(messages):
        count = len(messages)
        outs = [far_shape((count * cap, width), BF16)] * shard_count
        *parts, keys = streamed(
            functools.partial(pick_rows_kernel, count, cap),
            tuple(outs + [far_shape((count, 8, tokens), F32)]),
            *messages,
            scalars=me,
        )
        return parts, keys

    def pick_grads(keys, grads):
        count = len(grads)
        outs = [far_shape((count * cap, width), BF16)] * shard_count
        kernel = functools.partial(pick_grads_kernel, count, cap)
        return streamed(kernel, tuple(outs), keys, *grads)

    def pick_both(message, grad, near):
        outs = [far_shape((2 * cap, width), BF16)] * shard_count
        kernel = functools.partial(pick_both_kernel, cap)
        return streamed(kernel, tuple(outs), message, grad, scalars=me, near=near)

    def block(width):
        return pl.BlockSpec((group, width), lambda i, me: (i, 0))

    def hidden_stage(parts, steps):
        parts = from_hbm(*parts)
        rows = steps * group
        return grouped(
            hidden_kernel,
            me,
            parts,
            cap,
            (up,),
            [vmem],
            (far_shape((rows, width), BF16), far_shape((rows, hidden), BF16), shape((rows, hidden), F32)),
            (block(width), block(hidden), block(hidden)),
            steps,
            {},
            2 * rows * width * hidden,
        )

    rows_of = lambda steps, size, dtype: far_shape((steps * group, size), dtype)

    def backs(steps):
        return (far_shape((planes, group, width), BF16), far_shape((steps, 8, group), F32))

    def back_blocks(base):
        return (
            pl.BlockSpec((1, group, width), lambda i, me: (me[0] ^ (base + i), 0, 0)),
            pl.BlockSpec((1, 8, group), lambda i, me: (i, 0, 0)),
        )

    def routed_stage(parts, act, slope, steps, base, filled):
        return grouped(
            routed_kernel,
            me,
            parts,
            cap,
            (act, slope, up, down, filled),
            [block(hidden), block(hidden), vmem, vmem, pl.BlockSpec(memory_space=pl.ANY)],
            (rows_of(steps, width, BF16), rows_of(steps, hidden, BF16)) + backs(steps),
            (block(width), block(hidden)) + back_blocks(base),
            steps,
            {1 + len(parts) + 4: 2},
            4 * steps * group * width * hidden,
        )

    def whole_stage(parts, base, filled):
        extra = () if filled is None else (filled,)
        return grouped(
            far_kernel,
            me,
            parts,
            2 * cap,
            (up, down) + extra,
            [vmem, vmem] + [pl.BlockSpec(memory_space=pl.ANY)] * len(extra),
            (
                rows_of(1, width, BF16),
                rows_of(1, hidden, BF16),
                rows_of(1, width, BF16),
                rows_of(1, hidden, BF16),
            )
            + backs(1),
            (block(width), block(hidden), block(width), block(hidden)) + back_blocks(base),
            1,
            {1 + len(parts) + 2: 4} if extra else {},
            6 * group * width * hidden,
        )

    message, targets = streamed(
        functools.partial(message_kernel, planes, shard_count, cap),
        (far_shape((tokens + 16, width), BF16), far_shape((2, tokens), jnp.int32)),
        resid,
        ids,
        gates,
    )
    message2 = across(message, 2)
    message1 = across(message, 1)
    grad2 = across(out_grad, 2)
    grad1 = across(out_grad, 1)
    message3 = across(message2, 1)
    own = pick_both(message, out_grad, ())
    own = spread_out(own)
    own = from_hbm(*own)
    rows_0, act_0, scaled_0, pre_0, row_grad, own_terms = whole_stage(own, 0, None)
    near_rows, near_keys = pick_rows([message1, message2])
    near_rows = spread_out(near_rows)
    arrived, early = lax.optimization_barrier((near_rows[1], early))
    near_rows[1] = arrived
    grad3 = across(grad2, 1)
    near_grads = pick_grads(near_keys, [grad1, grad2])
    near_grads = spread_out(near_grads)
    rows_1, act_1, slope_1 = hidden_stage(near_rows, 2)
    far = pick_both(message3, grad3, (0, 1))
    far = spread_out(far)
    scaled_1, pre_1, row_grad, near_terms = routed_stage(near_grads, act_1, slope_1, 2, 1, row_grad)
    rows_2, act_2, scaled_2, pre_2, row_grad, far_terms = whole_stage(far, 3, row_grad)

    def finish():
        blocks = [own_terms[0]]
        blocks += [across(near_terms[bit - 1], bit) for bit in (1, 2)]
        blocks += [across(far_terms[0], 3)]
        down_grad = outer_stage((act_0, scaled_0), (act_1, scaled_1), (act_2, scaled_2))
        up_grad = outer_stage((rows_0, pre_0), (rows_1, pre_1), (rows_2, pre_2))
        blocks, down_grad, up_grad = lax.optimization_barrier((blocks, down_grad, up_grad))
        mixed = call(
            functools.partial(mix_kernel, planes, cap),
            tuple([shape((8, 128), F32)] * shard_count),
            me,
            *blocks,
            in_specs=[smem] + [vmem] * planes,
        )
        mixed = spread_out(mixed)
        gate_grad = call(
            functools.partial(found_kernel, cap, shard_count),
            far_shape((2, tokens), F32),
            me,
            targets,
            gates,
            *mixed,
            in_specs=[smem] + [vmem] * (2 + shard_count),
            out_specs=vmem,
        )
        return down_grad, up_grad, gate_grad

    return targets, row_grad.reshape(-1, width), finish, early


def plain_experts(resid, out_grad, ids, gates, up, down, cap, experts, swap, early):
    tokens, width = resid.shape
    slots = experts * cap
    send_rows, targets = call(
        functools.partial(rows_kernel, experts, cap),
        (shape((slots, width), BF16), shape((2, tokens), jnp.int32)),
        resid,
        ids,
    )
    rows = swap(send_rows)
    send_scaled = call(grads_kernel, shape((slots, width), BF16), out_grad, gates, targets)
    scaled = swap(send_scaled)
    hidden = jnp.dot(rows, up, preferred_element_type=F32)
    sigmoid = jax.nn.sigmoid(hidden)
    act = (hidden * sigmoid).astype(BF16)
    slope = sigmoid * (1.0 + hidden * (1.0 - sigmoid))
    pre_grad, row_grad, term = expert_stage(scaled, act, slope, up, down)

    def finish():
        terms = swap(term.astype(BF16).reshape(experts, cap))
        gate_grad = call(
            gate_kernel,
            shape((2, tokens), F32),
            jnp.broadcast_to(terms.reshape(1, slots), (8, slots)),
            targets,
            gates,
        )
        return (
            dot(act, scaled, 0, 0).astype(BF16),
            dot(rows, pre_grad, 0, 0).astype(BF16),
            gate_grad,
        )

    return targets, row_grad, finish, early


def spread(heads, width):
    return (iota((heads, width), 1) // (width // heads) == iota((heads, width), 0)).astype(F32)


def ends_kernel(
    inputs_ref, writes_ref, decays_ref, cum_ref, cumt_ref, grown_ref, left_ref, faded_ref, send_ref
):
    decays = decays_ref[...]
    heads, tokens = decays.shape
    parts, padded, width = send_ref.shape
    upto = (iota((tokens, tokens), 0) >= iota((tokens, tokens), 1)).astype(BF16)
    cum = sum(dot(upto, part, 1, 1) for part in pieces_of(decays, 3))
    cum_ref[...] = cum
    cumt = fine_dot(decays, upto, 1, 1, 3)
    for head in range(heads):
        cumt_ref[head] = cumt[head : head + 1, :]
    total = cum[tokens - 1 : tokens, :]
    wide = spread(heads, width).astype(BF16)
    grown_ref[...] = fine_dot(jnp.exp(cum), wide, 1, 0, 1).astype(BF16)
    remaining = fine_dot(jnp.exp(total - cum), wide, 1, 0, 2)
    left_ref[...] = remaining.astype(BF16)
    scaled = (inputs_ref[...].astype(F32) * remaining).astype(BF16)
    faded_ref[...] = scaled
    ends = dot(writes_ref[...], scaled, 0, 0)
    kept = fine_dot(jnp.exp(jnp.broadcast_to(total, (8, heads))), wide, 1, 0, 3)[0:1, :]
    high, low = pieces_of(kept, 2)
    rows = ends.shape[0] // parts
    for part in range(parts):
        send_ref[part, 0:rows, :] = ends[part * rows : (part + 1) * rows, :].astype(BF16)
        send_ref[part, rows : rows + 1, :] = high
        send_ref[part, rows + 1 : rows + 2, :] = low
        send_ref[part, rows + 2 :, :] = jnp.zeros((padded - rows - 2, width), BF16)


def scan_kernel(reverse, ends_ref, kept_ref, out_ref):
    parts, rows, _ = out_ref.shape
    state = jnp.zeros(out_ref.shape[1:], F32)
    for step in range(parts):
        at = parts - 1 - step if reverse else step
        out_ref[at] = state.astype(BF16)
        kept = kept_ref[at, rows : rows + 1, :].astype(F32) + kept_ref[
            at, rows + 1 : rows + 2, :
        ].astype(F32)
        state = state * kept + ends_ref[at, 0:rows, :].astype(F32)


def home_kernel(
    back_ref, targets_ref, resid_ref, out_grad_ref, reads_ref, grown_ref, grad_ref, adjoint_ref
):
    hit0, hit1 = one_hot(targets_ref[...], back_ref.shape[0])
    select = jnp.where(hit0 | hit1, 1.0, 0.0).astype(BF16)
    d_normed = dot(select, back_ref[...], 0, 0)
    resid = resid_ref[...].astype(F32)
    inverse = lax.rsqrt(jnp.mean(resid * resid, axis=1, keepdims=True) + EPSILON)
    normed = resid * inverse
    mean = jnp.mean(d_normed * normed, axis=1, keepdims=True)
    grad = (out_grad_ref[...].astype(F32) + inverse * (d_normed - normed * mean)).astype(BF16)
    grad_ref[...] = grad
    scaled = (grad.astype(F32) * grown_ref[...].astype(F32)).astype(BF16)
    adjoint_ref[...] = dot(reads_ref[...], scaled, 0, 0).astype(BF16)


def inside_kernel(
    base,
    inputs_ref,
    grads_ref,
    writes_ref,
    reads_ref,
    state_ref,
    cum_ref,
    cumt_ref,
    dx_ref,
    dwrite_ref,
    dread_ref,
    dcum_ref,
    dcumt_ref,
    score_ref,
    total_ref,
):
    step = pl.program_id(0)
    steps = pl.num_programs(0)
    tokens, lanes = inputs_ref.shape
    each = cumt_ref.shape[0]
    size = lanes // each

    @pl.when(step == 0)
    def _():
        score_ref[...] = dot(reads_ref[...], writes_ref[...], 1, 1)
        total_ref[...] = jnp.zeros_like(total_ref)
        dread_ref[...] = jnp.zeros_like(dread_ref)
        dcum_ref[...] = jnp.zeros_like(dcum_ref)

    inputs = inputs_ref[...]
    grads = grads_ref[...]
    cum = cum_ref[...]
    scores = score_ref[...]
    causal = iota((tokens, tokens), 0) >= iota((tokens, tokens), 1)
    column = iota(cum.shape, 1)
    lane = iota((tokens, lanes), 1) // size
    dx = jnp.zeros((tokens, lanes), F32)
    sums = jnp.zeros(cum.shape, F32)
    grown = jnp.zeros((tokens, lanes), F32)
    state = state_ref[...]
    read_state = dot(reads_ref[...], state, 1, 0)
    inter = grads.astype(F32) * read_state
    total = jnp.zeros((tokens, tokens), F32)
    for k in range(each):
        head = (base + step) * each + k
        at_t = jnp.sum(jnp.where(column == head, cum, 0.0), axis=1, keepdims=True)
        at_s = cumt_ref[k]
        decay = jnp.exp(jnp.where(causal, at_t - at_s, -1e30))
        mine = lane == k
        grads_k = jnp.where(mine, grads, jnp.zeros_like(grads))
        weights = dot(grads_k, inputs, 1, 1) * decay
        total = total + weights
        dx = dx + dot((decay * scores).astype(BF16), grads_k, 0, 0)
        both = weights * scores
        grow = jnp.exp(at_t)
        row = jnp.sum(both, axis=1, keepdims=True) + grow * jnp.sum(
            jnp.where(mine, inter, 0.0), axis=1, keepdims=True
        )
        sums = sums + jnp.where(column == head, row, 0.0)
        dcumt_ref[k] = jnp.sum(both, axis=0, keepdims=True)
        grown = grown + jnp.where(mine, grow, 0.0)
    total_ref[...] += total
    dcum_ref[...] += sums
    dx_ref[...] = dx.astype(BF16)
    dread_ref[...] += dot((grown * grads.astype(F32)).astype(BF16), state, 1, 1)

    @pl.when(step == steps - 1)
    def _():
        total_b = total_ref[...].astype(BF16)
        dread_ref[...] += dot(total_b, writes_ref[...], 1, 0)
        dwrite_ref[...] = dot(total_b, reads_ref[...], 0, 0)


def inside_stage(inputs, grads, writes, reads, state, cum, cumt, half):
    tokens, width = inputs.shape
    heads = cum.shape[1]
    n = writes.shape[1]
    lanes = max(128, width // heads)
    steps = width // lanes // 2
    each = heads // (width // lanes)
    base = half * steps
    part = pl.BlockSpec((tokens, lanes), lambda i: (0, base + i))
    return call(
        functools.partial(inside_kernel, base),
        (
            far_shape((tokens, width // 2), BF16),
            far_shape((tokens, n), F32),
            far_shape((tokens, n), F32),
            far_shape((tokens, heads), F32),
            far_shape((heads // 2, 1, tokens), F32),
        ),
        *from_hbm(inputs, grads, writes, reads, state, cum, cumt),
        grid=(steps,),
        in_specs=[
            part,
            part,
            one_step((tokens, n)),
            one_step((tokens, n)),
            pl.BlockSpec((n, lanes), lambda i: (0, base + i)),
            one_step((tokens, heads)),
            pl.BlockSpec((each, 1, tokens), lambda i: (base + i, 0, 0)),
        ],
        out_specs=(
            pl.BlockSpec((tokens, lanes), lambda i: (0, i)),
            one_step((tokens, n)),
            one_step((tokens, n)),
            one_step((tokens, heads)),
            pl.BlockSpec((each, 1, tokens), lambda i: (i, 0, 0)),
        ),
        scratch=[pltpu.VMEM((tokens, tokens), F32), pltpu.VMEM((tokens, tokens), F32)],
        cost=pl.CostEstimate(
            flops=4 * tokens * tokens * width,
            bytes_accessed=4 * tokens * width,
            transcendentals=heads * tokens * tokens // 2,
        ),
    )


def last_kernel(
    writes_ref,
    state_ref,
    adjoint_ref,
    cumt_ref,
    left_ref,
    faded_ref,
    dx0_ref,
    dwrite0_ref,
    dread0_ref,
    dcum0_ref,
    dcumt0_ref,
    dx1_ref,
    dwrite1_ref,
    dread1_ref,
    dcum1_ref,
    dcumt1_ref,
    input_grad_ref,
    dwrite_ref,
    dread_ref,
    decay_ref,
):
    tokens, width = left_ref.shape
    heads = cumt_ref.shape[0]
    half = width // 2
    wide = spread(heads, width).astype(BF16)
    adjoint = adjoint_ref[...]
    faded = faded_ref[...]
    values = dot(writes_ref[...], adjoint, 1, 0)
    moved = left_ref[...].astype(F32) * values
    input_grad_ref[:, 0:half] = (dx0_ref[...].astype(F32) + moved[:, 0:half]).astype(BF16)
    input_grad_ref[:, half:] = (dx1_ref[...].astype(F32) + moved[:, half:]).astype(BF16)
    dwrite_ref[...] = dwrite0_ref[...] + dwrite1_ref[...] + dot(faded, adjoint, 1, 1)
    dread_ref[...] = dread0_ref[...] + dread1_ref[...]
    shares = pieces_of(values * faded.astype(F32), 2)
    shares = sum(dot(wide, part, 1, 1) for part in shares)
    kept = jnp.sum(state_ref[...].astype(F32) * adjoint.astype(F32), axis=0, keepdims=True)
    kept = pieces_of(jnp.broadcast_to(kept, (8, width)), 3)
    kept = sum(dot(wide, part, 1, 1) for part in kept)[:, 0:1]
    flow = [ref[h] for ref in (dcumt0_ref, dcumt1_ref) for h in range(heads // 2)]
    total = jnp.concatenate([cumt_ref[h][:, tokens - 1 : tokens] for h in range(heads)], axis=0)
    after = (iota((tokens, tokens), 1) >= iota((tokens, tokens), 0)).astype(BF16)
    rows = -jnp.concatenate(flow, axis=0) - shares
    columns = dcum0_ref[...] + dcum1_ref[...]
    decay_ref[...] = (
        sum(dot(part, after, 0, 1) for part in pieces_of(columns, 3))
        + sum(dot(part, after, 1, 1) for part in pieces_of(rows, 3))
        + jnp.sum(shares, axis=1, keepdims=True)
        + kept * jnp.exp(total)
    )


def shards(
    mixer_input,
    write_proj,
    read_proj,
    log_decay,
    resid,
    out_grad,
    gate_probs,
    expert_ids,
    expert_up,
    expert_down,
):
    tokens, width = resid.shape
    heads = log_decay.shape[1]
    n = write_proj.shape[1]
    shard_count = lax.axis_size("seq")
    experts = lax.axis_size("grp") * shard_count
    cap = 4 * tokens // experts
    everyone = ("grp", "seq")
    up, down = expert_up[0], expert_down[0]
    ids = expert_ids.T
    gates = gate_probs.T

    def swap(x, axes):
        return lax.all_to_all(x, axes, split_axis=0, concat_axis=0, tiled=True)

    state_rows = n // shard_count
    padded = -(-(state_rows + 2) // 8) * 8
    cum, cumt, grown, left, faded, send_ends = streamed(
        ends_kernel,
        (
            far_shape((tokens, heads), F32),
            far_shape((heads, 1, tokens), F32),
            far_shape((tokens, width), BF16),
            far_shape((tokens, width), BF16),
            far_shape((tokens, width), BF16),
            far_shape((shard_count, padded, width), BF16),
        ),
        mixer_input,
        write_proj,
        log_decay.T,
    )
    ends = swap(send_ends, "seq")
    parts = far_shape((shard_count, state_rows, width), BF16)
    starts = call(functools.partial(scan_kernel, False), parts, ends, ends)
    state = swap(starts, "seq").reshape(n, width)

    planes = experts // shard_count
    if planes == 4 and shard_count <= 8 and cap in (16, 32, 64, 128) and tokens <= width:
        targets, row_grad, finish, state = routed_experts(
            resid, out_grad, ids, gates, up, down, cap, shard_count, planes, state
        )
    else:
        targets, row_grad, finish, state = plain_experts(
            resid, out_grad, ids, gates, up, down, cap, experts, lambda x: swap(x, everyone), state
        )
    back = swap(row_grad, everyone)
    down_grad, up_grad, gate_grad = finish()
    back, down_grad, up_grad = lax.optimization_barrier((back, down_grad, up_grad))
    resid_grad, send_adjoint = streamed(
        home_kernel,
        (far_shape((tokens, width), BF16), far_shape((n, width), BF16)),
        back,
        targets,
        resid,
        out_grad,
        read_proj,
        grown,
        near=(0,),
    )
    adjoints = swap(send_adjoint.reshape(shard_count, state_rows, width), "seq")
    inside = (mixer_input, resid_grad, write_proj, read_proj, state, cum, cumt)
    first = inside_stage(*inside, 0)
    later = call(functools.partial(scan_kernel, True), parts, adjoints, ends)
    adjoint = swap(later, "seq").reshape(n, width)
    second = inside_stage(*inside, 1)
    input_grad, write_grad, read_grad, decay_grad = streamed(
        last_kernel,
        (
            far_shape((tokens, width), BF16),
            far_shape((tokens, n), F32),
            far_shape((tokens, n), F32),
            far_shape((heads, tokens), F32),
        ),
        write_proj,
        state,
        adjoint,
        cumt,
        left,
        faded,
        *first,
        *second,
        near=(2,),
    )
    return (
        input_grad,
        write_grad,
        read_grad,
        decay_grad.T,
        resid_grad,
        gate_grad.T.astype(BF16),
        up_grad[None],
        down_grad[None],
    )


def solution(mesh):
    flat = P(("grp", "seq"), None)
    cube = P(("grp", "seq"), None, None)
    return jax.shard_map(
        shards,
        mesh=mesh,
        in_specs=(flat,) * 8 + (cube,) * 2,
        out_specs=(flat,) * 6 + (cube,) * 2,
        check_vma=False,
    )
```

```python
import functools

import jax
import jax.numpy as jnp
from jax import lax
from jax.experimental import pallas as pl
from jax.experimental.pallas import tpu as pltpu
from jax.sharding import PartitionSpec as P


EPSILON = 1e-06
F32 = jnp.float32
BF16 = jnp.bfloat16
VMEM_LIMIT = 20 * 1024 * 1024


def iota(shape, axis):
    return lax.broadcasted_iota(jnp.int32, shape, axis)


def dot(a, b, ca, cb, precision=None):
    return lax.dot_general(
        a, b, (((ca,), (cb,)), ((), ())), precision=precision, preferred_element_type=F32
    )


def call(kernel, outs, *args, grid=None, in_specs=None, out_specs=None, scratch=(), cost=None):
    whole = pl.BlockSpec(memory_space=pltpu.VMEM)
    many = isinstance(outs, (tuple, list))
    kwargs = {}
    if grid is not None:
        kwargs["grid"] = grid
    return pl.pallas_call(
        kernel,
        out_shape=outs,
        in_specs=in_specs if in_specs is not None else [whole] * len(args),
        out_specs=out_specs
        if out_specs is not None
        else (tuple([whole] * len(outs)) if many else whole),
        scratch_shapes=list(scratch),
        compiler_params=pltpu.CompilerParams(vmem_limit_bytes=VMEM_LIMIT),
        cost_estimate=cost,
        **kwargs,
    )(*args)


def pieces_of(x, count):
    parts = []
    for _ in range(count):
        part = x.astype(BF16)
        parts.append(part)
        x = x - part.astype(F32)
    return parts


def fine_dot(a, exact, ca, cb, count):
    return sum(dot(part, exact, ca, cb) for part in pieces_of(a, count))


def shape(dims, dtype):
    return jax.ShapeDtypeStruct(dims, dtype)


def far_shape(dims, dtype):
    return pltpu.HBM(dims, dtype)


def from_hbm(*arrays):
    return [pltpu.with_memory_space_constraint(x, pltpu.HBM) for x in arrays]


def one_step(dims):
    return pl.BlockSpec(dims, lambda i: (0,) * len(dims))


def streamed(kernel, outs, *args, near=(), scalars=None):
    fixed = [x if k in near else from_hbm(x)[0] for k, x in enumerate(args)]
    specs = [one_step(x.shape) for x in args]
    if scalars is not None:
        fixed = [scalars] + fixed
        specs = [pl.BlockSpec(memory_space=pltpu.SMEM)] + specs
    many = isinstance(outs, (tuple, list))
    blocks = tuple(one_step(out.shape) for out in outs) if many else one_step(outs.shape)
    return call(
        kernel,
        outs,
        *fixed,
        grid=(1,),
        in_specs=specs,
        out_specs=blocks,
    )


def one_hot(targets, slots):
    slot = iota((slots, targets.shape[1]), 0)
    first = slot == targets[0:1, :]
    second = slot == targets[1:2, :]
    return first, second


def rows_kernel(experts, cap, resid_ref, ids_ref, rows_ref, targets_ref):
    resid = resid_ref[...].astype(F32)
    inverse = lax.rsqrt(jnp.mean(resid * resid, axis=1, keepdims=True) + EPSILON)
    normed_b = (resid * inverse).astype(BF16)
    ids = ids_ref[...]
    tokens = ids.shape[1]
    number = iota((experts, tokens), 0)
    first = (number == ids[0:1, :]).astype(F32)
    second = (number == ids[1:2, :]).astype(F32)
    earlier = (iota((tokens, tokens), 0) < iota((tokens, tokens), 1)).astype(BF16)
    before = dot((first + second).astype(BF16), earlier, 1, 0)
    rank0 = jnp.sum(before * first, axis=0, keepdims=True).astype(jnp.int32)
    rank1 = jnp.sum(before * second, axis=0, keepdims=True).astype(jnp.int32)
    targets = jnp.concatenate([ids[0:1, :] * cap + rank0, ids[1:2, :] * cap + rank1], axis=0)
    targets_ref[...] = targets
    hit0, hit1 = one_hot(targets, experts * cap)
    select = jnp.where(hit0 | hit1, 1.0, 0.0).astype(BF16)
    rows_ref[...] = dot(select, normed_b, 1, 0).astype(BF16)


def grads_kernel(out_grad_ref, gates_ref, targets_ref, rows_ref):
    slots = rows_ref.shape[0]
    hit0, hit1 = one_hot(targets_ref[...], slots)
    gates = gates_ref[...].astype(BF16).astype(F32)
    select = jnp.where(hit0, gates[0:1, :], 0.0) + jnp.where(hit1, gates[1:2, :], 0.0)
    rows_ref[...] = dot(select.astype(BF16), out_grad_ref[...], 1, 0).astype(BF16)


def expert_kernel(scaled_ref, act_ref, slope_ref, up_ref, down_ref, pre_ref, row_ref, term_ref):
    act_grad = dot(scaled_ref[...], down_ref[...], 1, 1)
    pre = (act_grad * slope_ref[...]).astype(BF16)
    pre_ref[...] = pre
    row_ref[...] = dot(pre, up_ref[...], 1, 1).astype(BF16)
    prod = act_grad * act_ref[...].astype(F32)
    high = prod.astype(BF16)
    low = (prod - high.astype(F32)).astype(BF16)
    ones = jnp.ones((8, prod.shape[1]), BF16)
    term_ref[...] = (dot(ones, high, 1, 1) + dot(ones, low, 1, 1))[None]


def expert_stage(scaled, act, slope, up, down):
    rows, width = scaled.shape
    hidden = act.shape[1]
    tile = min(256, rows)
    steps = rows // tile
    by_rows = lambda w: pl.BlockSpec((tile, w), lambda i: (i, 0))
    whole = pl.BlockSpec(memory_space=pltpu.VMEM)
    pre, row_grad, term = call(
        expert_kernel,
        (shape((rows, hidden), BF16), shape((rows, width), BF16), shape((steps, 8, tile), F32)),
        scaled,
        act,
        slope,
        up,
        down,
        grid=(steps,),
        in_specs=[by_rows(width), by_rows(hidden), by_rows(hidden), whole, whole],
        out_specs=(by_rows(hidden), by_rows(width), pl.BlockSpec((1, 8, tile), lambda i: (i, 0, 0))),
        cost=pl.CostEstimate(
            flops=4 * rows * width * hidden, bytes_accessed=20 * rows * width, transcendentals=0
        ),
    )
    return pre, row_grad, term[:, 0, :].reshape(-1)


def gate_kernel(terms_ref, targets_ref, gates_ref, out_ref):
    slots = terms_ref.shape[1]
    hit0, hit1 = one_hot(targets_ref[...], slots)
    terms = terms_ref[...]
    gates = gates_ref[...].astype(BF16).astype(F32)
    first = dot(terms, jnp.where(hit0, 1.0, 0.0).astype(BF16), 1, 0)
    second = dot(terms, jnp.where(hit1, 1.0, 0.0).astype(BF16), 1, 0)
    out_ref[...] = jnp.concatenate([first[0:1, :], second[0:1, :]], axis=0) / gates


def message_kernel(planes, shard_count, cap, resid_ref, ids_ref, gates_ref, message_ref, targets_ref):
    tokens, width = resid_ref.shape
    experts = planes * shard_count
    resid = resid_ref[...].astype(F32)
    inverse = lax.rsqrt(jnp.mean(resid * resid, axis=1, keepdims=True) + EPSILON)
    message_ref[0:tokens, :] = (resid * inverse).astype(BF16)
    ids = ids_ref[...]
    number = iota((experts, tokens), 0)
    first = (number == ids[0:1, :]).astype(F32)
    second = (number == ids[1:2, :]).astype(F32)
    earlier = (iota((tokens, tokens), 0) < iota((tokens, tokens), 1)).astype(BF16)
    before = dot((first + second).astype(BF16), earlier, 1, 0)
    ranks = jnp.concatenate(
        [
            jnp.sum(before * first, axis=0, keepdims=True),
            jnp.sum(before * second, axis=0, keepdims=True),
        ],
        axis=0,
    )
    targets_ref[...] = ids * cap + ranks.astype(jnp.int32)
    named = ids.astype(F32)
    plane = jnp.floor((named + 0.5) * (1.0 / shard_count))
    shard = named - plane * shard_count
    facts = jnp.concatenate([plane, shard, ranks, gates_ref[...]], axis=0)
    message_ref[tokens:, 0:tokens] = facts.astype(BF16)
    if width > tokens:
        message_ref[tokens:, tokens:] = jnp.zeros((8, width - tokens), BF16)


def named_rows(me_ref, message, slots, cap):
    tokens = message.shape[0] - 8
    facts = message[tokens:, 0:tokens].astype(F32)
    places = (facts[2:4, :].astype(jnp.int32) ^ me_ref[1]) * cap
    places = places + facts[4:6, :].astype(jnp.int32)
    places = jnp.where(facts[0:2, :] == me_ref[0].astype(F32), places, -1)
    hit0, hit1 = one_hot(places, slots)
    select = jnp.where(hit0 | hit1, 1.0, 0.0).astype(BF16)
    rows = dot(select, message[0:tokens, :], 1, 0).astype(BF16)
    keys = jnp.concatenate(
        [places.astype(F32), facts[6:8, :], jnp.zeros((4, tokens), F32)], axis=0
    )
    return keys, rows


def pick_rows_kernel(blocks, cap, me_ref, *refs):
    messages, outs, keys_ref = refs[:blocks], refs[blocks:-1], refs[-1]
    for m, message in enumerate(messages):
        keys_ref[m], rows = named_rows(me_ref, message, len(outs) * cap, cap)
        for x, out in enumerate(outs):
            out[m * cap : (m + 1) * cap, :] = rows[x * cap : (x + 1) * cap, :]


def scaled_rows(keys, grads, slots):
    hit0, hit1 = one_hot(keys[0:2, :].astype(jnp.int32), slots)
    select = jnp.where(hit0, keys[2:3, :], 0.0) + jnp.where(hit1, keys[3:4, :], 0.0)
    return dot(select.astype(BF16), grads, 1, 0).astype(BF16)


def pick_grads_kernel(blocks, cap, keys_ref, *refs):
    grads, outs = refs[:blocks], refs[blocks:]
    for m, grad in enumerate(grads):
        rows = scaled_rows(keys_ref[m], grad[...], len(outs) * cap)
        for x, out in enumerate(outs):
            out[m * cap : (m + 1) * cap, :] = rows[x * cap : (x + 1) * cap, :]


def pick_both_kernel(cap, me_ref, message_ref, grads_ref, *outs):
    slots = len(outs) * cap
    keys, rows = named_rows(me_ref, message_ref, slots, cap)
    scaled = scaled_rows(keys, grads_ref[...], slots)
    for x, out in enumerate(outs):
        out[0:cap, :] = rows[x * cap : (x + 1) * cap, :]
        out[cap:, :] = scaled[x * cap : (x + 1) * cap, :]


def gather_group(me_ref, parts, group_ref):
    cap = parts[0].shape[0]
    for x, part in enumerate(parts):
        at = pl.multiple_of((me_ref[1] ^ x) * cap, cap)
        group_ref[pl.ds(at, cap), :] = part[...]
    return group_ref[...]


def forward_group(rows, up_ref):
    hidden = dot(rows, up_ref[...], 1, 0)
    sigmoid = jax.nn.sigmoid(hidden)
    return (hidden * sigmoid).astype(BF16), sigmoid * (1.0 + hidden * (1.0 - sigmoid))


def hidden_kernel(count, me_ref, *refs):
    parts, (up_ref, rows_ref, act_ref, slope_ref) = refs[:count], refs[count:]
    act_ref[...], slope_ref[...] = forward_group(gather_group(me_ref, parts, rows_ref), up_ref)


def backward_group(scaled, act, slope, up_ref, down_ref, pre_ref, row_ref, term_ref):
    act_grad = dot(scaled, down_ref[...], 1, 1)
    pre = (act_grad * slope).astype(BF16)
    pre_ref[...] = pre
    row_ref[0] = dot(pre, up_ref[...], 1, 1).astype(BF16)
    prod = act_grad * act.astype(F32)
    high = prod.astype(BF16)
    low = (prod - high.astype(F32)).astype(BF16)
    ones = jnp.ones((8, prod.shape[1]), BF16)
    term_ref[0] = dot(ones, high, 1, 1) + dot(ones, low, 1, 1)


def routed_kernel(count, me_ref, *refs):
    parts = refs[:count]
    act_ref, slope_ref, up_ref, down_ref = refs[count : count + 4]
    scaled_ref, pre_ref, row_ref, term_ref = refs[-4:]
    scaled = gather_group(me_ref, parts, scaled_ref)
    backward_group(
        scaled, act_ref[...], slope_ref[...], up_ref, down_ref, pre_ref, row_ref, term_ref
    )


def far_kernel(count, me_ref, *refs):
    cap = refs[0].shape[0] // 2
    up_ref, down_ref = refs[count : count + 2]
    rows_ref, act_ref, scaled_ref, pre_ref, row_ref, term_ref = refs[-6:]
    rows = gather_group(me_ref, [part.at[0:cap, :] for part in refs[:count]], rows_ref)
    act, slope = forward_group(rows, up_ref)
    act_ref[...] = act
    scaled = gather_group(me_ref, [part.at[cap:, :] for part in refs[:count]], scaled_ref)
    backward_group(scaled, act, slope, up_ref, down_ref, pre_ref, row_ref, term_ref)


def mix_kernel(planes, cap, me_ref, *refs):
    blocks, outs = refs[:planes], refs[planes:]
    group = blocks[0].shape[1]
    table = jnp.concatenate(
        [block[0:1, :] for block in blocks] + [jnp.zeros((8 - planes, group), F32)], axis=0
    )
    for x, out in enumerate(outs):
        place, lane = iota((group, 128), 0), iota((group, 128), 1)
        take = (place == (me_ref[1] ^ x) * cap + lane) & (lane < cap)
        out[...] = fine_dot(table, jnp.where(take, 1.0, 0.0).astype(BF16), 1, 0, 2)


def found_kernel(cap, shard_count, me_ref, targets_ref, gates_ref, *refs):
    tables, out_ref = refs[:-1], refs[-1]
    targets = targets_ref[...].astype(F32)
    expert = jnp.floor((targets + 0.5) * (1.0 / cap))
    rank = (targets - expert * cap).astype(jnp.int32)
    plane = jnp.floor((expert + 0.5) * (1.0 / shard_count))
    shard = (expert - plane * shard_count).astype(jnp.int32)
    row = (shard ^ me_ref[1]) * 8 + (plane.astype(jnp.int32) ^ me_ref[0])
    table = jnp.concatenate([ref[...] for ref in tables], axis=0)
    gates = gates_ref[...].astype(BF16).astype(F32)
    tokens = targets.shape[1]
    found = []
    for k in range(2):
        hit = iota((table.shape[0], tokens), 0) == row[k : k + 1, :]
        hit = jnp.where(hit, 1.0, 0.0).astype(BF16)
        values = fine_dot(table, hit, 0, 0, 2)
        mine = iota(values.shape, 0) == rank[k : k + 1, :]
        found.append(jnp.sum(jnp.where(mine, values, 0.0), axis=0, keepdims=True))
    out_ref[...] = jnp.concatenate(found, axis=0) / gates


def grouped(kernel, me, parts, each, extras, extra_specs, outs, out_specs, steps, aliases, flops):
    width = parts[0].shape[1]
    return pl.pallas_call(
        functools.partial(kernel, len(parts)),
        out_shape=outs,
        grid_spec=pltpu.PrefetchScalarGridSpec(
            num_scalar_prefetch=1,
            grid=(steps,),
            in_specs=[pl.BlockSpec((each, width), lambda i, me: (i, 0))] * len(parts) + extra_specs,
            out_specs=out_specs,
        ),
        input_output_aliases=aliases,
        compiler_params=pltpu.CompilerParams(vmem_limit_bytes=VMEM_LIMIT),
        cost_estimate=pl.CostEstimate(
            flops=flops, bytes_accessed=6 * width * width, transcendentals=0
        ),
    )(me, *parts, *extras)


def outer_kernel(*refs):
    pairs, out_ref = zip(refs[0:-1:2], refs[1:-1:2]), refs[-1]
    out_ref[...] = sum(dot(a[...], b[...], 0, 0) for a, b in pairs).astype(BF16)


def outer_stage(*pairs):
    left, right = pairs[0][0].shape[1], pairs[0][1].shape[1]
    tile = min(256, right)
    column = lambda b: pl.BlockSpec((b.shape[0], tile), lambda i: (0, i))
    specs, args = [], []
    for a, b in pairs:
        specs += [one_step(a.shape), column(b)]
        args += from_hbm(a, b)
    rows = sum(a.shape[0] for a, _ in pairs)
    return call(
        outer_kernel,
        far_shape((left, right), BF16),
        *args,
        grid=(right // tile,),
        in_specs=specs,
        out_specs=pl.BlockSpec((left, tile), lambda i: (0, i)),
        cost=pl.CostEstimate(
            flops=2 * rows * left * right, bytes_accessed=6 * left * right, transcendentals=0
        ),
    )


def routed_experts(resid, out_grad, ids, gates, up, down, cap, shard_count, planes, early):
    tokens, width = resid.shape
    hidden = up.shape[1]
    group = shard_count * cap
    plane, shard = lax.axis_index("grp"), lax.axis_index("seq")
    me = jnp.stack([plane, shard]).astype(jnp.int32)
    smem = pl.BlockSpec(memory_space=pltpu.SMEM)
    vmem = pl.BlockSpec(memory_space=pltpu.VMEM)

    def across(x, bit):
        return lax.ppermute(x, "grp", [(i, i ^ bit) for i in range(planes)])

    def spread_out(parts):
        moved = [
            lax.ppermute(part, "seq", [(i, i ^ x) for i in range(shard_count)])
            for x, part in enumerate(parts)
            if x
        ]
        return [parts[0]] + moved

    def pick_rows(messages):
        count = len(messages)
        outs = [far_shape((count * cap, width), BF16)] * shard_count
        *parts, keys = streamed(
            functools.partial(pick_rows_kernel, count, cap),
            tuple(outs + [far_shape((count, 8, tokens), F32)]),
            *messages,
            scalars=me,
        )
        return parts, keys

    def pick_grads(keys, grads):
        count = len(grads)
        outs = [far_shape((count * cap, width), BF16)] * shard_count
        kernel = functools.partial(pick_grads_kernel, count, cap)
        return streamed(kernel, tuple(outs), keys, *grads)

    def pick_both(message, grad, near):
        outs = [far_shape((2 * cap, width), BF16)] * shard_count
        kernel = functools.partial(pick_both_kernel, cap)
        return streamed(kernel, tuple(outs), message, grad, scalars=me, near=near)

    def block(width):
        return pl.BlockSpec((group, width), lambda i, me: (i, 0))

    def hidden_stage(parts, steps):
        parts = from_hbm(*parts)
        rows = steps * group
        return grouped(
            hidden_kernel,
            me,
            parts,
            cap,
            (up,),
            [vmem],
            (far_shape((rows, width), BF16), far_shape((rows, hidden), BF16), shape((rows, hidden), F32)),
            (block(width), block(hidden), block(hidden)),
            steps,
            {},
            2 * rows * width * hidden,
        )

    rows_of = lambda steps, size, dtype: far_shape((steps * group, size), dtype)

    def backs(steps):
        return (far_shape((planes, group, width), BF16), far_shape((steps, 8, group), F32))

    def back_blocks(base):
        return (
            pl.BlockSpec((1, group, width), lambda i, me: (me[0] ^ (base + i), 0, 0)),
            pl.BlockSpec((1, 8, group), lambda i, me: (i, 0, 0)),
        )

    def routed_stage(parts, act, slope, steps, base, filled):
        return grouped(
            routed_kernel,
            me,
            parts,
            cap,
            (act, slope, up, down, filled),
            [block(hidden), block(hidden), vmem, vmem, pl.BlockSpec(memory_space=pl.ANY)],
            (rows_of(steps, width, BF16), rows_of(steps, hidden, BF16)) + backs(steps),
            (block(width), block(hidden)) + back_blocks(base),
            steps,
            {1 + len(parts) + 4: 2},
            4 * steps * group * width * hidden,
        )

    def whole_stage(parts, base, filled):
        extra = () if filled is None else (filled,)
        return grouped(
            far_kernel,
            me,
            parts,
            2 * cap,
            (up, down) + extra,
            [vmem, vmem] + [pl.BlockSpec(memory_space=pl.ANY)] * len(extra),
            (
                rows_of(1, width, BF16),
                rows_of(1, hidden, BF16),
                rows_of(1, width, BF16),
                rows_of(1, hidden, BF16),
            )
            + backs(1),
            (block(width), block(hidden), block(width), block(hidden)) + back_blocks(base),
            1,
            {1 + len(parts) + 2: 4} if extra else {},
            6 * group * width * hidden,
        )

    message, targets = streamed(
        functools.partial(message_kernel, planes, shard_count, cap),
        (far_shape((tokens + 8, width), BF16), far_shape((2, tokens), jnp.int32)),
        resid,
        ids,
        gates,
    )
    message2 = across(message, 2)
    message1 = across(message, 1)
    grad2 = across(out_grad, 2)
    grad1 = across(out_grad, 1)
    message3 = across(message2, 1)
    own = pick_both(message, out_grad, ())
    own = spread_out(own)
    own = from_hbm(*own)
    rows_0, act_0, scaled_0, pre_0, row_grad, own_terms = whole_stage(own, 0, None)
    near_rows, near_keys = pick_rows([message1, message2])
    near_rows = spread_out(near_rows)
    arrived, early = lax.optimization_barrier((near_rows[1], early))
    near_rows[1] = arrived
    grad3 = across(grad2, 1)
    near_grads = pick_grads(near_keys, [grad1, grad2])
    near_grads = spread_out(near_grads)
    rows_1, act_1, slope_1 = hidden_stage(near_rows, 2)
    far = pick_both(message3, grad3, (0, 1))
    far = spread_out(far)
    scaled_1, pre_1, row_grad, near_terms = routed_stage(near_grads, act_1, slope_1, 2, 1, row_grad)
    rows_2, act_2, scaled_2, pre_2, row_grad, far_terms = whole_stage(far, 3, row_grad)

    def finish():
        blocks = [own_terms[0]]
        blocks += [across(near_terms[bit - 1], bit) for bit in (1, 2)]
        blocks += [across(far_terms[0], 3)]
        down_grad = outer_stage((act_0, scaled_0), (act_1, scaled_1), (act_2, scaled_2))
        up_grad = outer_stage((rows_0, pre_0), (rows_1, pre_1), (rows_2, pre_2))
        blocks, down_grad, up_grad = lax.optimization_barrier((blocks, down_grad, up_grad))
        mixed = call(
            functools.partial(mix_kernel, planes, cap),
            tuple([shape((8, 128), F32)] * shard_count),
            me,
            *blocks,
            in_specs=[smem] + [vmem] * planes,
        )
        mixed = spread_out(mixed)
        gate_grad = call(
            functools.partial(found_kernel, cap, shard_count),
            far_shape((2, tokens), F32),
            me,
            targets,
            gates,
            *mixed,
            in_specs=[smem] + [vmem] * (2 + shard_count),
            out_specs=vmem,
        )
        return down_grad, up_grad, gate_grad

    return targets, row_grad.reshape(-1, width), finish, early


def plain_experts(resid, out_grad, ids, gates, up, down, cap, experts, swap, early):
    tokens, width = resid.shape
    slots = experts * cap
    send_rows, targets = call(
        functools.partial(rows_kernel, experts, cap),
        (shape((slots, width), BF16), shape((2, tokens), jnp.int32)),
        resid,
        ids,
    )
    rows = swap(send_rows)
    send_scaled = call(grads_kernel, shape((slots, width), BF16), out_grad, gates, targets)
    scaled = swap(send_scaled)
    hidden = jnp.dot(rows, up, preferred_element_type=F32)
    sigmoid = jax.nn.sigmoid(hidden)
    act = (hidden * sigmoid).astype(BF16)
    slope = sigmoid * (1.0 + hidden * (1.0 - sigmoid))
    pre_grad, row_grad, term = expert_stage(scaled, act, slope, up, down)

    def finish():
        terms = swap(term.astype(BF16).reshape(experts, cap))
        gate_grad = call(
            gate_kernel,
            shape((2, tokens), F32),
            jnp.broadcast_to(terms.reshape(1, slots), (8, slots)),
            targets,
            gates,
        )
        return (
            dot(act, scaled, 0, 0).astype(BF16),
            dot(rows, pre_grad, 0, 0).astype(BF16),
            gate_grad,
        )

    return targets, row_grad, finish, early


def spread(heads, width):
    return (iota((heads, width), 1) // (width // heads) == iota((heads, width), 0)).astype(F32)


def ends_kernel(
    inputs_ref, writes_ref, decays_ref, cum_ref, cumt_ref, grown_ref, left_ref, faded_ref, send_ref
):
    decays = decays_ref[...]
    heads, tokens = decays.shape
    parts, padded, width = send_ref.shape
    upto = (iota((tokens, tokens), 0) >= iota((tokens, tokens), 1)).astype(BF16)
    cum = sum(dot(upto, part, 1, 1) for part in pieces_of(decays, 3))
    cum_ref[...] = cum
    cumt = fine_dot(decays, upto, 1, 1, 3)
    for head in range(heads):
        cumt_ref[head] = cumt[head : head + 1, :]
    total = cum[tokens - 1 : tokens, :]
    wide = spread(heads, width).astype(BF16)
    grown_ref[...] = fine_dot(jnp.exp(cum), wide, 1, 0, 1).astype(BF16)
    remaining = fine_dot(jnp.exp(total - cum), wide, 1, 0, 2)
    left_ref[...] = remaining.astype(BF16)
    scaled = (inputs_ref[...].astype(F32) * remaining).astype(BF16)
    faded_ref[...] = scaled
    ends = dot(writes_ref[...], scaled, 0, 0)
    kept = fine_dot(jnp.exp(jnp.broadcast_to(total, (8, heads))), wide, 1, 0, 3)[0:1, :]
    high, low = pieces_of(kept, 2)
    rows = ends.shape[0] // parts
    for part in range(parts):
        send_ref[part, 0:rows, :] = ends[part * rows : (part + 1) * rows, :].astype(BF16)
        send_ref[part, rows : rows + 1, :] = high
        send_ref[part, rows + 1 : rows + 2, :] = low
        send_ref[part, rows + 2 :, :] = jnp.zeros((padded - rows - 2, width), BF16)


def scan_kernel(reverse, ends_ref, kept_ref, out_ref):
    parts, rows, _ = out_ref.shape
    state = jnp.zeros(out_ref.shape[1:], F32)
    for step in range(parts):
        at = parts - 1 - step if reverse else step
        out_ref[at] = state.astype(BF16)
        kept = kept_ref[at, rows : rows + 1, :].astype(F32) + kept_ref[
            at, rows + 1 : rows + 2, :
        ].astype(F32)
        state = state * kept + ends_ref[at, 0:rows, :].astype(F32)


def home_kernel(
    back_ref, targets_ref, resid_ref, out_grad_ref, reads_ref, grown_ref, grad_ref, adjoint_ref
):
    hit0, hit1 = one_hot(targets_ref[...], back_ref.shape[0])
    select = jnp.where(hit0 | hit1, 1.0, 0.0).astype(BF16)
    d_normed = dot(select, back_ref[...], 0, 0)
    resid = resid_ref[...].astype(F32)
    inverse = lax.rsqrt(jnp.mean(resid * resid, axis=1, keepdims=True) + EPSILON)
    normed = resid * inverse
    mean = jnp.mean(d_normed * normed, axis=1, keepdims=True)
    grad = (out_grad_ref[...].astype(F32) + inverse * (d_normed - normed * mean)).astype(BF16)
    grad_ref[...] = grad
    scaled = (grad.astype(F32) * grown_ref[...].astype(F32)).astype(BF16)
    adjoint_ref[...] = dot(reads_ref[...], scaled, 0, 0).astype(BF16)


def inside_kernel(
    base,
    inputs_ref,
    grads_ref,
    writes_ref,
    reads_ref,
    state_ref,
    cum_ref,
    cumt_ref,
    dx_ref,
    dwrite_ref,
    dread_ref,
    dcum_ref,
    dcumt_ref,
    score_ref,
    total_ref,
):
    step = pl.program_id(0)
    steps = pl.num_programs(0)
    tokens, lanes = inputs_ref.shape
    each = cumt_ref.shape[0]
    size = lanes // each

    @pl.when(step == 0)
    def _():
        score_ref[...] = dot(reads_ref[...], writes_ref[...], 1, 1)
        total_ref[...] = jnp.zeros_like(total_ref)
        dread_ref[...] = jnp.zeros_like(dread_ref)
        dcum_ref[...] = jnp.zeros_like(dcum_ref)

    inputs = inputs_ref[...]
    grads = grads_ref[...]
    cum = cum_ref[...]
    scores = score_ref[...]
    causal = iota((tokens, tokens), 0) >= iota((tokens, tokens), 1)
    column = iota(cum.shape, 1)
    lane = iota((tokens, lanes), 1) // size
    dx = jnp.zeros((tokens, lanes), F32)
    sums = jnp.zeros(cum.shape, F32)
    grown = jnp.zeros((tokens, lanes), F32)
    state = state_ref[...]
    read_state = dot(reads_ref[...], state, 1, 0)
    inter = grads.astype(F32) * read_state
    total = jnp.zeros((tokens, tokens), F32)
    for k in range(each):
        head = (base + step) * each + k
        at_t = jnp.sum(jnp.where(column == head, cum, 0.0), axis=1, keepdims=True)
        at_s = cumt_ref[k]
        decay = jnp.exp(jnp.where(causal, at_t - at_s, -1e30))
        mine = lane == k
        grads_k = jnp.where(mine, grads, jnp.zeros_like(grads))
        weights = dot(grads_k, inputs, 1, 1) * decay
        total = total + weights
        dx = dx + dot((decay * scores).astype(BF16), grads_k, 0, 0)
        both = weights * scores
        grow = jnp.exp(at_t)
        row = jnp.sum(both, axis=1, keepdims=True) + grow * jnp.sum(
            jnp.where(mine, inter, 0.0), axis=1, keepdims=True
        )
        sums = sums + jnp.where(column == head, row, 0.0)
        dcumt_ref[k] = jnp.sum(both, axis=0, keepdims=True)
        grown = grown + jnp.where(mine, grow, 0.0)
    total_ref[...] += total
    dcum_ref[...] += sums
    dx_ref[...] = dx.astype(BF16)
    dread_ref[...] += dot((grown * grads.astype(F32)).astype(BF16), state, 1, 1)

    @pl.when(step == steps - 1)
    def _():
        total_b = total_ref[...].astype(BF16)
        dread_ref[...] += dot(total_b, writes_ref[...], 1, 0)
        dwrite_ref[...] = dot(total_b, reads_ref[...], 0, 0)


def inside_stage(inputs, grads, writes, reads, state, cum, cumt, half):
    tokens, width = inputs.shape
    heads = cum.shape[1]
    n = writes.shape[1]
    lanes = max(128, width // heads)
    steps = width // lanes // 2
    each = heads // (width // lanes)
    base = half * steps
    part = pl.BlockSpec((tokens, lanes), lambda i: (0, base + i))
    return call(
        functools.partial(inside_kernel, base),
        (
            far_shape((tokens, width // 2), BF16),
            far_shape((tokens, n), F32),
            far_shape((tokens, n), F32),
            far_shape((tokens, heads), F32),
            far_shape((heads // 2, 1, tokens), F32),
        ),
        *from_hbm(inputs, grads, writes, reads, state, cum, cumt),
        grid=(steps,),
        in_specs=[
            part,
            part,
            one_step((tokens, n)),
            one_step((tokens, n)),
            pl.BlockSpec((n, lanes), lambda i: (0, base + i)),
            one_step((tokens, heads)),
            pl.BlockSpec((each, 1, tokens), lambda i: (base + i, 0, 0)),
        ],
        out_specs=(
            pl.BlockSpec((tokens, lanes), lambda i: (0, i)),
            one_step((tokens, n)),
            one_step((tokens, n)),
            one_step((tokens, heads)),
            pl.BlockSpec((each, 1, tokens), lambda i: (i, 0, 0)),
        ),
        scratch=[pltpu.VMEM((tokens, tokens), F32), pltpu.VMEM((tokens, tokens), F32)],
        cost=pl.CostEstimate(
            flops=4 * tokens * tokens * width,
            bytes_accessed=4 * tokens * width,
            transcendentals=heads * tokens * tokens // 2,
        ),
    )


def last_kernel(
    writes_ref,
    state_ref,
    adjoint_ref,
    cumt_ref,
    left_ref,
    faded_ref,
    dx0_ref,
    dwrite0_ref,
    dread0_ref,
    dcum0_ref,
    dcumt0_ref,
    dx1_ref,
    dwrite1_ref,
    dread1_ref,
    dcum1_ref,
    dcumt1_ref,
    input_grad_ref,
    dwrite_ref,
    dread_ref,
    decay_ref,
):
    tokens, width = left_ref.shape
    heads = cumt_ref.shape[0]
    half = width // 2
    wide = spread(heads, width).astype(BF16)
    adjoint = adjoint_ref[...]
    faded = faded_ref[...]
    values = dot(writes_ref[...], adjoint, 1, 0)
    moved = left_ref[...].astype(F32) * values
    input_grad_ref[:, 0:half] = (dx0_ref[...].astype(F32) + moved[:, 0:half]).astype(BF16)
    input_grad_ref[:, half:] = (dx1_ref[...].astype(F32) + moved[:, half:]).astype(BF16)
    dwrite_ref[...] = dwrite0_ref[...] + dwrite1_ref[...] + dot(faded, adjoint, 1, 1)
    dread_ref[...] = dread0_ref[...] + dread1_ref[...]
    shares = pieces_of(values * faded.astype(F32), 2)
    shares = sum(dot(wide, part, 1, 1) for part in shares)
    kept = jnp.sum(state_ref[...].astype(F32) * adjoint.astype(F32), axis=0, keepdims=True)
    kept = pieces_of(jnp.broadcast_to(kept, (8, width)), 3)
    kept = sum(dot(wide, part, 1, 1) for part in kept)[:, 0:1]
    flow = [ref[h] for ref in (dcumt0_ref, dcumt1_ref) for h in range(heads // 2)]
    total = jnp.concatenate([cumt_ref[h][:, tokens - 1 : tokens] for h in range(heads)], axis=0)
    after = (iota((tokens, tokens), 1) >= iota((tokens, tokens), 0)).astype(BF16)
    rows = -jnp.concatenate(flow, axis=0) - shares
    columns = dcum0_ref[...] + dcum1_ref[...]
    decay_ref[...] = (
        sum(dot(part, after, 0, 1) for part in pieces_of(columns, 3))
        + sum(dot(part, after, 1, 1) for part in pieces_of(rows, 3))
        + jnp.sum(shares, axis=1, keepdims=True)
        + kept * jnp.exp(total)
    )


def shards(
    mixer_input,
    write_proj,
    read_proj,
    log_decay,
    resid,
    out_grad,
    gate_probs,
    expert_ids,
    expert_up,
    expert_down,
):
    tokens, width = resid.shape
    heads = log_decay.shape[1]
    n = write_proj.shape[1]
    shard_count = lax.axis_size("seq")
    experts = lax.axis_size("grp") * shard_count
    cap = 4 * tokens // experts
    everyone = ("grp", "seq")
    up, down = expert_up[0], expert_down[0]
    ids = expert_ids.T
    gates = gate_probs.T

    def swap(x, axes):
        return lax.all_to_all(x, axes, split_axis=0, concat_axis=0, tiled=True)

    state_rows = n // shard_count
    padded = -(-(state_rows + 2) // 8) * 8
    cum, cumt, grown, left, faded, send_ends = streamed(
        ends_kernel,
        (
            far_shape((tokens, heads), F32),
            far_shape((heads, 1, tokens), F32),
            far_shape((tokens, width), BF16),
            far_shape((tokens, width), BF16),
            far_shape((tokens, width), BF16),
            far_shape((shard_count, padded, width), BF16),
        ),
        mixer_input,
        write_proj,
        log_decay.T,
    )
    ends = swap(send_ends, "seq")
    parts = far_shape((shard_count, state_rows, width), BF16)
    starts = call(functools.partial(scan_kernel, False), parts, ends, ends)
    state = swap(starts, "seq").reshape(n, width)

    planes = experts // shard_count
    if planes == 4 and shard_count <= 8 and cap in (16, 32, 64, 128) and tokens <= width:
        targets, row_grad, finish, state = routed_experts(
            resid, out_grad, ids, gates, up, down, cap, shard_count, planes, state
        )
    else:
        targets, row_grad, finish, state = plain_experts(
            resid, out_grad, ids, gates, up, down, cap, experts, lambda x: swap(x, everyone), state
        )
    back = swap(row_grad, everyone)
    down_grad, up_grad, gate_grad = finish()
    back, down_grad, up_grad = lax.optimization_barrier((back, down_grad, up_grad))
    resid_grad, send_adjoint = streamed(
        home_kernel,
        (far_shape((tokens, width), BF16), far_shape((n, width), BF16)),
        back,
        targets,
        resid,
        out_grad,
        read_proj,
        grown,
        near=(0,),
    )
    adjoints = swap(send_adjoint.reshape(shard_count, state_rows, width), "seq")
    inside = (mixer_input, resid_grad, write_proj, read_proj, state, cum, cumt)
    first = inside_stage(*inside, 0)
    later = call(functools.partial(scan_kernel, True), parts, adjoints, ends)
    adjoint = swap(later, "seq").reshape(n, width)
    second = inside_stage(*inside, 1)
    input_grad, write_grad, read_grad, decay_grad = streamed(
        last_kernel,
        (
            far_shape((tokens, width), BF16),
            far_shape((tokens, n), F32),
            far_shape((tokens, n), F32),
            far_shape((heads, tokens), F32),
        ),
        write_proj,
        state,
        adjoint,
        cumt,
        left,
        faded,
        *first,
        *second,
        near=(2,),
    )
    return (
        input_grad,
        write_grad,
        read_grad,
        decay_grad.T,
        resid_grad,
        gate_grad.T.astype(BF16),
        up_grad[None],
        down_grad[None],
    )


def solution(mesh):
    flat = P(("grp", "seq"), None)
    cube = P(("grp", "seq"), None, None)
    return jax.shard_map(
        shards,
        mesh=mesh,
        in_specs=(flat,) * 8 + (cube,) * 2,
        out_specs=(flat,) * 6 + (cube,) * 2,
        check_vma=False,
    )
```

```python
import functools

import jax
import jax.numpy as jnp
from jax import lax
from jax.experimental import pallas as pl
from jax.experimental.pallas import tpu as pltpu
from jax.sharding import PartitionSpec as P


EPSILON = 1e-06
F32 = jnp.float32
BF16 = jnp.bfloat16
VMEM_LIMIT = 20 * 1024 * 1024


def iota(shape, axis):
    return lax.broadcasted_iota(jnp.int32, shape, axis)


def dot(a, b, ca, cb, precision=None):
    return lax.dot_general(
        a, b, (((ca,), (cb,)), ((), ())), precision=precision, preferred_element_type=F32
    )


def call(kernel, outs, *args, grid=None, in_specs=None, out_specs=None, scratch=(), cost=None):
    whole = pl.BlockSpec(memory_space=pltpu.VMEM)
    many = isinstance(outs, (tuple, list))
    kwargs = {}
    if grid is not None:
        kwargs["grid"] = grid
    return pl.pallas_call(
        kernel,
        out_shape=outs,
        in_specs=in_specs if in_specs is not None else [whole] * len(args),
        out_specs=out_specs
        if out_specs is not None
        else (tuple([whole] * len(outs)) if many else whole),
        scratch_shapes=list(scratch),
        compiler_params=pltpu.CompilerParams(vmem_limit_bytes=VMEM_LIMIT),
        cost_estimate=cost,
        **kwargs,
    )(*args)


def pieces_of(x, count):
    parts = []
    for _ in range(count):
        part = x.astype(BF16)
        parts.append(part)
        x = x - part.astype(F32)
    return parts


def fine_dot(a, exact, ca, cb, count):
    return sum(dot(part, exact, ca, cb) for part in pieces_of(a, count))


def shape(dims, dtype):
    return jax.ShapeDtypeStruct(dims, dtype)


def far_shape(dims, dtype):
    return pltpu.HBM(dims, dtype)


def from_hbm(*arrays):
    return [pltpu.with_memory_space_constraint(x, pltpu.HBM) for x in arrays]


def one_step(dims):
    return pl.BlockSpec(dims, lambda i: (0,) * len(dims))


def streamed(kernel, outs, *args, near=(), scalars=None):
    fixed = [x if k in near else from_hbm(x)[0] for k, x in enumerate(args)]
    specs = [one_step(x.shape) for x in args]
    if scalars is not None:
        fixed = [scalars] + fixed
        specs = [pl.BlockSpec(memory_space=pltpu.SMEM)] + specs
    many = isinstance(outs, (tuple, list))
    blocks = tuple(one_step(out.shape) for out in outs) if many else one_step(outs.shape)
    return call(
        kernel,
        outs,
        *fixed,
        grid=(1,),
        in_specs=specs,
        out_specs=blocks,
    )


def one_hot(targets, slots):
    slot = iota((slots, targets.shape[1]), 0)
    first = slot == targets[0:1, :]
    second = slot == targets[1:2, :]
    return first, second


def rows_kernel(experts, cap, resid_ref, ids_ref, rows_ref, targets_ref):
    resid = resid_ref[...].astype(F32)
    inverse = lax.rsqrt(jnp.mean(resid * resid, axis=1, keepdims=True) + EPSILON)
    normed_b = (resid * inverse).astype(BF16)
    ids = ids_ref[...]
    tokens = ids.shape[1]
    number = iota((experts, tokens), 0)
    first = (number == ids[0:1, :]).astype(F32)
    second = (number == ids[1:2, :]).astype(F32)
    earlier = (iota((tokens, tokens), 0) < iota((tokens, tokens), 1)).astype(BF16)
    before = dot((first + second).astype(BF16), earlier, 1, 0)
    rank0 = jnp.sum(before * first, axis=0, keepdims=True).astype(jnp.int32)
    rank1 = jnp.sum(before * second, axis=0, keepdims=True).astype(jnp.int32)
    targets = jnp.concatenate([ids[0:1, :] * cap + rank0, ids[1:2, :] * cap + rank1], axis=0)
    targets_ref[...] = targets
    hit0, hit1 = one_hot(targets, experts * cap)
    select = jnp.where(hit0 | hit1, 1.0, 0.0).astype(BF16)
    rows_ref[...] = dot(select, normed_b, 1, 0).astype(BF16)


def grads_kernel(out_grad_ref, gates_ref, targets_ref, rows_ref):
    slots = rows_ref.shape[0]
    hit0, hit1 = one_hot(targets_ref[...], slots)
    gates = gates_ref[...].astype(BF16).astype(F32)
    select = jnp.where(hit0, gates[0:1, :], 0.0) + jnp.where(hit1, gates[1:2, :], 0.0)
    rows_ref[...] = dot(select.astype(BF16), out_grad_ref[...], 1, 0).astype(BF16)


def expert_kernel(scaled_ref, act_ref, slope_ref, up_ref, down_ref, pre_ref, row_ref, term_ref):
    act_grad = dot(scaled_ref[...], down_ref[...], 1, 1)
    pre = (act_grad * slope_ref[...]).astype(BF16)
    pre_ref[...] = pre
    row_ref[...] = dot(pre, up_ref[...], 1, 1).astype(BF16)
    prod = act_grad * act_ref[...].astype(F32)
    high = prod.astype(BF16)
    low = (prod - high.astype(F32)).astype(BF16)
    ones = jnp.ones((8, prod.shape[1]), BF16)
    term_ref[...] = (dot(ones, high, 1, 1) + dot(ones, low, 1, 1))[None]


def expert_stage(scaled, act, slope, up, down):
    rows, width = scaled.shape
    hidden = act.shape[1]
    tile = min(256, rows)
    steps = rows // tile
    by_rows = lambda w: pl.BlockSpec((tile, w), lambda i: (i, 0))
    whole = pl.BlockSpec(memory_space=pltpu.VMEM)
    pre, row_grad, term = call(
        expert_kernel,
        (shape((rows, hidden), BF16), shape((rows, width), BF16), shape((steps, 8, tile), F32)),
        scaled,
        act,
        slope,
        up,
        down,
        grid=(steps,),
        in_specs=[by_rows(width), by_rows(hidden), by_rows(hidden), whole, whole],
        out_specs=(by_rows(hidden), by_rows(width), pl.BlockSpec((1, 8, tile), lambda i: (i, 0, 0))),
        cost=pl.CostEstimate(
            flops=4 * rows * width * hidden, bytes_accessed=20 * rows * width, transcendentals=0
        ),
    )
    return pre, row_grad, term[:, 0, :].reshape(-1)


def gate_kernel(terms_ref, targets_ref, gates_ref, out_ref):
    slots = terms_ref.shape[1]
    hit0, hit1 = one_hot(targets_ref[...], slots)
    terms = terms_ref[...]
    gates = gates_ref[...].astype(BF16).astype(F32)
    first = dot(terms, jnp.where(hit0, 1.0, 0.0).astype(BF16), 1, 0)
    second = dot(terms, jnp.where(hit1, 1.0, 0.0).astype(BF16), 1, 0)
    out_ref[...] = jnp.concatenate([first[0:1, :], second[0:1, :]], axis=0) / gates


def message_kernel(planes, shard_count, cap, resid_ref, ids_ref, gates_ref, message_ref, targets_ref):
    tokens, width = resid_ref.shape
    experts = planes * shard_count
    resid = resid_ref[...].astype(F32)
    inverse = lax.rsqrt(jnp.mean(resid * resid, axis=1, keepdims=True) + EPSILON)
    message_ref[0:tokens, :] = (resid * inverse).astype(BF16)
    ids = ids_ref[...]
    number = iota((experts, tokens), 0)
    first = (number == ids[0:1, :]).astype(F32)
    second = (number == ids[1:2, :]).astype(F32)
    earlier = (iota((tokens, tokens), 0) < iota((tokens, tokens), 1)).astype(BF16)
    before = dot((first + second).astype(BF16), earlier, 1, 0)
    ranks = jnp.concatenate(
        [
            jnp.sum(before * first, axis=0, keepdims=True),
            jnp.sum(before * second, axis=0, keepdims=True),
        ],
        axis=0,
    )
    targets_ref[...] = ids * cap + ranks.astype(jnp.int32)
    named = ids.astype(F32)
    plane = jnp.floor((named + 0.5) * (1.0 / shard_count))
    shard = named - plane * shard_count
    facts = jnp.concatenate([plane, shard, ranks, gates_ref[...]], axis=0)
    message_ref[tokens:, 0:tokens] = facts.astype(BF16)
    if width > tokens:
        message_ref[tokens:, tokens:] = jnp.zeros((8, width - tokens), BF16)


def named_rows(me_ref, message, slots, cap):
    tokens = message.shape[0] - 8
    facts = message[tokens:, 0:tokens].astype(F32)
    places = (facts[2:4, :].astype(jnp.int32) ^ me_ref[1]) * cap
    places = places + facts[4:6, :].astype(jnp.int32)
    places = jnp.where(facts[0:2, :] == me_ref[0].astype(F32), places, -1)
    hit0, hit1 = one_hot(places, slots)
    select = jnp.where(hit0 | hit1, 1.0, 0.0).astype(BF16)
    rows = dot(select, message[0:tokens, :], 1, 0).astype(BF16)
    keys = jnp.concatenate(
        [places.astype(F32), facts[6:8, :], jnp.zeros((4, tokens), F32)], axis=0
    )
    return keys, rows


def pick_rows_kernel(blocks, cap, me_ref, *refs):
    messages, outs, keys_ref = refs[:blocks], refs[blocks:-1], refs[-1]
    for m, message in enumerate(messages):
        keys_ref[m], rows = named_rows(me_ref, message, len(outs) * cap, cap)
        for x, out in enumerate(outs):
            out[m * cap : (m + 1) * cap, :] = rows[x * cap : (x + 1) * cap, :]


def scaled_rows(keys, grads, slots):
    hit0, hit1 = one_hot(keys[0:2, :].astype(jnp.int32), slots)
    select = jnp.where(hit0, keys[2:3, :], 0.0) + jnp.where(hit1, keys[3:4, :], 0.0)
    return dot(select.astype(BF16), grads, 1, 0).astype(BF16)


def pick_grads_kernel(blocks, cap, keys_ref, *refs):
    grads, outs = refs[:blocks], refs[blocks:]
    for m, grad in enumerate(grads):
        rows = scaled_rows(keys_ref[m], grad[...], len(outs) * cap)
        for x, out in enumerate(outs):
            out[m * cap : (m + 1) * cap, :] = rows[x * cap : (x + 1) * cap, :]


def pick_both_kernel(cap, me_ref, message_ref, grads_ref, *outs):
    slots = len(outs) * cap
    keys, rows = named_rows(me_ref, message_ref, slots, cap)
    scaled = scaled_rows(keys, grads_ref[...], slots)
    for x, out in enumerate(outs):
        out[0:cap, :] = rows[x * cap : (x + 1) * cap, :]
        out[cap:, :] = scaled[x * cap : (x + 1) * cap, :]


def gather_group(me_ref, parts, group_ref):
    cap = parts[0].shape[0]
    for x, part in enumerate(parts):
        at = pl.multiple_of((me_ref[1] ^ x) * cap, cap)
        group_ref[pl.ds(at, cap), :] = part[...]
    return group_ref[...]


def forward_group(rows, up_ref):
    hidden = dot(rows, up_ref[...], 1, 0)
    sigmoid = jax.nn.sigmoid(hidden)
    return (hidden * sigmoid).astype(BF16), sigmoid * (1.0 + hidden * (1.0 - sigmoid))


def hidden_kernel(count, me_ref, *refs):
    parts, (up_ref, rows_ref, act_ref, slope_ref) = refs[:count], refs[count:]
    act_ref[...], slope_ref[...] = forward_group(gather_group(me_ref, parts, rows_ref), up_ref)


def backward_group(scaled, act, slope, up_ref, down_ref, pre_ref, row_ref, term_ref):
    act_grad = dot(scaled, down_ref[...], 1, 1)
    pre = (act_grad * slope).astype(BF16)
    pre_ref[...] = pre
    row_ref[0] = dot(pre, up_ref[...], 1, 1).astype(BF16)
    prod = act_grad * act.astype(F32)
    term_ref[0] = dot(jnp.ones((8, prod.shape[1]), BF16), prod.astype(BF16), 1, 1)


def routed_kernel(count, me_ref, *refs):
    parts = refs[:count]
    act_ref, slope_ref, up_ref, down_ref = refs[count : count + 4]
    scaled_ref, pre_ref, row_ref, term_ref = refs[-4:]
    scaled = gather_group(me_ref, parts, scaled_ref)
    backward_group(
        scaled, act_ref[...], slope_ref[...], up_ref, down_ref, pre_ref, row_ref, term_ref
    )


def far_kernel(count, me_ref, *refs):
    cap = refs[0].shape[0] // 2
    up_ref, down_ref = refs[count : count + 2]
    rows_ref, act_ref, scaled_ref, pre_ref, row_ref, term_ref = refs[-6:]
    rows = gather_group(me_ref, [part.at[0:cap, :] for part in refs[:count]], rows_ref)
    act, slope = forward_group(rows, up_ref)
    act_ref[...] = act
    scaled = gather_group(me_ref, [part.at[cap:, :] for part in refs[:count]], scaled_ref)
    backward_group(scaled, act, slope, up_ref, down_ref, pre_ref, row_ref, term_ref)


def mix_kernel(planes, cap, me_ref, *refs):
    blocks, outs = refs[:planes], refs[planes:]
    group = blocks[0].shape[1]
    table = jnp.concatenate(
        [block[0:1, :] for block in blocks] + [jnp.zeros((8 - planes, group), F32)], axis=0
    )
    for x, out in enumerate(outs):
        place, lane = iota((group, 128), 0), iota((group, 128), 1)
        take = (place == (me_ref[1] ^ x) * cap + lane) & (lane < cap)
        out[...] = fine_dot(table, jnp.where(take, 1.0, 0.0).astype(BF16), 1, 0, 2)


def found_kernel(cap, shard_count, me_ref, targets_ref, gates_ref, *refs):
    tables, out_ref = refs[:-1], refs[-1]
    targets = targets_ref[...].astype(F32)
    expert = jnp.floor((targets + 0.5) * (1.0 / cap))
    rank = (targets - expert * cap).astype(jnp.int32)
    plane = jnp.floor((expert + 0.5) * (1.0 / shard_count))
    shard = (expert - plane * shard_count).astype(jnp.int32)
    row = (shard ^ me_ref[1]) * 8 + (plane.astype(jnp.int32) ^ me_ref[0])
    table = jnp.concatenate([ref[...] for ref in tables], axis=0)
    gates = gates_ref[...].astype(BF16).astype(F32)
    tokens = targets.shape[1]
    found = []
    for k in range(2):
        hit = iota((table.shape[0], tokens), 0) == row[k : k + 1, :]
        hit = jnp.where(hit, 1.0, 0.0).astype(BF16)
        values = fine_dot(table, hit, 0, 0, 2)
        mine = iota(values.shape, 0) == rank[k : k + 1, :]
        found.append(jnp.sum(jnp.where(mine, values, 0.0), axis=0, keepdims=True))
    out_ref[...] = jnp.concatenate(found, axis=0) / gates


def grouped(kernel, me, parts, each, extras, extra_specs, outs, out_specs, steps, aliases, flops):
    width = parts[0].shape[1]
    return pl.pallas_call(
        functools.partial(kernel, len(parts)),
        out_shape=outs,
        grid_spec=pltpu.PrefetchScalarGridSpec(
            num_scalar_prefetch=1,
            grid=(steps,),
            in_specs=[pl.BlockSpec((each, width), lambda i, me: (i, 0))] * len(parts) + extra_specs,
            out_specs=out_specs,
        ),
        input_output_aliases=aliases,
        compiler_params=pltpu.CompilerParams(vmem_limit_bytes=VMEM_LIMIT),
        cost_estimate=pl.CostEstimate(
            flops=flops, bytes_accessed=6 * width * width, transcendentals=0
        ),
    )(me, *parts, *extras)


def outer_kernel(*refs):
    pairs, out_ref = zip(refs[0:-1:2], refs[1:-1:2]), refs[-1]
    out_ref[...] = sum(dot(a[...], b[...], 0, 0) for a, b in pairs).astype(BF16)


def outer_stage(*pairs):
    left, right = pairs[0][0].shape[1], pairs[0][1].shape[1]
    tile = min(256, right)
    column = lambda b: pl.BlockSpec((b.shape[0], tile), lambda i: (0, i))
    specs, args = [], []
    for a, b in pairs:
        specs += [one_step(a.shape), column(b)]
        args += from_hbm(a, b)
    rows = sum(a.shape[0] for a, _ in pairs)
    return call(
        outer_kernel,
        far_shape((left, right), BF16),
        *args,
        grid=(right // tile,),
        in_specs=specs,
        out_specs=pl.BlockSpec((left, tile), lambda i: (0, i)),
        cost=pl.CostEstimate(
            flops=2 * rows * left * right, bytes_accessed=6 * left * right, transcendentals=0
        ),
    )


def routed_experts(resid, out_grad, ids, gates, up, down, cap, shard_count, planes, early):
    tokens, width = resid.shape
    hidden = up.shape[1]
    group = shard_count * cap
    plane, shard = lax.axis_index("grp"), lax.axis_index("seq")
    me = jnp.stack([plane, shard]).astype(jnp.int32)
    smem = pl.BlockSpec(memory_space=pltpu.SMEM)
    vmem = pl.BlockSpec(memory_space=pltpu.VMEM)

    def across(x, bit):
        return lax.ppermute(x, "grp", [(i, i ^ bit) for i in range(planes)])

    def spread_out(parts):
        moved = [
            lax.ppermute(part, "seq", [(i, i ^ x) for i in range(shard_count)])
            for x, part in enumerate(parts)
            if x
        ]
        return [parts[0]] + moved

    def pick_rows(messages):
        count = len(messages)
        outs = [far_shape((count * cap, width), BF16)] * shard_count
        *parts, keys = streamed(
            functools.partial(pick_rows_kernel, count, cap),
            tuple(outs + [far_shape((count, 8, tokens), F32)]),
            *messages,
            scalars=me,
        )
        return parts, keys

    def pick_grads(keys, grads):
        count = len(grads)
        outs = [far_shape((count * cap, width), BF16)] * shard_count
        kernel = functools.partial(pick_grads_kernel, count, cap)
        return streamed(kernel, tuple(outs), keys, *grads)

    def pick_both(message, grad, near):
        outs = [far_shape((2 * cap, width), BF16)] * shard_count
        kernel = functools.partial(pick_both_kernel, cap)
        return streamed(kernel, tuple(outs), message, grad, scalars=me, near=near)

    def block(width):
        return pl.BlockSpec((group, width), lambda i, me: (i, 0))

    def hidden_stage(parts, steps):
        parts = from_hbm(*parts)
        rows = steps * group
        return grouped(
            hidden_kernel,
            me,
            parts,
            cap,
            (up,),
            [vmem],
            (far_shape((rows, width), BF16), far_shape((rows, hidden), BF16), shape((rows, hidden), F32)),
            (block(width), block(hidden), block(hidden)),
            steps,
            {},
            2 * rows * width * hidden,
        )

    rows_of = lambda steps, size, dtype: far_shape((steps * group, size), dtype)

    def backs(steps):
        return (far_shape((planes, group, width), BF16), far_shape((steps, 8, group), F32))

    def back_blocks(base):
        return (
            pl.BlockSpec((1, group, width), lambda i, me: (me[0] ^ (base + i), 0, 0)),
            pl.BlockSpec((1, 8, group), lambda i, me: (i, 0, 0)),
        )

    def routed_stage(parts, act, slope, steps, base, filled):
        return grouped(
            routed_kernel,
            me,
            parts,
            cap,
            (act, slope, up, down, filled),
            [block(hidden), block(hidden), vmem, vmem, pl.BlockSpec(memory_space=pl.ANY)],
            (rows_of(steps, width, BF16), rows_of(steps, hidden, BF16)) + backs(steps),
            (block(width), block(hidden)) + back_blocks(base),
            steps,
            {1 + len(parts) + 4: 2},
            4 * steps * group * width * hidden,
        )

    def whole_stage(parts, base, filled):
        extra = () if filled is None else (filled,)
        return grouped(
            far_kernel,
            me,
            parts,
            2 * cap,
            (up, down) + extra,
            [vmem, vmem] + [pl.BlockSpec(memory_space=pl.ANY)] * len(extra),
            (
                rows_of(1, width, BF16),
                rows_of(1, hidden, BF16),
                rows_of(1, width, BF16),
                rows_of(1, hidden, BF16),
            )
            + backs(1),
            (block(width), block(hidden), block(width), block(hidden)) + back_blocks(base),
            1,
            {1 + len(parts) + 2: 4} if extra else {},
            6 * group * width * hidden,
        )

    message, targets = streamed(
        functools.partial(message_kernel, planes, shard_count, cap),
        (far_shape((tokens + 8, width), BF16), far_shape((2, tokens), jnp.int32)),
        resid,
        ids,
        gates,
    )
    message2 = across(message, 2)
    message1 = across(message, 1)
    grad2 = across(out_grad, 2)
    grad1 = across(out_grad, 1)
    message3 = across(message2, 1)
    own = pick_both(message, out_grad, ())
    own = spread_out(own)
    own = from_hbm(*own)
    rows_0, act_0, scaled_0, pre_0, row_grad, own_terms = whole_stage(own, 0, None)
    near_rows, near_keys = pick_rows([message1, message2])
    near_rows = spread_out(near_rows)
    arrived, early = lax.optimization_barrier((near_rows[1], early))
    near_rows[1] = arrived
    grad3 = across(grad2, 1)
    near_grads = pick_grads(near_keys, [grad1, grad2])
    near_grads = spread_out(near_grads)
    rows_1, act_1, slope_1 = hidden_stage(near_rows, 2)
    far = pick_both(message3, grad3, (0, 1))
    far = spread_out(far)
    scaled_1, pre_1, row_grad, near_terms = routed_stage(near_grads, act_1, slope_1, 2, 1, row_grad)
    rows_2, act_2, scaled_2, pre_2, row_grad, far_terms = whole_stage(far, 3, row_grad)

    def finish():
        blocks = [own_terms[0]]
        blocks += [across(near_terms[bit - 1], bit) for bit in (1, 2)]
        blocks += [across(far_terms[0], 3)]
        down_grad = outer_stage((act_0, scaled_0), (act_1, scaled_1), (act_2, scaled_2))
        up_grad = outer_stage((rows_0, pre_0), (rows_1, pre_1), (rows_2, pre_2))
        blocks, down_grad, up_grad = lax.optimization_barrier((blocks, down_grad, up_grad))
        mixed = call(
            functools.partial(mix_kernel, planes, cap),
            tuple([shape((8, 128), F32)] * shard_count),
            me,
            *blocks,
            in_specs=[smem] + [vmem] * planes,
        )
        mixed = spread_out(mixed)
        gate_grad = call(
            functools.partial(found_kernel, cap, shard_count),
            far_shape((2, tokens), F32),
            me,
            targets,
            gates,
            *mixed,
            in_specs=[smem] + [vmem] * (2 + shard_count),
            out_specs=vmem,
        )
        return down_grad, up_grad, gate_grad

    return targets, row_grad.reshape(-1, width), finish, early


def plain_experts(resid, out_grad, ids, gates, up, down, cap, experts, swap, early):
    tokens, width = resid.shape
    slots = experts * cap
    send_rows, targets = call(
        functools.partial(rows_kernel, experts, cap),
        (shape((slots, width), BF16), shape((2, tokens), jnp.int32)),
        resid,
        ids,
    )
    rows = swap(send_rows)
    send_scaled = call(grads_kernel, shape((slots, width), BF16), out_grad, gates, targets)
    scaled = swap(send_scaled)
    hidden = jnp.dot(rows, up, preferred_element_type=F32)
    sigmoid = jax.nn.sigmoid(hidden)
    act = (hidden * sigmoid).astype(BF16)
    slope = sigmoid * (1.0 + hidden * (1.0 - sigmoid))
    pre_grad, row_grad, term = expert_stage(scaled, act, slope, up, down)

    def finish():
        terms = swap(term.astype(BF16).reshape(experts, cap))
        gate_grad = call(
            gate_kernel,
            shape((2, tokens), F32),
            jnp.broadcast_to(terms.reshape(1, slots), (8, slots)),
            targets,
            gates,
        )
        return (
            dot(act, scaled, 0, 0).astype(BF16),
            dot(rows, pre_grad, 0, 0).astype(BF16),
            gate_grad,
        )

    return targets, row_grad, finish, early


def spread(heads, width):
    return (iota((heads, width), 1) // (width // heads) == iota((heads, width), 0)).astype(F32)


def ends_kernel(
    inputs_ref, writes_ref, decays_ref, cum_ref, cumt_ref, grown_ref, left_ref, faded_ref, send_ref
):
    decays = decays_ref[...]
    heads, tokens = decays.shape
    parts, padded, width = send_ref.shape
    upto = (iota((tokens, tokens), 0) >= iota((tokens, tokens), 1)).astype(BF16)
    cum = sum(dot(upto, part, 1, 1) for part in pieces_of(decays, 3))
    cum_ref[...] = cum
    cumt = fine_dot(decays, upto, 1, 1, 3)
    for head in range(heads):
        cumt_ref[head] = cumt[head : head + 1, :]
    total = cum[tokens - 1 : tokens, :]
    wide = spread(heads, width).astype(BF16)
    grown_ref[...] = fine_dot(jnp.exp(cum), wide, 1, 0, 1).astype(BF16)
    remaining = fine_dot(jnp.exp(total - cum), wide, 1, 0, 2)
    left_ref[...] = remaining.astype(BF16)
    scaled = (inputs_ref[...].astype(F32) * remaining).astype(BF16)
    faded_ref[...] = scaled
    ends = dot(writes_ref[...], scaled, 0, 0)
    kept = fine_dot(jnp.exp(jnp.broadcast_to(total, (8, heads))), wide, 1, 0, 3)[0:1, :]
    high, low = pieces_of(kept, 2)
    rows = ends.shape[0] // parts
    for part in range(parts):
        send_ref[part, 0:rows, :] = ends[part * rows : (part + 1) * rows, :].astype(BF16)
        send_ref[part, rows : rows + 1, :] = high
        send_ref[part, rows + 1 : rows + 2, :] = low
        send_ref[part, rows + 2 :, :] = jnp.zeros((padded - rows - 2, width), BF16)


def scan_kernel(reverse, ends_ref, kept_ref, out_ref):
    parts, rows, _ = out_ref.shape
    state = jnp.zeros(out_ref.shape[1:], F32)
    for step in range(parts):
        at = parts - 1 - step if reverse else step
        out_ref[at] = state.astype(BF16)
        kept = kept_ref[at, rows : rows + 1, :].astype(F32) + kept_ref[
            at, rows + 1 : rows + 2, :
        ].astype(F32)
        state = state * kept + ends_ref[at, 0:rows, :].astype(F32)


def home_kernel(
    back_ref, targets_ref, resid_ref, out_grad_ref, reads_ref, grown_ref, grad_ref, adjoint_ref
):
    hit0, hit1 = one_hot(targets_ref[...], back_ref.shape[0])
    select = jnp.where(hit0 | hit1, 1.0, 0.0).astype(BF16)
    d_normed = dot(select, back_ref[...], 0, 0)
    resid = resid_ref[...].astype(F32)
    inverse = lax.rsqrt(jnp.mean(resid * resid, axis=1, keepdims=True) + EPSILON)
    normed = resid * inverse
    mean = jnp.mean(d_normed * normed, axis=1, keepdims=True)
    grad = (out_grad_ref[...].astype(F32) + inverse * (d_normed - normed * mean)).astype(BF16)
    grad_ref[...] = grad
    scaled = (grad.astype(F32) * grown_ref[...].astype(F32)).astype(BF16)
    adjoint_ref[...] = dot(reads_ref[...], scaled, 0, 0).astype(BF16)


def inside_kernel(
    base,
    inputs_ref,
    grads_ref,
    writes_ref,
    reads_ref,
    state_ref,
    cum_ref,
    cumt_ref,
    dx_ref,
    dwrite_ref,
    dread_ref,
    dcum_ref,
    dcumt_ref,
    score_ref,
    total_ref,
):
    step = pl.program_id(0)
    steps = pl.num_programs(0)
    tokens, lanes = inputs_ref.shape
    each = cumt_ref.shape[0]
    size = lanes // each

    @pl.when(step == 0)
    def _():
        score_ref[...] = dot(reads_ref[...], writes_ref[...], 1, 1)
        total_ref[...] = jnp.zeros_like(total_ref)
        dread_ref[...] = jnp.zeros_like(dread_ref)
        dcum_ref[...] = jnp.zeros_like(dcum_ref)

    inputs = inputs_ref[...]
    grads = grads_ref[...]
    cum = cum_ref[...]
    scores = score_ref[...]
    causal = iota((tokens, tokens), 0) >= iota((tokens, tokens), 1)
    column = iota(cum.shape, 1)
    lane = iota((tokens, lanes), 1) // size
    dx = jnp.zeros((tokens, lanes), F32)
    sums = jnp.zeros(cum.shape, F32)
    grown = jnp.zeros((tokens, lanes), F32)
    state = state_ref[...]
    read_state = dot(reads_ref[...], state, 1, 0)
    inter = grads.astype(F32) * read_state
    total = jnp.zeros((tokens, tokens), F32)
    for k in range(each):
        head = (base + step) * each + k
        at_t = jnp.sum(jnp.where(column == head, cum, 0.0), axis=1, keepdims=True)
        at_s = cumt_ref[k]
        decay = jnp.exp(jnp.where(causal, at_t - at_s, -1e30))
        mine = lane == k
        grads_k = jnp.where(mine, grads, jnp.zeros_like(grads))
        weights = dot(grads_k, inputs, 1, 1) * decay
        total = total + weights
        dx = dx + dot((decay * scores).astype(BF16), grads_k, 0, 0)
        both = weights * scores
        grow = jnp.exp(at_t)
        row = jnp.sum(both, axis=1, keepdims=True) + grow * jnp.sum(
            jnp.where(mine, inter, 0.0), axis=1, keepdims=True
        )
        sums = sums + jnp.where(column == head, row, 0.0)
        dcumt_ref[k] = jnp.sum(both, axis=0, keepdims=True)
        grown = grown + jnp.where(mine, grow, 0.0)
    total_ref[...] += total
    dcum_ref[...] += sums
    dx_ref[...] = dx.astype(BF16)
    dread_ref[...] += dot((grown * grads.astype(F32)).astype(BF16), state, 1, 1)

    @pl.when(step == steps - 1)
    def _():
        total_b = total_ref[...].astype(BF16)
        dread_ref[...] += dot(total_b, writes_ref[...], 1, 0)
        dwrite_ref[...] = dot(total_b, reads_ref[...], 0, 0)


def inside_stage(inputs, grads, writes, reads, state, cum, cumt, half):
    tokens, width = inputs.shape
    heads = cum.shape[1]
    n = writes.shape[1]
    lanes = max(128, width // heads)
    steps = width // lanes // 2
    each = heads // (width // lanes)
    base = half * steps
    part = pl.BlockSpec((tokens, lanes), lambda i: (0, base + i))
    return call(
        functools.partial(inside_kernel, base),
        (
            far_shape((tokens, width // 2), BF16),
            far_shape((tokens, n), F32),
            far_shape((tokens, n), F32),
            far_shape((tokens, heads), F32),
            far_shape((heads // 2, 1, tokens), F32),
        ),
        *from_hbm(inputs, grads, writes, reads, state, cum, cumt),
        grid=(steps,),
        in_specs=[
            part,
            part,
            one_step((tokens, n)),
            one_step((tokens, n)),
            pl.BlockSpec((n, lanes), lambda i: (0, base + i)),
            one_step((tokens, heads)),
            pl.BlockSpec((each, 1, tokens), lambda i: (base + i, 0, 0)),
        ],
        out_specs=(
            pl.BlockSpec((tokens, lanes), lambda i: (0, i)),
            one_step((tokens, n)),
            one_step((tokens, n)),
            one_step((tokens, heads)),
            pl.BlockSpec((each, 1, tokens), lambda i: (i, 0, 0)),
        ),
        scratch=[pltpu.VMEM((tokens, tokens), F32), pltpu.VMEM((tokens, tokens), F32)],
        cost=pl.CostEstimate(
            flops=4 * tokens * tokens * width,
            bytes_accessed=4 * tokens * width,
            transcendentals=heads * tokens * tokens // 2,
        ),
    )


def last_kernel(
    writes_ref,
    state_ref,
    adjoint_ref,
    cumt_ref,
    left_ref,
    faded_ref,
    dx0_ref,
    dwrite0_ref,
    dread0_ref,
    dcum0_ref,
    dcumt0_ref,
    dx1_ref,
    dwrite1_ref,
    dread1_ref,
    dcum1_ref,
    dcumt1_ref,
    input_grad_ref,
    dwrite_ref,
    dread_ref,
    decay_ref,
):
    tokens, width = left_ref.shape
    heads = cumt_ref.shape[0]
    half = width // 2
    wide = spread(heads, width).astype(BF16)
    adjoint = adjoint_ref[...]
    faded = faded_ref[...]
    values = dot(writes_ref[...], adjoint, 1, 0)
    moved = left_ref[...].astype(F32) * values
    input_grad_ref[:, 0:half] = (dx0_ref[...].astype(F32) + moved[:, 0:half]).astype(BF16)
    input_grad_ref[:, half:] = (dx1_ref[...].astype(F32) + moved[:, half:]).astype(BF16)
    dwrite_ref[...] = dwrite0_ref[...] + dwrite1_ref[...] + dot(faded, adjoint, 1, 1)
    dread_ref[...] = dread0_ref[...] + dread1_ref[...]
    shares = pieces_of(values * faded.astype(F32), 2)
    shares = sum(dot(wide, part, 1, 1) for part in shares)
    kept = jnp.sum(state_ref[...].astype(F32) * adjoint.astype(F32), axis=0, keepdims=True)
    kept = pieces_of(jnp.broadcast_to(kept, (8, width)), 3)
    kept = sum(dot(wide, part, 1, 1) for part in kept)[:, 0:1]
    flow = [ref[h] for ref in (dcumt0_ref, dcumt1_ref) for h in range(heads // 2)]
    total = jnp.concatenate([cumt_ref[h][:, tokens - 1 : tokens] for h in range(heads)], axis=0)
    after = (iota((tokens, tokens), 1) >= iota((tokens, tokens), 0)).astype(BF16)
    rows = -jnp.concatenate(flow, axis=0) - shares
    columns = dcum0_ref[...] + dcum1_ref[...]
    decay_ref[...] = (
        sum(dot(part, after, 0, 1) for part in pieces_of(columns, 3))
        + sum(dot(part, after, 1, 1) for part in pieces_of(rows, 3))
        + jnp.sum(shares, axis=1, keepdims=True)
        + kept * jnp.exp(total)
    )


def shards(
    mixer_input,
    write_proj,
    read_proj,
    log_decay,
    resid,
    out_grad,
    gate_probs,
    expert_ids,
    expert_up,
    expert_down,
):
    tokens, width = resid.shape
    heads = log_decay.shape[1]
    n = write_proj.shape[1]
    shard_count = lax.axis_size("seq")
    experts = lax.axis_size("grp") * shard_count
    cap = 4 * tokens // experts
    everyone = ("grp", "seq")
    up, down = expert_up[0], expert_down[0]
    ids = expert_ids.T
    gates = gate_probs.T

    def swap(x, axes):
        return lax.all_to_all(x, axes, split_axis=0, concat_axis=0, tiled=True)

    state_rows = n // shard_count
    padded = -(-(state_rows + 2) // 8) * 8
    cum, cumt, grown, left, faded, send_ends = streamed(
        ends_kernel,
        (
            far_shape((tokens, heads), F32),
            far_shape((heads, 1, tokens), F32),
            far_shape((tokens, width), BF16),
            far_shape((tokens, width), BF16),
            far_shape((tokens, width), BF16),
            far_shape((shard_count, padded, width), BF16),
        ),
        mixer_input,
        write_proj,
        log_decay.T,
    )
    ends = swap(send_ends, "seq")
    parts = far_shape((shard_count, state_rows, width), BF16)
    starts = call(functools.partial(scan_kernel, False), parts, ends, ends)
    state = swap(starts, "seq").reshape(n, width)

    planes = experts // shard_count
    if planes == 4 and shard_count <= 8 and cap in (16, 32, 64, 128) and tokens <= width:
        targets, row_grad, finish, state = routed_experts(
            resid, out_grad, ids, gates, up, down, cap, shard_count, planes, state
        )
    else:
        targets, row_grad, finish, state = plain_experts(
            resid, out_grad, ids, gates, up, down, cap, experts, lambda x: swap(x, everyone), state
        )
    back = swap(row_grad, everyone)
    down_grad, up_grad, gate_grad = finish()
    back, down_grad, up_grad = lax.optimization_barrier((back, down_grad, up_grad))
    resid_grad, send_adjoint = streamed(
        home_kernel,
        (far_shape((tokens, width), BF16), far_shape((n, width), BF16)),
        back,
        targets,
        resid,
        out_grad,
        read_proj,
        grown,
        near=(0,),
    )
    adjoints = swap(send_adjoint.reshape(shard_count, state_rows, width), "seq")
    inside = (mixer_input, resid_grad, write_proj, read_proj, state, cum, cumt)
    first = inside_stage(*inside, 0)
    later = call(functools.partial(scan_kernel, True), parts, adjoints, ends)
    adjoint = swap(later, "seq").reshape(n, width)
    second = inside_stage(*inside, 1)
    input_grad, write_grad, read_grad, decay_grad = streamed(
        last_kernel,
        (
            far_shape((tokens, width), BF16),
            far_shape((tokens, n), F32),
            far_shape((tokens, n), F32),
            far_shape((heads, tokens), F32),
        ),
        write_proj,
        state,
        adjoint,
        cumt,
        left,
        faded,
        *first,
        *second,
        near=(2,),
    )
    return (
        input_grad,
        write_grad,
        read_grad,
        decay_grad.T,
        resid_grad,
        gate_grad.T.astype(BF16),
        up_grad[None],
        down_grad[None],
    )


def solution(mesh):
    flat = P(("grp", "seq"), None)
    cube = P(("grp", "seq"), None, None)
    return jax.shard_map(
        shards,
        mesh=mesh,
        in_specs=(flat,) * 8 + (cube,) * 2,
        out_specs=(flat,) * 6 + (cube,) * 2,
        check_vma=False,
    )
```
